256 devices in a mesh: kv: 4 (over y), blk: 64 (over z, x, core).
Axes of the slice: x: 4, y: 4, z: 8, core: 2. Of those that a mesh axis runs over, the one named last changes fastest.
Arguments:
- embeds: bfloat16 [3, 512, 4096], P(None, None, 'blk'), may hold values from -6 to 6
- attn_gain: float32 [4096], P('blk'), may hold values from 0.25 to 1.75
- w_query: bfloat16 [4096, 4096], P('blk', 'kv'), may hold values from -0.1875 to 0.1875
- w_key: bfloat16 [4096, 512], P('blk', 'kv'), may hold values from -0.09375 to 0.09375
- w_value: bfloat16 [4096, 512], P('blk', 'kv'), may hold values from -0.09375 to 0.09375
- w_out: bfloat16 [4096, 4096], P('kv', 'blk'), may hold values from -0.375 to 0.375
- cache_kv: bfloat16 [2048, 4, 2, 128, 128], P('blk', 'kv'), may hold values from -102 to 102, as said below
- lengths: int32 [512], replicated, may hold values from 1 to 8192, as said below
- block_table: int32 [512, 64], replicated, may hold values from 0 to 2048, as said below
- parents: int32 [3, 512], replicated, may hold values from 0 to 511, as said below
Outputs:
- out_rows: bfloat16 [3, 512, 4096], P(None, None, 'blk')
- appended: bfloat16 [3, 512, 4, 2, 128], P(None, 'blk', 'kv')
The draws below stay inside these ranges and needn't reach their ends.
Inputs may be any that keep to these rules, and one draw needn't show every extreme that they name: `lengths`: one beam holds exactly 8192 tokens. `block_table`: row b names the slots of beam b's blocks of 128 tokens in order; entries at and past ceil(lengths[b] / 128) equal 2048; no slot is named twice. parents[s, b] lies in the aligned group of 8 beams that holds b. `cache_kv`: slots that no row of block_table names are never read.
All inputs are finite; a program needn't handle non-finite values.
Results may differ from the reference program's by a relative error of at most 0.0044.
The reference program's roundings to bfloat16 on the way count: a program that leaves them out, or rounds other values in their place, can miss the bound.
Values may be sent and summed in bfloat16 or wider, within the bound.
No kernel may reach another device: no remote copies, remote signals or barrier semaphores. Data moves between devices by JAX's collectives and lax.ppermute only.
A program may use at most 64 MiB of HBM per device.

```python
import math
import jax
import jax.numpy as jnp
from jax import lax

D = 4096
H = 32
KVH = 4
HD = 128
QPK = 8
GROUP = 8
BLK = 128
MAXLEN = 8192
MAXBLK = 64
STEPS = 3
SPANB = 2
BEAMS = 512
CACHE_SLOT_COUNT = 2048


def layout_draw(key):
    base_key = jax.random.fold_in(key, 7177)
    key_count, extended_key, key_tail, key_shuffle = jax.random.split(base_key, 4)
    beam_ids = jnp.arange(BEAMS, dtype=jnp.int32)
    longest = jax.random.randint(extended_key, (), 0, BEAMS)
    counts = jax.random.randint(key_count, (BEAMS,), 1, 2 * SPANB)
    counts = jnp.where(beam_ids == longest, MAXBLK, counts)
    tail_len = jax.random.randint(key_tail, (BEAMS,), 1, BLK + 1)
    token_counts = jnp.where(beam_ids == longest, MAXLEN, (counts - 1) * BLK + tail_len)
    shuffled = jax.random.permutation(key_shuffle, CACHE_SLOT_COUNT).astype(jnp.int32)
    starts = jnp.cumsum(counts) - counts
    block_pos = jnp.arange(MAXBLK, dtype=jnp.int32)
    slot_index = jnp.clip(starts[:, None] + block_pos[None, :], 0, CACHE_SLOT_COUNT - 1)
    slot_table = jnp.where(block_pos[None, :] < counts[:, None], shuffled[slot_index], CACHE_SLOT_COUNT)
    return (token_counts.astype(jnp.int32), slot_table.astype(jnp.int32))


def draw_lengths(key, part):
    return layout_draw(key)[0]


def draw_block_table(key, part):
    return layout_draw(key)[1]


def draw_parents(key, part):
    offsets = jax.random.randint(jax.random.fold_in(key, 3301), (STEPS, BEAMS), 0, GROUP)
    group_base = jnp.arange(BEAMS, dtype=jnp.int32) // GROUP * GROUP
    return (group_base[None, :] + offsets).astype(jnp.int32)


def draw_cache_kv(key, part):
    array_shape = (CACHE_SLOT_COUNT, KVH, 2, BLK, HD)
    key_main = jax.random.fold_in(jax.random.fold_in(key, 5501), 0)
    values = jnp.clip(jax.random.normal(key_main, array_shape, jnp.float32), -6.0, 6.0)
    return values.astype(jnp.bfloat16)


def steps_of(rng, shape, cuts, least, high):
    loudness, own = 1.0, jax.random.fold_in(rng, 6)
    for dim, parts in cuts:
        draws = jnp.exp(jax.random.uniform(jax.random.fold_in(own, dim), (parts,), jnp.float32, least / len(cuts), high / len(cuts)))
        loudness = loudness * jnp.repeat(draws, shape[dim] // parts).reshape([-1 if axis == dim else 1 for axis in range(len(shape))])
    return loudness


def bell_draw(own_key, extent, deviation, limit, cuts=(), kind=jnp.bfloat16):
    result = jax.random.normal(own_key, extent, jnp.float32) * deviation
    if len(cuts) > 0:
        result = steps_of(own_key, extent, cuts, -0.22, 0.18) * result
    return jnp.clip(result, min=-limit, max=limit).astype(kind)


def setup_inputs(seed: int = 0) -> dict:
    splits = jax.random.split(jax.random.key(seed), 11)
    embeds = bell_draw(splits[0], (STEPS, BEAMS, D), 1.0, 6.0, ((2, 64),))
    attn_gain = jnp.clip(1.0 + 0.15 * jax.random.normal(splits[1], (D,), jnp.float32), 0.25, 1.75)
    w_query = bell_draw(splits[2], (D, H * HD), (D // 4) ** -0.5, 0.1875, ((0, 64), (1, 4)))
    w_key = bell_draw(splits[3], (D, KVH * HD), D ** -0.5, 0.09375, ((0, 64), (1, 4)))
    w_value = bell_draw(splits[4], (D, KVH * HD), D ** -0.5, 0.09375, ((0, 64), (1, 4)))
    w_out = bell_draw(splits[5], (H * HD, D), (H * HD // 16) ** -0.5, 0.375, ((0, 4), (1, 64)))
    cache_kv = draw_cache_kv(jax.random.fold_in(splits[10], 71), 0)
    lengths = draw_lengths(jax.random.fold_in(splits[10], 71), 0)
    block_table = draw_block_table(jax.random.fold_in(splits[10], 71), 0)
    parents = draw_parents(jax.random.fold_in(splits[10], 71), 0)
    return {"embeds": embeds, "attn_gain": attn_gain, "w_query": w_query, "w_key": w_key, "w_value": w_value, "w_out": w_out, "cache_kv": cache_kv, "lengths": lengths, "block_table": block_table, "parents": parents}


NEGATIVE = -1e+30
EPSILON = 1e-05
ROPE_BASE = 5000000.0

def rotate(vector, position):
    half_dim = vector.shape[-1] // 2
    exponent = jnp.arange(half_dim, dtype=jnp.float32) * (2.0 / vector.shape[-1])
    frequency = ROPE_BASE ** (-exponent)
    angles = position.astype(jnp.float32)[:, None] * frequency[None, :]
    target_shape = (position.shape[0],) + (1,) * (vector.ndim - 2) + (half_dim,)
    cosines = jnp.cos(angles).reshape(target_shape)
    sine_part = jnp.sin(angles).reshape(target_shape)
    first_half = vector[..., :half_dim]
    second_half = vector[..., half_dim:]
    return jnp.concatenate([first_half * cosines - second_half * sine_part, second_half * cosines + first_half * sine_part], axis=-1)

def attend_beam(beam_id, query_all, recent, root_beams, lengths, block_table, cache_kv):
    scaling = 1.0 / math.sqrt(HD)
    root_beam = root_beams[beam_id]
    length = lengths[root_beam]
    block_count = (length + BLK - 1) // BLK
    beam_query = query_all[beam_id].astype(jnp.float32)
    token_index = jnp.arange(BLK, dtype=jnp.int32)

    def block_scores(block_pos):
        cached = cache_kv[block_table[root_beam, block_pos]].astype(jnp.float32)
        scores = jnp.einsum('gqd,gkd->gqk', beam_query, cached[:, 0]) * scaling
        is_valid = block_pos * BLK + token_index < length
        return (scores, is_valid, cached[:, 1])

    def pass_max(block_pos, running):
        scores, is_valid, unused = block_scores(block_pos)
        return jnp.maximum(running, lax.optimization_barrier(jnp.max(jnp.where(is_valid[None, None, :], scores, NEGATIVE), axis=-1)))
    latest_key_rows = recent[:, beam_id, :, 0].astype(jnp.float32)
    latest_value_rows = recent[:, beam_id, :, 1].astype(jnp.float32)
    recent_scores = jnp.einsum('gqd,tgd->gqt', beam_query, latest_key_rows) * scaling
    ceiling = lax.fori_loop(0, block_count, pass_max, lax.optimization_barrier(jnp.max(recent_scores, axis=-1)))

    def pass_sum(block_pos, running):
        numerator, denominator = running
        scores, is_valid, cached_values = block_scores(block_pos)
        weights = jnp.exp(jnp.where(is_valid[None, None, :], scores - ceiling[..., None], NEGATIVE))
        rounded = lax.optimization_barrier(weights.astype(jnp.bfloat16)).astype(jnp.float32)
        return (numerator + jnp.einsum('gqk,gkd->gqd', rounded, cached_values), denominator + lax.optimization_barrier(jnp.sum(weights, axis=-1)))
    recent_weights = jnp.exp(recent_scores - ceiling[..., None])
    recent_rounded = lax.optimization_barrier(recent_weights.astype(jnp.bfloat16)).astype(jnp.float32)
    start_numer = jnp.einsum('gqt,tgd->gqd', recent_rounded, latest_value_rows)
    start_denom = lax.optimization_barrier(jnp.sum(recent_weights, axis=-1))
    numerator, denominator = lax.fori_loop(0, block_count, pass_sum, (start_numer, start_denom))
    return (numerator / denominator[..., None]).astype(jnp.bfloat16).reshape(H * HD)

def reference(embeds, attn_gain, w_query, w_key, w_value, w_out, cache_kv, lengths, block_table, parents):
    root_beams = jnp.arange(BEAMS, dtype=jnp.int32)
    appended = jnp.zeros((STEPS, BEAMS, KVH, 2, HD), jnp.bfloat16)
    outputs = []
    for step_index in range(STEPS):
        root_beams = root_beams[parents[step_index]]
        appended = appended[:, parents[step_index]]
        stream = embeds[step_index].astype(jnp.float32)
        inverse_rms = lax.rsqrt(lax.optimization_barrier(jnp.mean(stream * stream, axis=1)) + EPSILON)
        normed = (stream * inverse_rms[:, None] * attn_gain[None, :]).astype(jnp.bfloat16)
        position = (lengths[root_beams] + step_index).astype(jnp.int32)
        query_all = rotate(jnp.dot(normed, w_query, preferred_element_type=jnp.float32).reshape(BEAMS, KVH, QPK, HD), position).astype(jnp.bfloat16)
        key_new = rotate(jnp.dot(normed, w_key, preferred_element_type=jnp.float32).reshape(BEAMS, KVH, HD), position).astype(jnp.bfloat16)
        value_new = jnp.dot(normed, w_value, preferred_element_type=jnp.float32).reshape(BEAMS, KVH, HD).astype(jnp.bfloat16)
        appended = appended.at[step_index].set(jnp.stack([key_new, value_new], axis=2))
        recent = appended[:step_index + 1]
        attended = lax.map(lambda beam_id: attend_beam(beam_id, query_all, recent, root_beams, lengths, block_table, cache_kv), jnp.arange(BEAMS, dtype=jnp.int32))
        projected = jnp.dot(attended, w_out, preferred_element_type=jnp.float32)
        outputs.append((stream + projected).astype(jnp.bfloat16))
    return (jnp.stack(outputs), appended)
```

```python
import functools
import math

import jax
import jax.numpy as jnp
from jax import lax
from jax.experimental import pallas as pl
from jax.experimental.pallas import tpu as pltpu
from jax.sharding import Mesh
from jax.sharding import PartitionSpec as P

GROUP = 8
NEGATIVE = -1e30
EPSILON = 1e-05
ROPE_BASE = 5000000.0
STEPS = 3
HEADS = 8
HD = 128
SB = STEPS * GROUP
ROWS = HEADS * SB
BLOCK = ROWS + 8
ZN, XN, CN = 8, 4, 2
JN = XN * CN
PAIRS = [(s, u) for s in range(STEPS) for u in range(s + 1)]
SCALE = 1.0 / math.sqrt(HD)
XC = ("x", "core")
BLK = ("z", "x", "core")


def exchange(value, axis):
    return lax.all_to_all(value, axis, 0, 0, tiled=True)


def spread(value, axis, count):
    return exchange(jnp.broadcast_to(value[None], (count,) + value.shape), axis)


def after_projection(parent_ref, parts_ref, cos_ref, sin_ref, q_ref, k_ref, v_ref, hold):
    total = parts_ref[0]
    for source in range(1, ZN):
        total = total + parts_ref[source]
    cosines = cos_ref[...]
    sines = sin_ref[...]

    def turn(part):
        return part * cosines + pltpu.roll(part, HD // 2, 1) * sines

    for head in range(HEADS):
        hold[head * SB : (head + 1) * SB] = turn(total[:, head * HD : (head + 1) * HD])
    q_ref[...] = hold[...].astype(jnp.bfloat16)
    start = HEADS * HD
    fresh_key = turn(total[:, start : start + HD]).astype(jnp.bfloat16).astype(jnp.float32)
    fresh_value = total[:, start + HD :].astype(jnp.bfloat16).astype(jnp.float32)
    for index, (step, token) in enumerate(PAIRS):
        for ref, fresh in ((k_ref, fresh_key), (v_ref, fresh_value)):
            if token == step:
                ref[index] = fresh[step * GROUP : (step + 1) * GROUP]
            else:
                before = PAIRS.index((step - 1, token))
                for beam in range(GROUP):
                    parent = parent_ref[step * GROUP + beam]
                    ref[index, pl.ds(beam, 1), :] = ref[before, pl.ds(parent, 1), :]


def attention(
    owner_ref, group_ref, count_ref, q_ref, root_ref, own_ref, other_ref, out_ref, top_ref, sum_ref
):
    groups = ZN * XN
    top_ref[...] = jnp.full_like(top_ref, NEGATIVE)
    sum_ref[...] = jnp.zeros_like(sum_ref)
    out_ref[...] = jnp.zeros_like(out_ref)
    tokens = lax.broadcasted_iota(jnp.int32, (SB, HD), 1)
    slots = own_ref.shape[0]

    def visit(cache_ref, offset):
        def step(slot, carry):
            count = count_ref[offset + slot]

            @pl.when(count > 0)
            def _():
                group = group_ref[offset + slot]
                owner = owner_ref[offset + slot]
                keys = cache_ref[slot, 0]
                values = cache_ref[slot, 1]
                live = (root_ref[group] == owner) & (tokens < count)
                live = jnp.concatenate([live] * HEADS, axis=0)
                scores = (
                    lax.dot_general(
                        q_ref[group],
                        keys,
                        (((1,), (1,)), ((), ())),
                        preferred_element_type=jnp.float32,
                    )
                    * SCALE
                )
                scores = jnp.where(live, scores, NEGATIVE)
                old = top_ref[group]
                new = jnp.maximum(old, jnp.max(scores, axis=1, keepdims=True))
                weights = jnp.where(live, jnp.exp(scores - new), 0.0)
                fade = jnp.exp(old - new)
                top_ref[group] = new
                sum_ref[group] = sum_ref[group] * fade + jnp.sum(weights, axis=1, keepdims=True)
                out_ref[group, 0:ROWS, :] = out_ref[group, 0:ROWS, :] * fade + jnp.dot(
                    weights.astype(jnp.bfloat16), values, preferred_element_type=jnp.float32
                )

            return carry

        lax.fori_loop(0, slots, step, 0)

    visit(own_ref, 0)
    visit(other_ref, slots)
    lanes = lax.broadcasted_iota(jnp.int32, (GROUP, HD), 1)

    def pack(group, carry):
        tile = jnp.zeros((GROUP, HD), jnp.float32)
        for part in range(HEADS * STEPS):
            rows = slice(part * GROUP, (part + 1) * GROUP)
            tile = jnp.where(lanes == part, top_ref[group, rows, :], tile)
            tile = jnp.where(lanes == part + HD // 2, sum_ref[group, rows, :], tile)
        out_ref[group, ROWS:BLOCK, :] = tile
        return carry

    lax.fori_loop(0, groups, pack, 0)


def merge(parts_ref, out_ref):
    count = parts_ref.shape[0]
    stats = [parts_ref[source, 0, ROWS:BLOCK, :] for source in range(count)]
    top = functools.reduce(jnp.maximum, stats)
    fades = [jnp.exp(stat - top) for stat in stats]
    total = sum(fade * pltpu.roll(stat, HD // 2, 1) for fade, stat in zip(fades, stats))
    lanes = lax.broadcasted_iota(jnp.int32, (GROUP, HD), 1)
    out_ref[0, ROWS:BLOCK, :] = jnp.where(lanes < HD // 2, top, pltpu.roll(total, HD // 2, 1))
    for part in range(HEADS * STEPS):
        rows = slice(part * GROUP, (part + 1) * GROUP)
        out_ref[0, rows, :] = sum(
            fades[source][:, part : part + 1] * parts_ref[source, 0, rows, :]
            for source in range(count)
        )


def finish(parts_ref, q_ref, k_ref, v_ref, out_ref, hold):
    count = parts_ref.shape[0]
    stats = [parts_ref[source, ROWS:BLOCK, :] for source in range(count)]
    cached_top = functools.reduce(jnp.maximum, stats)
    queries = q_ref[...].astype(jnp.float32)
    lanes = lax.broadcasted_iota(jnp.int32, (GROUP, HD), 1)
    fresh = {}
    tops = cached_top
    for head in range(HEADS):
        for step in range(STEPS):
            part = head * STEPS + step
            row = head * SB + step * GROUP
            tile = queries[row : row + GROUP]
            for token in range(step + 1):
                key = k_ref[PAIRS.index((step, token))]
                score = jnp.sum(tile * key, axis=1, keepdims=True) * SCALE
                fresh[part, token] = score
                tops = jnp.where(lanes == part, jnp.maximum(tops, score), tops)
    fades = [jnp.exp(stat - tops) for stat in stats]
    total = sum(fade * pltpu.roll(stat, HD // 2, 1) for fade, stat in zip(fades, stats))
    for head in range(HEADS):
        for step in range(STEPS):
            part = head * STEPS + step
            rows = slice(part * GROUP, (part + 1) * GROUP)
            ceiling = tops[:, part : part + 1]
            below = total[:, part : part + 1]
            above = sum(
                fades[source][:, part : part + 1] * parts_ref[source, rows, :]
                for source in range(count)
            )
            for token in range(step + 1):
                weight = jnp.exp(fresh[part, token] - ceiling)
                below = below + weight
                above = above + weight.astype(jnp.bfloat16).astype(jnp.float32) * v_ref[
                    PAIRS.index((step, token))
                ]
            hold[step * GROUP : (step + 1) * GROUP, head * HD : (head + 1) * HD] = above / below
    out_ref[...] = hold[...].astype(jnp.bfloat16)


def compose(parents_near):
    digits = jnp.arange(GROUP, dtype=jnp.int32)
    roots = [parents_near[0]]
    for step in range(1, STEPS):
        pick = parents_near[step][:, :, None] == digits
        roots.append(jnp.sum(jnp.where(pick, roots[-1][:, None, :], 0), axis=-1))
    return jnp.stack(roots)


def body(
    embeds, attn_gain, w_query, w_key, w_value, w_out, cache_kv, lengths, block_table, parents
):
    z = lax.axis_index("z")
    x = lax.axis_index("x")
    core = lax.axis_index("core")
    here = (z * XN + x) * CN + core
    width_part = embeds.shape[2]
    groups = ZN * JN
    beams = groups * GROUP
    slots = cache_kv.shape[0]
    width = width_part * groups
    gathered = width_part * JN

    cache = cache_kv[:, 0]
    other_cache = lax.ppermute(cache, "core", [(0, 1), (1, 0)])

    base = jnp.arange(groups, dtype=jnp.int32)[None, :, None] * GROUP
    parents_near = parents.reshape(STEPS, groups, GROUP) - base
    roots_near = compose(parents_near)
    roots = roots_near + base
    length_of = lengths.reshape(groups, GROUP)
    own_roots = lax.dynamic_slice_in_dim(roots_near, here, 1, 1)[:, 0]
    own_parents = lax.dynamic_slice_in_dim(parents_near, here, 1, 1)[:, 0]
    own_lengths = lax.dynamic_slice_in_dim(length_of, here, 1, 0)[0]
    digits = jnp.arange(GROUP, dtype=jnp.int32)
    position = jnp.sum(
        jnp.where(own_roots[:, :, None] == digits, own_lengths[None, None, :], 0), axis=-1
    ) + jnp.arange(STEPS, dtype=jnp.int32)[:, None]
    exponent = jnp.arange(HD // 2, dtype=jnp.float32) * (2.0 / HD)
    frequency = ROPE_BASE ** (-exponent)
    angles = position.reshape(SB).astype(jnp.float32)[:, None] * frequency[None, :]
    cosines = jnp.cos(angles)
    sines = jnp.sin(angles)
    cosines = jnp.concatenate([cosines, cosines], axis=1)
    sines = jnp.concatenate([-sines, sines], axis=1)
    own_ids = here * slots + jnp.arange(slots, dtype=jnp.int32)
    other_ids = (here + 1 - 2 * core) * slots + jnp.arange(slots, dtype=jnp.int32)
    ids = jnp.concatenate([own_ids, other_ids])
    table = block_table.reshape(-1, 128)
    codes = jnp.arange(table.size, dtype=jnp.int32).reshape(table.shape)
    code = jnp.max(jnp.where(table[None] == ids[:, None, None], codes[None], -1), axis=(1, 2))
    spans = jnp.broadcast_to(lengths[:, None], block_table.shape).reshape(table.shape)
    span = jnp.max(jnp.where(table[None] == ids[:, None, None], spans[None], 0), axis=(1, 2))
    owner = code // block_table.shape[1]
    count = span - (code % block_table.shape[1]) * HD
    group = owner // GROUP
    mine = (code >= 0) & (group % CN == core)
    count = jnp.where(mine, count, 0)
    group = jnp.where(mine, (group // CN % XN) * ZN + group // JN, 0)
    root_tiles = lax.dynamic_slice_in_dim(roots.reshape(STEPS, ZN, XN, CN, GROUP), core, 1, 3)
    root_tiles = root_tiles[:, :, :, 0].transpose(2, 1, 0, 3).reshape(ZN * XN, SB)
    root_tiles = jnp.broadcast_to(root_tiles[:, :, None], (ZN * XN, SB, HD))

    rows = ZN * SB
    half = rows // 2
    by_row = embeds.reshape(STEPS, ZN, JN, GROUP, width_part).transpose(2, 1, 0, 3, 4)
    by_row = by_row.reshape(JN, rows, width_part)
    high = lax.reduce_precision(attn_gain, 8, 7)
    middle = lax.reduce_precision(attn_gain - high, 8, 7)
    low = attn_gain - high - middle
    gain_rows = jnp.stack(
        [jnp.concatenate([high, middle]), jnp.concatenate([low, jnp.zeros_like(low)])]
    ).astype(jnp.bfloat16)
    gain_rows = jnp.concatenate([gain_rows, jnp.zeros((6, HD), jnp.bfloat16)])
    packed = jnp.concatenate(
        [
            jnp.concatenate([by_row[:, :half], by_row[:, half:]], axis=2),
            jnp.broadcast_to(gain_rows[None], (JN, 8, HD)),
        ],
        axis=1,
    )
    packed = exchange(packed, XC)
    stream = jnp.concatenate(
        [packed[:, :half, :width_part], packed[:, :half, width_part:]], axis=1
    )
    stream = stream.transpose(1, 0, 2).reshape(rows, gathered).astype(jnp.float32)
    tails = packed[:, half : half + 2].astype(jnp.float32)
    gain = tails[:, 0, :width_part] + tails[:, 0, width_part:] + tails[:, 1, :width_part]
    gain = gain.reshape(gathered)
    squares = jnp.sum(stream * stream, axis=1)
    squares = jnp.pad(squares, (0, 256 - rows)).reshape(2, 128)
    squares = jnp.sum(spread(squares, "z", ZN), axis=0).reshape(256)[:rows]
    inverse = lax.rsqrt(squares / width + EPSILON)
    normed = (stream * inverse[:, None] * gain[None, :]).astype(jnp.bfloat16)

    weights = jnp.concatenate([w_query, w_key, w_value], axis=1)
    weights = spread(weights, "x", XN)
    weights = spread(weights, "core", CN)
    weights = weights.reshape(CN, XN, width_part, -1).transpose(1, 0, 2, 3)
    weights = weights.reshape(gathered, -1)
    projected = jnp.dot(normed, weights, preferred_element_type=jnp.float32)
    projected = exchange(projected.reshape(ZN, SB, -1), "z")

    small = jax.ShapeDtypeStruct((len(PAIRS), GROUP, HD), jnp.float32)
    vmem = pl.BlockSpec(memory_space=pltpu.VMEM)
    smem = pl.BlockSpec(memory_space=pltpu.SMEM)
    queries, key_chain, value_chain = pl.pallas_call(
        after_projection,
        out_shape=(jax.ShapeDtypeStruct((ROWS, HD), jnp.bfloat16), small, small),
        in_specs=[smem, vmem, vmem, vmem],
        out_specs=(vmem, vmem, vmem),
        scratch_shapes=[pltpu.VMEM((ROWS, HD), jnp.float32)],
    )(own_parents.reshape(SB), projected, cosines, sines)
    last = PAIRS.index((STEPS - 1, 0))
    appended = jnp.stack([key_chain[last:], value_chain[last:]], axis=2)
    appended = appended[:, :, None].astype(jnp.bfloat16)

    everyone = spread(queries, "z", ZN)
    everyone = spread(everyone.reshape(ZN * ROWS, HD), "x", XN).reshape(XN * ZN, ROWS, HD)
    partial = pl.pallas_call(
        attention,
        out_shape=jax.ShapeDtypeStruct((XN * ZN, BLOCK, HD), jnp.float32),
        in_specs=[smem, smem, smem, vmem, vmem, vmem, vmem],
        out_specs=vmem,
        scratch_shapes=[
            pltpu.VMEM((XN * ZN, ROWS, HD), jnp.float32),
            pltpu.VMEM((XN * ZN, ROWS, HD), jnp.float32),
        ],
        compiler_params=pltpu.CompilerParams(vmem_limit_bytes=40 << 20),
    )(owner, group, count, everyone, root_tiles, cache, other_cache)

    partial = exchange(partial.reshape(XN, ZN * BLOCK, HD), "x").reshape(XN, ZN, BLOCK, HD)
    partial = pl.pallas_call(
        merge,
        grid=(ZN,),
        out_shape=jax.ShapeDtypeStruct((ZN, BLOCK, HD), jnp.float32),
        in_specs=[pl.BlockSpec((XN, 1, BLOCK, HD), lambda i: (0, i, 0, 0))],
        out_specs=pl.BlockSpec((1, BLOCK, HD), lambda i: (i, 0, 0)),
    )(partial)
    partial = exchange(partial, "z")
    attended = pl.pallas_call(
        finish,
        out_shape=jax.ShapeDtypeStruct((SB, HEADS * HD), jnp.bfloat16),
        in_specs=[vmem] * 4,
        out_specs=vmem,
        scratch_shapes=[pltpu.VMEM((SB, HEADS * HD), jnp.float32)],
    )(partial, queries, key_chain, value_chain)

    attended = spread(attended, "z", ZN).reshape(rows, HEADS * HD)
    turned = spread(w_out.T, "x", XN)
    turned = spread(turned, "core", CN)
    turned = turned.reshape(CN, XN, width_part, -1).transpose(1, 0, 2, 3).reshape(gathered, -1)
    result = lax.dot_general(
        attended, turned, (((1,), (1,)), ((), ())), preferred_element_type=jnp.float32
    )
    result = lax.psum(result, "kv")
    result = (stream + result).astype(jnp.bfloat16)
    result = result.reshape(rows, JN, width_part).transpose(1, 0, 2)
    result = jnp.concatenate([result[:, :half], result[:, half:]], axis=2)
    result = exchange(result, XC)
    result = jnp.concatenate([result[:, :, :width_part], result[:, :, width_part:]], axis=1)
    result = result.reshape(JN, ZN, STEPS, GROUP, width_part).transpose(2, 1, 0, 3, 4)
    return (result.reshape(STEPS, beams, width_part), appended)


def solution(mesh):
    fine = Mesh(mesh.devices.reshape(-1, ZN, XN, CN), ("kv",) + BLK)
    return jax.shard_map(
        body,
        mesh=fine,
        in_specs=(
            P(None, None, BLK),
            P(BLK),
            P(BLK, "kv"),
            P(BLK, "kv"),
            P(BLK, "kv"),
            P("kv", BLK),
            P(BLK, "kv", None, None, None),
            P(),
            P(),
            P(),
        ),
        out_specs=(P(None, None, BLK), P(None, BLK, "kv", None, None)),
        check_vma=False,
    )
```

```python
import functools
import math

import jax
import jax.numpy as jnp
from jax import lax
from jax.experimental import pallas as pl
from jax.experimental.pallas import tpu as pltpu
from jax.sharding import Mesh
from jax.sharding import PartitionSpec as P

GROUP = 8
NEGATIVE = -1e30
EPSILON = 1e-05
ROPE_BASE = 5000000.0
STEPS = 3
HEADS = 8
HD = 128
SB = STEPS * GROUP
ROWS = HEADS * SB
BLOCK = ROWS + 3 * GROUP
ZN, XN, CN = 8, 4, 2
JN = XN * CN
KN = 4
PART = 64
QUARTER = ZN * SB // KN
PAIRS = [(s, u) for s in range(STEPS) for u in range(s + 1)]
SCALE = 1.0 / math.sqrt(HD)
XC = ("x", "core")
BLK = ("z", "x", "core")


def exchange(value, axis):
    return lax.all_to_all(value, axis, 0, 0, tiled=True)


def spread(value, axis, count):
    return exchange(jnp.broadcast_to(value[None], (count,) + value.shape), axis)


def ring(value):
    own = [value]
    for hop in range(1, XN):
        own.append(lax.ppermute(value, "x", [(i, (i + hop) % XN) for i in range(XN)]))
    return own + [lax.ppermute(part, "core", [(0, 1), (1, 0)]) for part in own]


def join(place_ref, chunks, wide):
    core = place_ref[1]
    for hop in range(XN):
        wide[hop, pl.ds(pl.multiple_of(core * PART, PART), PART), :] = chunks[hop][...]
        wide[hop, pl.ds(pl.multiple_of((1 - core) * PART, PART), PART), :] = chunks[XN + hop][...]


def project(place_ref, rows_ref, *rest):
    chunks, out_ref, wide = rest[: 2 * XN], rest[2 * XN], rest[2 * XN + 1]
    join(place_ref, chunks, wide)
    x = place_ref[0]
    for start in range(0, out_ref.shape[1], 256):
        out_ref[:, start : start + 256] = sum(
            jnp.dot(
                rows_ref[(x + XN - hop) % XN],
                wide[hop, :, start : start + 256],
                preferred_element_type=jnp.float32,
            )
            for hop in range(XN)
        )


def deliver(place_ref, rows_ref, *rest):
    chunks, out_ref, wide = rest[: 2 * XN], rest[2 * XN], rest[2 * XN + 1]
    join(place_ref, chunks, wide)
    x = place_ref[0]
    for hop in range(XN):
        result = lax.dot_general(
            rows_ref[...],
            wide[hop],
            (((1,), (1,)), ((), ())),
            preferred_element_type=jnp.float32,
        )
        for kv in range(KN):
            out_ref[kv, (x + XN - hop) % XN] = result[kv * QUARTER : (kv + 1) * QUARTER]


def settle(place_ref, parts_ref, stream_ref, out_ref):
    kv = place_ref[2]
    lanes = lax.broadcasted_iota(jnp.int32, (SB, 2 * PART), 1)
    for x in range(XN):
        total = parts_ref[0, x]
        for source in range(1, KN):
            total = total + parts_ref[source, x]
        total = stream_ref[x, pl.ds(pl.multiple_of(kv * QUARTER, 8), QUARTER), :] + total
        upper, lower = total[:SB], total[SB:]
        first = jnp.where(lanes < PART, upper, pltpu.roll(lower, PART, 1)).astype(jnp.bfloat16)
        second = jnp.where(lanes < PART, pltpu.roll(upper, PART, 1), lower).astype(jnp.bfloat16)
        for target in range(KN):
            out_ref[target, x, 0] = first
            out_ref[target, x, 1] = second


def after_projection(
    parent_ref, parts_ref, cos_ref, sin_ref, q_ref, all_ref, k_ref, v_ref, hold
):
    total = parts_ref[0]
    for source in range(1, ZN):
        total = total + parts_ref[source]
    cosines = cos_ref[...]
    sines = sin_ref[...]

    def turn(part):
        return part * cosines + pltpu.roll(part, HD // 2, 1) * sines

    for head in range(HEADS):
        hold[head * SB : (head + 1) * SB] = turn(total[:, head * HD : (head + 1) * HD])
    queries = hold[...].astype(jnp.bfloat16)
    q_ref[...] = queries
    for target in range(ZN):
        all_ref[target] = queries
    start = HEADS * HD
    fresh_key = turn(total[:, start : start + HD]).astype(jnp.bfloat16).astype(jnp.float32)
    fresh_value = total[:, start + HD :].astype(jnp.bfloat16).astype(jnp.float32)
    for index, (step, token) in enumerate(PAIRS):
        for ref, fresh in ((k_ref, fresh_key), (v_ref, fresh_value)):
            if token == step:
                ref[index] = fresh[step * GROUP : (step + 1) * GROUP]
            else:
                before = PAIRS.index((step - 1, token))
                for beam in range(GROUP):
                    parent = parent_ref[step * GROUP + beam]
                    ref[index, pl.ds(beam, 1), :] = ref[before, pl.ds(parent, 1), :]


def attention(
    owner_ref,
    group_ref,
    count_ref,
    q_ref,
    root_ref,
    own_ref,
    other_ref,
    out_ref,
    top_ref,
    sum_ref,
    hold,
):
    groups = ZN * XN
    top_ref[...] = jnp.full_like(top_ref, NEGATIVE)
    sum_ref[...] = jnp.zeros_like(sum_ref)
    hold[...] = jnp.zeros_like(hold)
    tokens = lax.broadcasted_iota(jnp.int32, (SB, HD), 1)
    slots = own_ref.shape[0]

    def visit(cache_ref, offset):
        def step(slot, carry):
            count = count_ref[offset + slot]

            @pl.when(count > 0)
            def _():
                group = group_ref[offset + slot]
                owner = owner_ref[offset + slot]
                keys = cache_ref[slot, 0]
                values = cache_ref[slot, 1]
                live = (root_ref[group] == owner) & (tokens < count)
                live = jnp.concatenate([live] * HEADS, axis=0)
                scores = (
                    lax.dot_general(
                        q_ref[group],
                        keys,
                        (((1,), (1,)), ((), ())),
                        preferred_element_type=jnp.float32,
                    )
                    * SCALE
                )
                scores = jnp.where(live, scores, NEGATIVE)
                old = top_ref[group]
                new = jnp.maximum(old, jnp.max(scores, axis=1, keepdims=True))
                weights = jnp.where(live, jnp.exp(scores - new), 0.0)
                fade = jnp.exp(old - new)
                top_ref[group] = new
                sum_ref[group] = sum_ref[group] * fade + jnp.sum(weights, axis=1, keepdims=True)
                hold[group] = hold[group] * fade + jnp.dot(
                    weights.astype(jnp.bfloat16), values, preferred_element_type=jnp.float32
                )

            return carry

        lax.fori_loop(0, slots, step, 0)

    visit(own_ref, 0)
    visit(other_ref, slots)
    lanes = lax.broadcasted_iota(jnp.int32, (GROUP, HD), 1)

    def pack(group, carry):
        tile = jnp.zeros((GROUP, HD), jnp.float32)
        for part in range(HEADS * STEPS):
            rows = slice(part * GROUP, (part + 1) * GROUP)
            tile = jnp.where(lanes == part, top_ref[group, rows, :], tile)
            tile = jnp.where(lanes == part + HD // 2, sum_ref[group, rows, :], tile)
        out_ref[group] = seal([hold[group]], tile)
        return carry

    lax.fori_loop(0, groups, pack, 0)


def seal(sums, stat):
    high = stat.astype(jnp.bfloat16).astype(jnp.float32)
    middle = (stat - high).astype(jnp.bfloat16).astype(jnp.float32)
    low = stat - high - middle
    return jnp.concatenate(sums + [high, middle, low], axis=0).astype(jnp.bfloat16)


def unseal(block):
    block = block.astype(jnp.float32)
    stat = block[ROWS : ROWS + GROUP] + block[ROWS + GROUP : ROWS + 2 * GROUP]
    return block[:ROWS], stat + block[ROWS + 2 * GROUP :]


def merge(parts_ref, out_ref):
    count = parts_ref.shape[0]
    sums, stats = zip(*[unseal(parts_ref[source, 0]) for source in range(count)])
    top = functools.reduce(jnp.maximum, stats)
    fades = [jnp.exp(stat - top) for stat in stats]
    total = sum(fade * pltpu.roll(stat, HD // 2, 1) for fade, stat in zip(fades, stats))
    lanes = lax.broadcasted_iota(jnp.int32, (GROUP, HD), 1)
    stat = jnp.where(lanes < HD // 2, top, pltpu.roll(total, HD // 2, 1))
    merged = []
    for part in range(HEADS * STEPS):
        rows = slice(part * GROUP, (part + 1) * GROUP)
        merged.append(
            sum(fades[source][:, part : part + 1] * sums[source][rows] for source in range(count))
        )
    out_ref[0] = seal(merged, stat)


def finish(parts_ref, q_ref, k_ref, v_ref, out_ref, hold):
    count = parts_ref.shape[0]
    sums, stats = zip(*[unseal(parts_ref[source]) for source in range(count)])
    cached_top = functools.reduce(jnp.maximum, stats)
    queries = q_ref[...].astype(jnp.float32)
    lanes = lax.broadcasted_iota(jnp.int32, (GROUP, HD), 1)
    fresh = {}
    tops = cached_top
    for head in range(HEADS):
        for step in range(STEPS):
            part = head * STEPS + step
            row = head * SB + step * GROUP
            tile = queries[row : row + GROUP]
            for token in range(step + 1):
                key = k_ref[PAIRS.index((step, token))]
                score = jnp.sum(tile * key, axis=1, keepdims=True) * SCALE
                fresh[part, token] = score
                tops = jnp.where(lanes == part, jnp.maximum(tops, score), tops)
    fades = [jnp.exp(stat - tops) for stat in stats]
    total = sum(fade * pltpu.roll(stat, HD // 2, 1) for fade, stat in zip(fades, stats))
    for head in range(HEADS):
        for step in range(STEPS):
            part = head * STEPS + step
            rows = slice(part * GROUP, (part + 1) * GROUP)
            ceiling = tops[:, part : part + 1]
            below = total[:, part : part + 1]
            above = sum(
                fades[source][:, part : part + 1] * sums[source][rows] for source in range(count)
            )
            for token in range(step + 1):
                weight = jnp.exp(fresh[part, token] - ceiling)
                below = below + weight
                above = above + weight.astype(jnp.bfloat16).astype(jnp.float32) * v_ref[
                    PAIRS.index((step, token))
                ]
            hold[step * GROUP : (step + 1) * GROUP, head * HD : (head + 1) * HD] = above / below
    attended = hold[...].astype(jnp.bfloat16)
    for target in range(ZN):
        out_ref[target] = attended


def compose(parents_near):
    digits = jnp.arange(GROUP, dtype=jnp.int32)
    roots = [parents_near[0]]
    for step in range(1, STEPS):
        pick = parents_near[step][:, :, None] == digits
        roots.append(jnp.sum(jnp.where(pick, roots[-1][:, None, :], 0), axis=-1))
    return jnp.stack(roots)


def body(
    embeds, attn_gain, w_query, w_key, w_value, w_out, cache_kv, lengths, block_table, parents
):
    z = lax.axis_index("z")
    x = lax.axis_index("x")
    core = lax.axis_index("core")
    here = (z * XN + x) * CN + core
    groups = ZN * JN
    beams = groups * GROUP
    slots = cache_kv.shape[0]
    width = PART * groups

    weights = ring(jnp.concatenate([w_query, w_key, w_value], axis=1))
    turned = ring(w_out.T)
    place = jnp.stack([x, core, lax.axis_index("kv")]).astype(jnp.int32)
    vmem = pl.BlockSpec(memory_space=pltpu.VMEM)
    smem = pl.BlockSpec(memory_space=pltpu.SMEM)
    cache = cache_kv[:, 0]
    other_cache = lax.ppermute(cache, "core", [(0, 1), (1, 0)])

    base = jnp.arange(groups, dtype=jnp.int32)[None, :, None] * GROUP
    parents_near = parents.reshape(STEPS, groups, GROUP) - base
    roots_near = compose(parents_near)
    roots = roots_near + base
    length_of = lengths.reshape(groups, GROUP)
    own_roots = lax.dynamic_slice_in_dim(roots_near, here, 1, 1)[:, 0]
    own_parents = lax.dynamic_slice_in_dim(parents_near, here, 1, 1)[:, 0]
    own_lengths = lax.dynamic_slice_in_dim(length_of, here, 1, 0)[0]
    digits = jnp.arange(GROUP, dtype=jnp.int32)
    position = jnp.sum(
        jnp.where(own_roots[:, :, None] == digits, own_lengths[None, None, :], 0), axis=-1
    ) + jnp.arange(STEPS, dtype=jnp.int32)[:, None]
    exponent = jnp.arange(HD // 2, dtype=jnp.float32) * (2.0 / HD)
    frequency = ROPE_BASE ** (-exponent)
    angles = position.reshape(SB).astype(jnp.float32)[:, None] * frequency[None, :]
    cosines = jnp.cos(angles)
    sines = jnp.sin(angles)
    cosines = jnp.concatenate([cosines, cosines], axis=1)
    sines = jnp.concatenate([-sines, sines], axis=1)
    own_ids = here * slots + jnp.arange(slots, dtype=jnp.int32)
    other_ids = (here + 1 - 2 * core) * slots + jnp.arange(slots, dtype=jnp.int32)
    ids = jnp.concatenate([own_ids, other_ids])
    table = block_table.reshape(-1, 128)
    codes = jnp.arange(table.size, dtype=jnp.int32).reshape(table.shape)
    code = jnp.max(jnp.where(table[None] == ids[:, None, None], codes[None], -1), axis=(1, 2))
    spans = jnp.broadcast_to(lengths[:, None], block_table.shape).reshape(table.shape)
    span = jnp.max(jnp.where(table[None] == ids[:, None, None], spans[None], 0), axis=(1, 2))
    owner = code // block_table.shape[1]
    count = span - (code % block_table.shape[1]) * HD
    group = owner // GROUP
    mine = (code >= 0) & (group % CN == core)
    count = jnp.where(mine, count, 0)
    group = jnp.where(mine, (group // CN % XN) * ZN + group // JN, 0)
    root_tiles = lax.dynamic_slice_in_dim(roots.reshape(STEPS, ZN, XN, CN, GROUP), core, 1, 3)
    root_tiles = root_tiles[:, :, :, 0].transpose(2, 1, 0, 3).reshape(ZN * XN, SB)
    root_tiles = jnp.broadcast_to(root_tiles[:, :, None], (ZN * XN, SB, HD))

    rows = ZN * SB
    half = rows // 2
    by_row = embeds.reshape(STEPS, ZN // 2, 2, JN, GROUP, PART).transpose(3, 1, 0, 4, 2, 5)
    by_row = by_row.reshape(JN, half, 2 * PART)
    high = lax.reduce_precision(attn_gain, 8, 7)
    middle = lax.reduce_precision(attn_gain - high, 8, 7)
    low = attn_gain - high - middle
    gain_rows = jnp.stack(
        [jnp.concatenate([high, middle]), jnp.concatenate([low, jnp.zeros_like(low)])]
    ).astype(jnp.bfloat16)
    gain_rows = jnp.concatenate([gain_rows, jnp.zeros((6, HD), jnp.bfloat16)])
    packed = jnp.concatenate([by_row, jnp.broadcast_to(gain_rows[None], (JN, 8, HD))], axis=1)
    packed = exchange(packed, XC)
    stream = packed[:, :half].reshape(XN, CN, ZN // 2, SB, 2, PART).transpose(0, 2, 4, 3, 1, 5)
    stream = stream.reshape(XN, rows, 2 * PART).astype(jnp.float32)
    tails = packed[:, half : half + 2].astype(jnp.float32)
    gain = tails[:, 0, :PART] + tails[:, 0, PART:] + tails[:, 1, :PART]
    gain = gain.reshape(XN, 1, 2 * PART)
    squares = jnp.sum(stream * stream, axis=(0, 2))
    squares = jnp.pad(squares, (0, 256 - rows)).reshape(2, 128)
    squares = jnp.sum(spread(squares, "z", ZN), axis=0).reshape(256)[:rows]
    inverse = lax.rsqrt(squares / width + EPSILON)
    normed = (stream * inverse[None, :, None] * gain).astype(jnp.bfloat16)
    columns = weights[0].shape[1]
    projected = pl.pallas_call(
        project,
        out_shape=jax.ShapeDtypeStruct((rows, columns), jnp.float32),
        in_specs=[smem] + [vmem] * (1 + 2 * XN),
        out_specs=vmem,
        scratch_shapes=[pltpu.VMEM((XN, 2 * PART, columns), jnp.bfloat16)],
    )(place, normed, *weights)
    projected = exchange(projected.reshape(ZN, SB, columns), "z")

    small = jax.ShapeDtypeStruct((len(PAIRS), GROUP, HD), jnp.float32)
    queries, everyone, key_chain, value_chain = pl.pallas_call(
        after_projection,
        out_shape=(
            jax.ShapeDtypeStruct((ROWS, HD), jnp.bfloat16),
            jax.ShapeDtypeStruct((ZN, ROWS, HD), jnp.bfloat16),
            small,
            small,
        ),
        in_specs=[smem, vmem, vmem, vmem],
        out_specs=(vmem,) * 4,
        scratch_shapes=[pltpu.VMEM((ROWS, HD), jnp.float32)],
    )(own_parents.reshape(SB), projected, cosines, sines)
    last = PAIRS.index((STEPS - 1, 0))
    appended = jnp.stack([key_chain[last:], value_chain[last:]], axis=2)
    appended = appended[:, :, None].astype(jnp.bfloat16)

    everyone = exchange(everyone, "z")
    everyone = spread(everyone.reshape(ZN * ROWS, HD), "x", XN).reshape(XN * ZN, ROWS, HD)
    partial = pl.pallas_call(
        attention,
        out_shape=jax.ShapeDtypeStruct((XN * ZN, BLOCK, HD), jnp.bfloat16),
        in_specs=[smem, smem, smem, vmem, vmem, vmem, vmem],
        out_specs=vmem,
        scratch_shapes=[
            pltpu.VMEM((XN * ZN, ROWS, HD), jnp.float32),
            pltpu.VMEM((XN * ZN, ROWS, HD), jnp.float32),
            pltpu.VMEM((XN * ZN, ROWS, HD), jnp.float32),
        ],
        compiler_params=pltpu.CompilerParams(vmem_limit_bytes=40 << 20),
    )(owner, group, count, everyone, root_tiles, cache, other_cache)

    partial = exchange(partial.reshape(XN, ZN * BLOCK, HD), "x").reshape(XN, ZN, BLOCK, HD)
    partial = pl.pallas_call(
        merge,
        grid=(ZN,),
        out_shape=jax.ShapeDtypeStruct((ZN, BLOCK, HD), jnp.bfloat16),
        in_specs=[pl.BlockSpec((XN, 1, BLOCK, HD), lambda i: (0, i, 0, 0))],
        out_specs=pl.BlockSpec((1, BLOCK, HD), lambda i: (i, 0, 0)),
    )(partial)
    partial = exchange(partial, "z")
    attended = pl.pallas_call(
        finish,
        out_shape=jax.ShapeDtypeStruct((ZN, SB, HEADS * HD), jnp.bfloat16),
        in_specs=[vmem] * 4,
        out_specs=vmem,
        scratch_shapes=[pltpu.VMEM((SB, HEADS * HD), jnp.float32)],
    )(partial, queries, key_chain, value_chain)

    attended = exchange(attended, "z").reshape(rows, HEADS * HD)
    result = pl.pallas_call(
        deliver,
        out_shape=jax.ShapeDtypeStruct((KN, XN, QUARTER, 2 * PART), jnp.float32),
        in_specs=[smem] + [vmem] * (1 + 2 * XN),
        out_specs=vmem,
        scratch_shapes=[pltpu.VMEM((XN, 2 * PART, HEADS * HD), jnp.bfloat16)],
    )(place, attended, *turned)
    result = exchange(result, "kv")
    result = pl.pallas_call(
        settle,
        out_shape=jax.ShapeDtypeStruct((KN, XN, CN, SB, 2 * PART), jnp.bfloat16),
        in_specs=[smem, vmem, vmem],
        out_specs=vmem,
    )(place, result, stream)
    result = exchange(result.reshape(KN * JN, SB, 2 * PART), ("kv",) + XC)
    result = result.reshape(KN, JN, STEPS, GROUP, 2, PART).transpose(2, 0, 4, 1, 3, 5)
    return (result.reshape(STEPS, beams, PART), appended)


def solution(mesh):
    fine = Mesh(mesh.devices.reshape(-1, ZN, XN, CN), ("kv",) + BLK)
    return jax.shard_map(
        body,
        mesh=fine,
        in_specs=(
            P(None, None, BLK),
            P(BLK),
            P(BLK, "kv"),
            P(BLK, "kv"),
            P(BLK, "kv"),
            P("kv", BLK),
            P(BLK, "kv", None, None, None),
            P(),
            P(),
            P(),
        ),
        out_specs=(P(None, None, BLK), P(None, BLK, "kv", None, None)),
        check_vma=False,
    )
```

```python
import functools
import math

import jax
import jax.numpy as jnp
from jax import lax
from jax.experimental import pallas as pl
from jax.experimental.pallas import tpu as pltpu
from jax.sharding import Mesh
from jax.sharding import PartitionSpec as P

GROUP = 8
NEGATIVE = -1e30
EPSILON = 1e-05
ROPE_BASE = 5000000.0
STEPS = 3
HEADS = 8
HD = 128
SB = STEPS * GROUP
ROWS = HEADS * SB
BLOCK = ROWS + 3 * GROUP
ZN, XN, CN = 8, 4, 2
JN = XN * CN
KN = 4
PART = 64
PAIR = GROUP // KN
PAIRS = [(s, u) for s in range(STEPS) for u in range(s + 1)]
SCALE = 1.0 / math.sqrt(HD)
XC = ("x", "core")
BLK = ("z", "x", "core")


def exchange(value, axis):
    return lax.all_to_all(value, axis, 0, 0, tiled=True)


def spread(value, axis, count):
    return exchange(jnp.broadcast_to(value[None], (count,) + value.shape), axis)


def ring(value):
    own = [value]
    for hop in range(1, XN):
        own.append(lax.ppermute(value, "x", [(i, (i + hop) % XN) for i in range(XN)]))
    return own + [lax.ppermute(part, "core", [(0, 1), (1, 0)]) for part in own]


def join(place_ref, chunks, wide):
    core = place_ref[1]
    for hop in range(XN):
        wide[hop, pl.ds(pl.multiple_of(core * PART, PART), PART), :] = chunks[hop][...]
        wide[hop, pl.ds(pl.multiple_of((1 - core) * PART, PART), PART), :] = chunks[XN + hop][...]


def project(place_ref, rows_ref, *rest):
    chunks, out_ref, wide = rest[: 2 * XN], rest[2 * XN], rest[2 * XN + 1]
    join(place_ref, chunks, wide)
    x = place_ref[0]
    for start in range(0, out_ref.shape[1], 256):
        out_ref[:, start : start + 256] = sum(
            jnp.dot(
                rows_ref[(x + XN - hop) % XN],
                wide[hop, :, start : start + 256],
                preferred_element_type=jnp.float32,
            )
            for hop in range(XN)
        )


def collect(place_ref, *rest):
    join(place_ref, rest[: 2 * XN], rest[2 * XN + 1])
    x = place_ref[0]
    for hop in range(XN):
        start = pl.multiple_of((x + XN - hop) % XN * 2 * PART, 2 * PART)
        rest[2 * XN][pl.ds(start, 2 * PART), :] = rest[2 * XN + 1][hop]


def deliver(place_ref, parts_ref, stream_ref, *rest):
    wides, out_ref = rest[:KN], rest[KN]
    kv = place_ref[2]
    count = ZN * GROUP
    lanes = lax.broadcasted_iota(jnp.int32, (count // 2, 2 * PART), 1)
    for x in range(XN):
        columns = slice(x * 2 * PART, (x + 1) * 2 * PART)
        total = stream_ref[x] + sum(
            lax.dot_general(
                parts_ref[(kv + KN - hop) % KN],
                wides[hop][columns, :],
                (((1,), (1,)), ((), ())),
                preferred_element_type=jnp.float32,
            )
            for hop in range(KN)
        )
        upper, lower = total[: count // 2], total[count // 2 :]
        first = jnp.where(lanes < PART, upper, pltpu.roll(lower, PART, 1)).astype(jnp.bfloat16)
        second = jnp.where(lanes < PART, pltpu.roll(upper, PART, 1), lower).astype(jnp.bfloat16)
        for target in range(KN):
            out_ref[target, x, 0] = first
            out_ref[target, x, 1] = second


def after_projection(
    parent_ref, parts_ref, cos_ref, sin_ref, q_ref, all_ref, k_ref, v_ref, hold
):
    total = parts_ref[0]
    for source in range(1, ZN):
        total = total + parts_ref[source]
    cosines = cos_ref[...]
    sines = sin_ref[...]

    def turn(part):
        return part * cosines + pltpu.roll(part, HD // 2, 1) * sines

    for head in range(HEADS):
        hold[head * SB : (head + 1) * SB] = turn(total[:, head * HD : (head + 1) * HD])
    queries = hold[...].astype(jnp.bfloat16)
    q_ref[...] = queries
    for target in range(ZN):
        all_ref[target] = queries
    start = HEADS * HD
    fresh_key = turn(total[:, start : start + HD]).astype(jnp.bfloat16).astype(jnp.float32)
    fresh_value = total[:, start + HD :].astype(jnp.bfloat16).astype(jnp.float32)
    for index, (step, token) in enumerate(PAIRS):
        for ref, fresh in ((k_ref, fresh_key), (v_ref, fresh_value)):
            if token == step:
                ref[index] = fresh[step * GROUP : (step + 1) * GROUP]
            else:
                before = PAIRS.index((step - 1, token))
                for beam in range(GROUP):
                    parent = parent_ref[step * GROUP + beam]
                    ref[index, pl.ds(beam, 1), :] = ref[before, pl.ds(parent, 1), :]


def attention(
    owner_ref,
    group_ref,
    count_ref,
    q_ref,
    root_ref,
    own_ref,
    other_ref,
    out_ref,
    top_ref,
    sum_ref,
    hold,
):
    groups = ZN * XN
    top_ref[...] = jnp.full_like(top_ref, NEGATIVE)
    sum_ref[...] = jnp.zeros_like(sum_ref)
    hold[...] = jnp.zeros_like(hold)
    tokens = lax.broadcasted_iota(jnp.int32, (SB, HD), 1)
    slots = own_ref.shape[0]

    def visit(cache_ref, offset):
        def step(slot, carry):
            count = count_ref[offset + slot]

            @pl.when(count > 0)
            def _():
                group = group_ref[offset + slot]
                owner = owner_ref[offset + slot]
                keys = cache_ref[slot, 0]
                values = cache_ref[slot, 1]
                live = (root_ref[group] == owner) & (tokens < count)
                live = jnp.concatenate([live] * HEADS, axis=0)
                scores = (
                    lax.dot_general(
                        q_ref[group],
                        keys,
                        (((1,), (1,)), ((), ())),
                        preferred_element_type=jnp.float32,
                    )
                    * SCALE
                )
                scores = jnp.where(live, scores, NEGATIVE)
                old = top_ref[group]
                new = jnp.maximum(old, jnp.max(scores, axis=1, keepdims=True))
                weights = jnp.where(live, jnp.exp(scores - new), 0.0)
                fade = jnp.exp(old - new)
                top_ref[group] = new
                sum_ref[group] = sum_ref[group] * fade + jnp.sum(weights, axis=1, keepdims=True)
                hold[group] = hold[group] * fade + jnp.dot(
                    weights.astype(jnp.bfloat16), values, preferred_element_type=jnp.float32
                )

            return carry

        lax.fori_loop(0, slots, step, 0)

    visit(own_ref, 0)
    visit(other_ref, slots)
    lanes = lax.broadcasted_iota(jnp.int32, (GROUP, HD), 1)

    def pack(group, carry):
        tile = jnp.zeros((GROUP, HD), jnp.float32)
        for part in range(HEADS * STEPS):
            rows = slice(part * GROUP, (part + 1) * GROUP)
            tile = jnp.where(lanes == part, top_ref[group, rows, :], tile)
            tile = jnp.where(lanes == part + HD // 2, sum_ref[group, rows, :], tile)
        out_ref[group] = seal([hold[group]], tile)
        return carry

    lax.fori_loop(0, groups, pack, 0)


def seal(sums, stat):
    high = stat.astype(jnp.bfloat16).astype(jnp.float32)
    middle = (stat - high).astype(jnp.bfloat16).astype(jnp.float32)
    low = stat - high - middle
    return jnp.concatenate(sums + [high, middle, low], axis=0).astype(jnp.bfloat16)


def unseal(block):
    block = block.astype(jnp.float32)
    stat = block[ROWS : ROWS + GROUP] + block[ROWS + GROUP : ROWS + 2 * GROUP]
    return block[:ROWS], stat + block[ROWS + 2 * GROUP :]


def merge(parts_ref, out_ref):
    count = parts_ref.shape[0]
    sums, stats = zip(*[unseal(parts_ref[source, 0]) for source in range(count)])
    top = functools.reduce(jnp.maximum, stats)
    fades = [jnp.exp(stat - top) for stat in stats]
    total = sum(fade * pltpu.roll(stat, HD // 2, 1) for fade, stat in zip(fades, stats))
    lanes = lax.broadcasted_iota(jnp.int32, (GROUP, HD), 1)
    stat = jnp.where(lanes < HD // 2, top, pltpu.roll(total, HD // 2, 1))
    merged = []
    for part in range(HEADS * STEPS):
        rows = slice(part * GROUP, (part + 1) * GROUP)
        merged.append(
            sum(fades[source][:, part : part + 1] * sums[source][rows] for source in range(count))
        )
    out_ref[0] = seal(merged, stat)


def finish(parts_ref, q_ref, k_ref, v_ref, out_ref, hold, shares):
    count = parts_ref.shape[0]
    sums, stats = zip(*[unseal(parts_ref[source]) for source in range(count)])
    cached_top = functools.reduce(jnp.maximum, stats)
    queries = q_ref[...].astype(jnp.float32)
    lanes = lax.broadcasted_iota(jnp.int32, (GROUP, HD), 1)
    fresh = {}
    tops = cached_top
    for head in range(HEADS):
        for step in range(STEPS):
            part = head * STEPS + step
            row = head * SB + step * GROUP
            tile = queries[row : row + GROUP]
            for token in range(step + 1):
                key = k_ref[PAIRS.index((step, token))]
                score = jnp.sum(tile * key, axis=1, keepdims=True) * SCALE
                fresh[part, token] = score
                tops = jnp.where(lanes == part, jnp.maximum(tops, score), tops)
    fades = [jnp.exp(stat - tops) for stat in stats]
    total = sum(fade * pltpu.roll(stat, HD // 2, 1) for fade, stat in zip(fades, stats))
    for head in range(HEADS):
        for step in range(STEPS):
            part = head * STEPS + step
            rows = slice(part * GROUP, (part + 1) * GROUP)
            ceiling = tops[:, part : part + 1]
            below = total[:, part : part + 1]
            above = sum(
                fades[source][:, part : part + 1] * sums[source][rows] for source in range(count)
            )
            for token in range(step + 1):
                weight = jnp.exp(fresh[part, token] - ceiling)
                below = below + weight
                above = above + weight.astype(jnp.bfloat16).astype(jnp.float32) * v_ref[
                    PAIRS.index((step, token))
                ]
            hold[step * GROUP : (step + 1) * GROUP, head * HD : (head + 1) * HD] = above / below
    shares[...] = jnp.zeros_like(shares)
    for kv in range(KN):
        for step in range(STEPS):
            row = step * GROUP + kv * PAIR
            shares[kv, step * PAIR : (step + 1) * PAIR, :] = hold[row : row + PAIR, :]
    for kv in range(KN):
        share = shares[kv].astype(jnp.bfloat16)
        for target in range(ZN):
            out_ref[kv, target] = share


def compose(parents_near):
    digits = jnp.arange(GROUP, dtype=jnp.int32)
    roots = [parents_near[0]]
    for step in range(1, STEPS):
        pick = parents_near[step][:, :, None] == digits
        roots.append(jnp.sum(jnp.where(pick, roots[-1][:, None, :], 0), axis=-1))
    return jnp.stack(roots)


def body(
    embeds, attn_gain, w_query, w_key, w_value, w_out, cache_kv, lengths, block_table, parents
):
    z = lax.axis_index("z")
    x = lax.axis_index("x")
    core = lax.axis_index("core")
    here = (z * XN + x) * CN + core
    groups = ZN * JN
    beams = groups * GROUP
    slots = cache_kv.shape[0]
    width = PART * groups

    weights = ring(jnp.concatenate([w_query, w_key, w_value], axis=1))
    turned = ring(w_out.T)
    kv = lax.axis_index("kv")
    place = jnp.stack([x, core, kv]).astype(jnp.int32)
    vmem = pl.BlockSpec(memory_space=pltpu.VMEM)
    smem = pl.BlockSpec(memory_space=pltpu.SMEM)
    cache = cache_kv[:, 0]
    other_cache = lax.ppermute(cache, "core", [(0, 1), (1, 0)])

    base = jnp.arange(groups, dtype=jnp.int32)[None, :, None] * GROUP
    parents_near = parents.reshape(STEPS, groups, GROUP) - base
    roots_near = compose(parents_near)
    roots = roots_near + base
    length_of = lengths.reshape(groups, GROUP)
    own_roots = lax.dynamic_slice_in_dim(roots_near, here, 1, 1)[:, 0]
    own_parents = lax.dynamic_slice_in_dim(parents_near, here, 1, 1)[:, 0]
    own_lengths = lax.dynamic_slice_in_dim(length_of, here, 1, 0)[0]
    digits = jnp.arange(GROUP, dtype=jnp.int32)
    position = jnp.sum(
        jnp.where(own_roots[:, :, None] == digits, own_lengths[None, None, :], 0), axis=-1
    ) + jnp.arange(STEPS, dtype=jnp.int32)[:, None]
    exponent = jnp.arange(HD // 2, dtype=jnp.float32) * (2.0 / HD)
    frequency = ROPE_BASE ** (-exponent)
    angles = position.reshape(SB).astype(jnp.float32)[:, None] * frequency[None, :]
    cosines = jnp.cos(angles)
    sines = jnp.sin(angles)
    cosines = jnp.concatenate([cosines, cosines], axis=1)
    sines = jnp.concatenate([-sines, sines], axis=1)
    own_ids = here * slots + jnp.arange(slots, dtype=jnp.int32)
    other_ids = (here + 1 - 2 * core) * slots + jnp.arange(slots, dtype=jnp.int32)
    ids = jnp.concatenate([own_ids, other_ids])
    table = block_table.reshape(-1, 128)
    codes = jnp.arange(table.size, dtype=jnp.int32).reshape(table.shape)
    code = jnp.max(jnp.where(table[None] == ids[:, None, None], codes[None], -1), axis=(1, 2))
    spans = jnp.broadcast_to(lengths[:, None], block_table.shape).reshape(table.shape)
    span = jnp.max(jnp.where(table[None] == ids[:, None, None], spans[None], 0), axis=(1, 2))
    owner = code // block_table.shape[1]
    count = span - (code % block_table.shape[1]) * HD
    group = owner // GROUP
    mine = (code >= 0) & (group % CN == core)
    count = jnp.where(mine, count, 0)
    group = jnp.where(mine, (group // CN % XN) * ZN + group // JN, 0)
    root_tiles = lax.dynamic_slice_in_dim(roots.reshape(STEPS, ZN, XN, CN, GROUP), core, 1, 3)
    root_tiles = root_tiles[:, :, :, 0].transpose(2, 1, 0, 3).reshape(ZN * XN, SB)
    root_tiles = jnp.broadcast_to(root_tiles[:, :, None], (ZN * XN, SB, HD))

    rows = ZN * SB
    half = rows // 2
    by_row = embeds.reshape(STEPS, ZN // 2, 2, JN, GROUP, PART).transpose(3, 1, 0, 4, 2, 5)
    by_row = by_row.reshape(JN, half, 2 * PART)
    high = lax.reduce_precision(attn_gain, 8, 7)
    middle = lax.reduce_precision(attn_gain - high, 8, 7)
    low = attn_gain - high - middle
    gain_rows = jnp.stack(
        [jnp.concatenate([high, middle]), jnp.concatenate([low, jnp.zeros_like(low)])]
    ).astype(jnp.bfloat16)
    gain_rows = jnp.concatenate([gain_rows, jnp.zeros((6, HD), jnp.bfloat16)])
    packed = jnp.concatenate([by_row, jnp.broadcast_to(gain_rows[None], (JN, 8, HD))], axis=1)
    squares = jnp.sum(jnp.square(embeds.astype(jnp.float32)), axis=2)
    squares = squares.reshape(STEPS, ZN, JN, GROUP).transpose(2, 1, 0, 3).reshape(JN, rows)
    squares = jnp.pad(squares, ((0, 0), (0, 256 - rows))).reshape(JN, 2, 128)
    squares = jnp.broadcast_to(squares[None], (ZN, JN, 2, 128)).reshape(groups, 2, 128)
    squares = exchange(squares, BLK)
    packed = exchange(packed, XC)
    stream = packed[:, :half].reshape(XN, CN, ZN // 2, SB, 2, PART).transpose(0, 2, 4, 3, 1, 5)
    stream = stream.reshape(XN, rows, 2 * PART).astype(jnp.float32)
    tails = packed[:, half : half + 2].astype(jnp.float32)
    gain = tails[:, 0, :PART] + tails[:, 0, PART:] + tails[:, 1, :PART]
    gain = gain.reshape(XN, 1, 2 * PART)
    squares = jnp.sum(squares, axis=0).reshape(256)[:rows]
    inverse = lax.rsqrt(squares / width + EPSILON)
    normed = (stream * inverse[None, :, None] * gain).astype(jnp.bfloat16)
    columns = weights[0].shape[1]
    projected = pl.pallas_call(
        project,
        out_shape=jax.ShapeDtypeStruct((rows, columns), jnp.float32),
        in_specs=[smem] + [vmem] * (1 + 2 * XN),
        out_specs=vmem,
        scratch_shapes=[pltpu.VMEM((XN, 2 * PART, columns), jnp.bfloat16)],
    )(place, normed, *weights)
    projected = exchange(projected.reshape(ZN, SB, columns), "z")
    projected, turned = lax.optimization_barrier((projected, turned))
    wide = pl.pallas_call(
        collect,
        out_shape=jax.ShapeDtypeStruct((2 * PART * XN, HEADS * HD), jnp.bfloat16),
        in_specs=[smem] + [vmem] * (2 * XN),
        out_specs=vmem,
        scratch_shapes=[pltpu.VMEM((XN, 2 * PART, HEADS * HD), jnp.bfloat16)],
    )(place, *turned)
    wides = [wide] + [
        lax.ppermute(wide, "kv", [(i, (i + hop) % KN) for i in range(KN)])
        for hop in range(1, KN)
    ]
    shares = stream.reshape(XN, ZN, STEPS, KN, PAIR, 2 * PART)
    shares = lax.dynamic_index_in_dim(shares, kv, 3, keepdims=False)
    shares = shares.reshape(XN, ZN, STEPS * PAIR, 2 * PART)
    shares = jnp.pad(shares, ((0, 0), (0, 0), (0, GROUP - STEPS * PAIR), (0, 0)))
    shares = shares.reshape(XN, ZN * GROUP, 2 * PART)

    small = jax.ShapeDtypeStruct((len(PAIRS), GROUP, HD), jnp.float32)
    queries, everyone, key_chain, value_chain = pl.pallas_call(
        after_projection,
        out_shape=(
            jax.ShapeDtypeStruct((ROWS, HD), jnp.bfloat16),
            jax.ShapeDtypeStruct((ZN, ROWS, HD), jnp.bfloat16),
            small,
            small,
        ),
        in_specs=[smem, vmem, vmem, vmem],
        out_specs=(vmem,) * 4,
        scratch_shapes=[pltpu.VMEM((ROWS, HD), jnp.float32)],
    )(own_parents.reshape(SB), projected, cosines, sines)
    last = PAIRS.index((STEPS - 1, 0))
    appended = jnp.stack([key_chain[last:], value_chain[last:]], axis=2)
    appended = appended[:, :, None].astype(jnp.bfloat16)

    everyone = exchange(everyone, "z")
    everyone = spread(everyone.reshape(ZN * ROWS, HD), "x", XN).reshape(XN * ZN, ROWS, HD)
    partial = pl.pallas_call(
        attention,
        out_shape=jax.ShapeDtypeStruct((XN * ZN, BLOCK, HD), jnp.bfloat16),
        in_specs=[smem, smem, smem, vmem, vmem, vmem, vmem],
        out_specs=vmem,
        scratch_shapes=[
            pltpu.VMEM((XN * ZN, ROWS, HD), jnp.float32),
            pltpu.VMEM((XN * ZN, ROWS, HD), jnp.float32),
            pltpu.VMEM((XN * ZN, ROWS, HD), jnp.float32),
        ],
        compiler_params=pltpu.CompilerParams(vmem_limit_bytes=40 << 20),
    )(owner, group, count, everyone, root_tiles, cache, other_cache)

    partial = exchange(partial.reshape(XN, ZN * BLOCK, HD), "x").reshape(XN, ZN, BLOCK, HD)
    partial, wides = lax.optimization_barrier((partial, wides))
    partial = pl.pallas_call(
        merge,
        grid=(ZN,),
        out_shape=jax.ShapeDtypeStruct((ZN, BLOCK, HD), jnp.bfloat16),
        in_specs=[pl.BlockSpec((XN, 1, BLOCK, HD), lambda i: (0, i, 0, 0))],
        out_specs=pl.BlockSpec((1, BLOCK, HD), lambda i: (i, 0, 0)),
    )(partial)
    partial = exchange(partial, "z")
    attended = pl.pallas_call(
        finish,
        out_shape=jax.ShapeDtypeStruct((KN, ZN, GROUP, HEADS * HD), jnp.bfloat16),
        in_specs=[vmem] * 4,
        out_specs=vmem,
        scratch_shapes=[
            pltpu.VMEM((SB, HEADS * HD), jnp.float32),
            pltpu.VMEM((KN, GROUP, HEADS * HD), jnp.float32),
        ],
    )(partial, queries, key_chain, value_chain)

    attended = exchange(attended.reshape(KN * ZN, GROUP, HEADS * HD), ("kv", "z"))
    attended = attended.reshape(KN, ZN * GROUP, HEADS * HD)
    result = pl.pallas_call(
        deliver,
        out_shape=jax.ShapeDtypeStruct((KN, XN, CN, ZN * GROUP // 2, 2 * PART), jnp.bfloat16),
        in_specs=[smem] + [vmem] * (2 + KN),
        out_specs=vmem,
    )(place, attended, shares, *wides)
    result = exchange(result.reshape(KN * JN, ZN * GROUP // 2, 2 * PART), ("kv",) + XC)
    result = result.reshape(KN, JN, ZN // 2, GROUP, 2, PART)[:, :, :, : STEPS * PAIR]
    result = result.reshape(KN, JN, ZN // 2, STEPS, PAIR, 2, PART).transpose(3, 5, 2, 1, 0, 4, 6)
    return (result.reshape(STEPS, beams, PART), appended)


def solution(mesh):
    fine = Mesh(mesh.devices.reshape(-1, ZN, XN, CN), ("kv",) + BLK)
    return jax.shard_map(
        body,
        mesh=fine,
        in_specs=(
            P(None, None, BLK),
            P(BLK),
            P(BLK, "kv"),
            P(BLK, "kv"),
            P(BLK, "kv"),
            P("kv", BLK),
            P(BLK, "kv", None, None, None),
            P(),
            P(),
            P(),
        ),
        out_specs=(P(None, None, BLK), P(None, BLK, "kv", None, None)),
        check_vma=False,
    )
```

```python
import functools
import math

import jax
import jax.numpy as jnp
from jax import lax
from jax.experimental import pallas as pl
from jax.experimental.pallas import tpu as pltpu
from jax.sharding import Mesh
from jax.sharding import PartitionSpec as P

GROUP = 8
NEGATIVE = -1e30
EPSILON = 1e-05
ROPE_BASE = 5000000.0
STEPS = 3
HEADS = 8
HD = 128
SB = STEPS * GROUP
ROWS = HEADS * SB
BLOCK = ROWS + 3 * GROUP
ZN, XN, CN = 8, 4, 2
JN = XN * CN
KN = 4
PART = 64
SEGMENTS = 5
DEPTH = 12
QUARTER = ZN * SB // KN
PAIRS = [(s, u) for s in range(STEPS) for u in range(s + 1)]
SCALE = 1.0 / math.sqrt(HD)
XC = ("x", "core")
BLK = ("z", "x", "core")


def exchange(value, axis):
    return lax.all_to_all(value, axis, 0, 0, tiled=True)


def spread(value, axis, count):
    return exchange(jnp.broadcast_to(value[None], (count,) + value.shape), axis)


def swap(value):
    return lax.ppermute(value, "core", [(0, 1), (1, 0)])


def shift(value, hop):
    return lax.ppermute(value, "x", [(i, (i + hop) % XN) for i in range(XN)])


def ring(value):
    both = jnp.concatenate([value, swap(value)], axis=0)
    return [both] + [shift(both, hop) for hop in range(1, XN)]


def join(place_ref, chunks, wide):
    core = place_ref[1]
    for hop in range(XN):
        for side, start in ((0, core * PART), (1, (1 - core) * PART)):
            rows = pl.ds(pl.multiple_of(start, PART), PART)
            wide[hop, rows, :] = chunks[hop][side * PART : (side + 1) * PART, :]


def project(place_ref, rows_ref, *rest):
    chunks, out_ref, wide = rest[:XN], rest[XN], rest[XN + 1]
    join(place_ref, chunks, wide)
    x = place_ref[0]
    for start in range(0, out_ref.shape[1], 256):
        out_ref[:, start : start + 256] = sum(
            jnp.dot(
                rows_ref[(x + XN - hop) % XN],
                wide[hop, :, start : start + 256],
                preferred_element_type=jnp.float32,
            )
            for hop in range(XN)
        )


def deliver(place_ref, rows_ref, *rest):
    chunks, out_ref, wide = rest[:XN], rest[XN], rest[XN + 1]
    join(place_ref, chunks, wide)
    x = place_ref[0]
    for hop in range(XN):
        result = lax.dot_general(
            rows_ref[...],
            wide[hop],
            (((1,), (1,)), ((), ())),
            preferred_element_type=jnp.float32,
        )
        for kv in range(KN):
            out_ref[kv, (x + XN - hop) % XN] = result[kv * QUARTER : (kv + 1) * QUARTER]


def settle(place_ref, parts_ref, stream_ref, out_ref):
    kv = place_ref[2]
    lanes = lax.broadcasted_iota(jnp.int32, (SB, 2 * PART), 1)
    for x in range(XN):
        total = parts_ref[0, x]
        for source in range(1, KN):
            total = total + parts_ref[source, x]
        total = stream_ref[x, pl.ds(pl.multiple_of(kv * QUARTER, 8), QUARTER), :] + total
        upper, lower = total[:SB], total[SB:]
        first = jnp.where(lanes < PART, upper, pltpu.roll(lower, PART, 1)).astype(jnp.bfloat16)
        second = jnp.where(lanes < PART, pltpu.roll(upper, PART, 1), lower).astype(jnp.bfloat16)
        for target in range(KN):
            out_ref[target, x, 0] = first
            out_ref[target, x, 1] = second


def after_projection(
    parent_ref, parts_ref, cos_ref, sin_ref, q_ref, all_ref, k_ref, v_ref, hold
):
    total = parts_ref[0]
    for source in range(1, ZN):
        total = total + parts_ref[source]
    cosines = cos_ref[...]
    sines = sin_ref[...]

    def turn(part):
        return part * cosines + pltpu.roll(part, HD // 2, 1) * sines

    for head in range(HEADS):
        hold[head * SB : (head + 1) * SB] = turn(total[:, head * HD : (head + 1) * HD])
    queries = hold[...].astype(jnp.bfloat16)
    q_ref[...] = queries
    for target in range(ZN):
        all_ref[target] = queries
    start = HEADS * HD
    fresh_key = turn(total[:, start : start + HD]).astype(jnp.bfloat16).astype(jnp.float32)
    fresh_value = total[:, start + HD :].astype(jnp.bfloat16).astype(jnp.float32)
    for index, (step, token) in enumerate(PAIRS):
        for ref, fresh in ((k_ref, fresh_key), (v_ref, fresh_value)):
            if token == step:
                ref[index] = fresh[step * GROUP : (step + 1) * GROUP]
            else:
                before = PAIRS.index((step - 1, token))
                for beam in range(GROUP):
                    parent = parent_ref[step * GROUP + beam]
                    ref[index, pl.ds(beam, 1), :] = ref[before, pl.ds(parent, 1), :]


def attention(place_ref, table_ref, length_ref, q_ref, root_ref, *rest):
    caches, rest = rest[: 2 * SEGMENTS], rest[2 * SEGMENTS :]
    out_ref, top_ref, sum_ref, hold, pages, arrived, beam_list, block_list = rest
    x, core, z = place_ref[0], place_ref[1], place_ref[3]
    blocks = table_ref.shape[0] // (ZN * GROUP)
    slots = caches[0].shape[0]
    top_ref[...] = jnp.full_like(top_ref, NEGATIVE)
    sum_ref[...] = jnp.zeros_like(sum_ref)
    hold[...] = jnp.zeros_like(hold)

    def scan_beam(beam, found):
        used = (length_ref[beam] + HD - 1) // HD

        def scan_block(block, found):
            slot = table_ref[beam * blocks + block]
            near = slot // (slots * JN) == z

            @pl.when(near)
            def _():
                beam_list[found] = beam
                block_list[found] = block

            return found + near.astype(jnp.int32)

        return lax.fori_loop(0, used, scan_block, found)

    found = lax.fori_loop(0, ZN * GROUP, scan_beam, 0)

    def fetch(item):
        slot = table_ref[beam_list[item] * blocks + block_list[item]]
        lane = item % DEPTH
        offset = slot % slots
        source = slot // slots % JN
        far = (source // CN + XN - x) % XN
        foreign = jnp.where(source % CN == core, 0, 1)
        half = slots // 2
        segment = jnp.where(far == 0, 0, jnp.where(far == 3, 1, jnp.where(far == 1, 2, 3)))
        late = (segment == 3) & (offset >= half)
        segment = jnp.where(late, 4, segment) + foreign * SEGMENTS
        offset = jnp.where(late, offset - half, offset)
        for index in range(2 * SEGMENTS):

            @pl.when(segment == index)
            def _(index=index):
                pltpu.make_async_copy(
                    caches[index].at[offset], pages.at[lane], arrived.at[lane]
                ).start()

    for item in range(DEPTH):

        @pl.when(item < found)
        def _(item=item):
            fetch(item)

    tokens = lax.broadcasted_iota(jnp.int32, (SB, HD), 1)

    def visit(item, carry):
        lane = item % DEPTH
        beam = beam_list[item]
        group = beam // GROUP
        count = length_ref[beam] - block_list[item] * HD
        live = (root_ref[group] == beam % GROUP) & (tokens < count)
        live = jnp.concatenate([live] * HEADS, axis=0)
        pltpu.make_async_copy(caches[0].at[0], pages.at[lane], arrived.at[lane]).wait()
        scores = (
            lax.dot_general(
                q_ref[group],
                pages[lane, 0],
                (((1,), (1,)), ((), ())),
                preferred_element_type=jnp.float32,
            )
            * SCALE
        )
        scores = jnp.where(live, scores, NEGATIVE)
        old = top_ref[group]
        new = jnp.maximum(old, jnp.max(scores, axis=1, keepdims=True))
        weights = jnp.where(live, jnp.exp(scores - new), 0.0)
        fade = jnp.exp(old - new)
        top_ref[group] = new
        sum_ref[group] = sum_ref[group] * fade + jnp.sum(weights, axis=1, keepdims=True)
        hold[group] = hold[group] * fade + jnp.dot(
            weights.astype(jnp.bfloat16), pages[lane, 1], preferred_element_type=jnp.float32
        )

        @pl.when(item + DEPTH < found)
        def _():
            fetch(item + DEPTH)

        return carry

    lax.fori_loop(0, found, visit, 0)
    lanes = lax.broadcasted_iota(jnp.int32, (GROUP, HD), 1)

    def pack(group, carry):
        tile = jnp.zeros((GROUP, HD), jnp.float32)
        for part in range(HEADS * STEPS):
            rows = slice(part * GROUP, (part + 1) * GROUP)
            tile = jnp.where(lanes == part, top_ref[group, rows, :], tile)
            tile = jnp.where(lanes == part + HD // 2, sum_ref[group, rows, :], tile)
        out_ref[group] = seal([hold[group]], tile)
        return carry

    lax.fori_loop(0, ZN, pack, 0)


def seal(sums, stat):
    high = stat.astype(jnp.bfloat16).astype(jnp.float32)
    middle = (stat - high).astype(jnp.bfloat16).astype(jnp.float32)
    low = stat - high - middle
    return jnp.concatenate(sums + [high, middle, low], axis=0).astype(jnp.bfloat16)


def unseal(block):
    block = block.astype(jnp.float32)
    stat = block[ROWS : ROWS + GROUP] + block[ROWS + GROUP : ROWS + 2 * GROUP]
    return block[:ROWS], stat + block[ROWS + 2 * GROUP :]


def finish(parts_ref, q_ref, k_ref, v_ref, out_ref, hold):
    count = parts_ref.shape[0]
    sums, stats = zip(*[unseal(parts_ref[source]) for source in range(count)])
    cached_top = functools.reduce(jnp.maximum, stats)
    queries = q_ref[...].astype(jnp.float32)
    lanes = lax.broadcasted_iota(jnp.int32, (GROUP, HD), 1)
    fresh = {}
    tops = cached_top
    for head in range(HEADS):
        for step in range(STEPS):
            part = head * STEPS + step
            row = head * SB + step * GROUP
            tile = queries[row : row + GROUP]
            for token in range(step + 1):
                key = k_ref[PAIRS.index((step, token))]
                score = jnp.sum(tile * key, axis=1, keepdims=True) * SCALE
                fresh[part, token] = score
                tops = jnp.where(lanes == part, jnp.maximum(tops, score), tops)
    fades = [jnp.exp(stat - tops) for stat in stats]
    total = sum(fade * pltpu.roll(stat, HD // 2, 1) for fade, stat in zip(fades, stats))
    for head in range(HEADS):
        for step in range(STEPS):
            part = head * STEPS + step
            rows = slice(part * GROUP, (part + 1) * GROUP)
            ceiling = tops[:, part : part + 1]
            below = total[:, part : part + 1]
            above = sum(
                fades[source][:, part : part + 1] * sums[source][rows] for source in range(count)
            )
            for token in range(step + 1):
                weight = jnp.exp(fresh[part, token] - ceiling)
                below = below + weight
                above = above + weight.astype(jnp.bfloat16).astype(jnp.float32) * v_ref[
                    PAIRS.index((step, token))
                ]
            hold[step * GROUP : (step + 1) * GROUP, head * HD : (head + 1) * HD] = above / below
    attended = hold[...].astype(jnp.bfloat16)
    for target in range(ZN):
        out_ref[target] = attended


def compose(parents_near):
    digits = jnp.arange(GROUP, dtype=jnp.int32)
    roots = [parents_near[0]]
    for step in range(1, STEPS):
        pick = parents_near[step][:, :, None] == digits
        roots.append(jnp.sum(jnp.where(pick, roots[-1][:, None, :], 0), axis=-1))
    return jnp.stack(roots)


def body(
    embeds, attn_gain, w_query, w_key, w_value, w_out, cache_kv, lengths, block_table, parents
):
    z = lax.axis_index("z")
    x = lax.axis_index("x")
    core = lax.axis_index("core")
    here = (z * XN + x) * CN + core
    groups = ZN * JN
    beams = groups * GROUP
    half_slots = cache_kv.shape[0] // 2
    width = PART * groups

    weights = ring(jnp.concatenate([w_query, w_key, w_value], axis=1))
    turned = ring(w_out.T)
    place = jnp.stack([x, core, lax.axis_index("kv"), z]).astype(jnp.int32)
    vmem = pl.BlockSpec(memory_space=pltpu.VMEM)
    smem = pl.BlockSpec(memory_space=pltpu.SMEM)
    cache = cache_kv[:, 0]

    base = jnp.arange(groups, dtype=jnp.int32)[None, :, None] * GROUP
    parents_near = parents.reshape(STEPS, groups, GROUP) - base
    roots_near = compose(parents_near)
    length_of = lengths.reshape(groups, GROUP)
    own_roots = lax.dynamic_slice_in_dim(roots_near, here, 1, 1)[:, 0]
    own_parents = lax.dynamic_slice_in_dim(parents_near, here, 1, 1)[:, 0]
    own_lengths = lax.dynamic_slice_in_dim(length_of, here, 1, 0)[0]
    digits = jnp.arange(GROUP, dtype=jnp.int32)
    position = jnp.sum(
        jnp.where(own_roots[:, :, None] == digits, own_lengths[None, None, :], 0), axis=-1
    ) + jnp.arange(STEPS, dtype=jnp.int32)[:, None]
    exponent = jnp.arange(HD // 2, dtype=jnp.float32) * (2.0 / HD)
    frequency = ROPE_BASE ** (-exponent)
    angles = position.reshape(SB).astype(jnp.float32)[:, None] * frequency[None, :]
    cosines = jnp.cos(angles)
    sines = jnp.sin(angles)
    cosines = jnp.concatenate([cosines, cosines], axis=1)
    sines = jnp.concatenate([-sines, sines], axis=1)
    lead = x * CN + core
    table = lax.dynamic_index_in_dim(
        block_table.reshape(ZN, JN, GROUP * block_table.shape[1]), lead, 1, keepdims=False
    ).reshape(-1)
    spans = lax.dynamic_index_in_dim(lengths.reshape(ZN, JN, GROUP), lead, 1, keepdims=False)
    root_tiles = lax.dynamic_index_in_dim(
        roots_near.reshape(STEPS, ZN, JN, GROUP), lead, 2, keepdims=False
    )
    root_tiles = root_tiles.transpose(1, 0, 2).reshape(ZN, SB)
    root_tiles = jnp.broadcast_to(root_tiles[:, :, None], (ZN, SB, HD))

    rows = ZN * SB
    half = rows // 2
    by_row = embeds.reshape(STEPS, ZN // 2, 2, JN, GROUP, PART).transpose(3, 1, 0, 4, 2, 5)
    by_row = by_row.reshape(JN, half, 2 * PART)
    high = lax.reduce_precision(attn_gain, 8, 7)
    middle = lax.reduce_precision(attn_gain - high, 8, 7)
    low = attn_gain - high - middle
    gain_rows = jnp.stack(
        [jnp.concatenate([high, middle]), jnp.concatenate([low, jnp.zeros_like(low)])]
    ).astype(jnp.bfloat16)
    gain_rows = jnp.concatenate([gain_rows, jnp.zeros((6, HD), jnp.bfloat16)])
    packed = jnp.concatenate([by_row, jnp.broadcast_to(gain_rows[None], (JN, 8, HD))], axis=1)
    packed = exchange(packed, XC)
    stream = packed[:, :half].reshape(XN, CN, ZN // 2, SB, 2, PART).transpose(0, 2, 4, 3, 1, 5)
    stream = stream.reshape(XN, rows, 2 * PART).astype(jnp.float32)
    tails = packed[:, half : half + 2].astype(jnp.float32)
    gain = tails[:, 0, :PART] + tails[:, 0, PART:] + tails[:, 1, :PART]
    gain = gain.reshape(XN, 1, 2 * PART)
    squares = jnp.sum(stream * stream, axis=(0, 2))
    squares = jnp.pad(squares, (0, 256 - rows)).reshape(2, 128)
    cache, squares = lax.optimization_barrier((cache, squares))
    left = shift(cache, 1)
    right = shift(cache, -1)
    across = [shift(left[:half_slots], 1), shift(right[half_slots:], -1)]
    squares = jnp.sum(spread(squares, "z", ZN), axis=0).reshape(256)[:rows]
    inverse = lax.rsqrt(squares / width + EPSILON)
    normed = (stream * inverse[None, :, None] * gain).astype(jnp.bfloat16)
    columns = weights[0].shape[1]
    projected = pl.pallas_call(
        project,
        out_shape=jax.ShapeDtypeStruct((rows, columns), jnp.float32),
        in_specs=[smem] + [vmem] * (1 + XN),
        out_specs=vmem,
        scratch_shapes=[pltpu.VMEM((XN, 2 * PART, columns), jnp.bfloat16)],
    )(place, normed, *weights)
    projected = exchange(projected.reshape(ZN, SB, columns), "z")

    small = jax.ShapeDtypeStruct((len(PAIRS), GROUP, HD), jnp.float32)
    queries, everyone, key_chain, value_chain = pl.pallas_call(
        after_projection,
        out_shape=(
            jax.ShapeDtypeStruct((ROWS, HD), jnp.bfloat16),
            jax.ShapeDtypeStruct((ZN, ROWS, HD), jnp.bfloat16),
            small,
            small,
        ),
        in_specs=[smem, vmem, vmem, vmem],
        out_specs=(vmem,) * 4,
        scratch_shapes=[pltpu.VMEM((ROWS, HD), jnp.float32)],
    )(own_parents.reshape(SB), projected, cosines, sines)
    caches = [cache, left, right, None, None]
    caches = caches + [swap(part) for part in caches[:3]]
    last = PAIRS.index((STEPS - 1, 0))
    appended = jnp.stack([key_chain[last:], value_chain[last:]], axis=2)
    appended = appended[:, :, None].astype(jnp.bfloat16)

    everyone = exchange(everyone, "z")
    everyone, across = lax.optimization_barrier((everyone, across))
    caches[3:5] = across
    caches = caches + [swap(part) for part in across]
    partial = pl.pallas_call(
        attention,
        out_shape=jax.ShapeDtypeStruct((ZN, BLOCK, HD), jnp.bfloat16),
        in_specs=[smem, smem, smem, vmem, vmem]
        + [pl.BlockSpec(memory_space=pl.ANY)] * (2 * SEGMENTS),
        out_specs=vmem,
        scratch_shapes=[
            pltpu.VMEM((ZN, ROWS, HD), jnp.float32),
            pltpu.VMEM((ZN, ROWS, HD), jnp.float32),
            pltpu.VMEM((ZN, ROWS, HD), jnp.float32),
            pltpu.VMEM((DEPTH,) + cache.shape[1:], jnp.bfloat16),
            pltpu.SemaphoreType.DMA((DEPTH,)),
            pltpu.SMEM((2 * half_slots * JN,), jnp.int32),
            pltpu.SMEM((2 * half_slots * JN,), jnp.int32),
        ],
    )(place, table, spans.reshape(-1), everyone, root_tiles, *caches)

    partial = exchange(partial, "z")
    attended = pl.pallas_call(
        finish,
        out_shape=jax.ShapeDtypeStruct((ZN, SB, HEADS * HD), jnp.bfloat16),
        in_specs=[vmem] * 4,
        out_specs=vmem,
        scratch_shapes=[pltpu.VMEM((SB, HEADS * HD), jnp.float32)],
    )(partial, queries, key_chain, value_chain)

    attended = exchange(attended, "z").reshape(rows, HEADS * HD)
    result = pl.pallas_call(
        deliver,
        out_shape=jax.ShapeDtypeStruct((KN, XN, QUARTER, 2 * PART), jnp.float32),
        in_specs=[smem] + [vmem] * (1 + XN),
        out_specs=vmem,
        scratch_shapes=[pltpu.VMEM((XN, 2 * PART, HEADS * HD), jnp.bfloat16)],
    )(place, attended, *turned)
    result = exchange(result, "kv")
    result = pl.pallas_call(
        settle,
        out_shape=jax.ShapeDtypeStruct((KN, XN, CN, SB, 2 * PART), jnp.bfloat16),
        in_specs=[smem, vmem, vmem],
        out_specs=vmem,
    )(place, result, stream)
    result = exchange(result.reshape(KN * JN, SB, 2 * PART), ("kv",) + XC)
    result = result.reshape(KN, JN, STEPS, GROUP, 2, PART).transpose(2, 0, 4, 1, 3, 5)
    return (result.reshape(STEPS, beams, PART), appended)


def solution(mesh):
    fine = Mesh(mesh.devices.reshape(-1, ZN, XN, CN), ("kv",) + BLK)
    return jax.shard_map(
        body,
        mesh=fine,
        in_specs=(
            P(None, None, BLK),
            P(BLK),
            P(BLK, "kv"),
            P(BLK, "kv"),
            P(BLK, "kv"),
            P("kv", BLK),
            P(BLK, "kv", None, None, None),
            P(),
            P(),
            P(),
        ),
        out_specs=(P(None, None, BLK), P(None, BLK, "kv", None, None)),
        check_vma=False,
    )
```

```python
import functools
import math

import jax
import jax.numpy as jnp
from jax import lax
from jax.experimental import pallas as pl
from jax.experimental.pallas import tpu as pltpu
from jax.sharding import Mesh
from jax.sharding import PartitionSpec as P

GROUP = 8
NEGATIVE = -1e30
EPSILON = 1e-05
ROPE_BASE = 5000000.0
STEPS = 3
HEADS = 8
HD = 128
SB = STEPS * GROUP
ROWS = HEADS * SB
BLOCK = ROWS + 3 * GROUP
ZN, XN, CN = 8, 4, 2
JN = XN * CN
KN = 4
PART = 64
SLOTS = 32
DEPTH = 12
QUARTER = ZN * SB // KN
PAIRS = [(s, u) for s in range(STEPS) for u in range(s + 1)]
SCALE = 1.0 / math.sqrt(HD)
XC = ("x", "core")
BLK = ("z", "x", "core")


def exchange(value, axis):
    return lax.all_to_all(value, axis, 0, 0, tiled=True)


def spread(value, axis, count):
    return exchange(jnp.broadcast_to(value[None], (count,) + value.shape), axis)


def swap(value):
    return lax.ppermute(value, "core", [(0, 1), (1, 0)])


def shift(value, hop):
    return lax.ppermute(value, "x", [(i, (i + hop) % XN) for i in range(XN)])


def ring(value):
    both = jnp.concatenate([value, swap(value)], axis=0)
    return [both] + [shift(both, hop) for hop in range(1, XN)]


def join(place_ref, chunks, wide):
    core = place_ref[1]
    for hop in range(XN):
        for side, start in ((0, core * PART), (1, (1 - core) * PART)):
            rows = pl.ds(pl.multiple_of(start, PART), PART)
            wide[hop, rows, :] = chunks[hop][side * PART : (side + 1) * PART, :]


def project(place_ref, rows_ref, *rest):
    chunks, out_ref, wide = rest[:XN], rest[XN], rest[XN + 1]
    join(place_ref, chunks, wide)
    x = place_ref[0]
    for start in range(0, out_ref.shape[1], 256):
        out_ref[:, start : start + 256] = sum(
            jnp.dot(
                rows_ref[(x + XN - hop) % XN],
                wide[hop, :, start : start + 256],
                preferred_element_type=jnp.float32,
            )
            for hop in range(XN)
        )


def deliver(place_ref, rows_ref, *rest):
    chunks, out_ref, wide = rest[:XN], rest[XN], rest[XN + 1]
    join(place_ref, chunks, wide)
    x = place_ref[0]
    for hop in range(XN):
        result = lax.dot_general(
            rows_ref[...],
            wide[hop],
            (((1,), (1,)), ((), ())),
            preferred_element_type=jnp.float32,
        )
        for kv in range(KN):
            out_ref[kv, (x + XN - hop) % XN] = result[kv * QUARTER : (kv + 1) * QUARTER]


def settle(place_ref, parts_ref, stream_ref, out_ref):
    kv = place_ref[2]
    lanes = lax.broadcasted_iota(jnp.int32, (SB, 2 * PART), 1)
    for x in range(XN):
        total = parts_ref[0, x]
        for source in range(1, KN):
            total = total + parts_ref[source, x]
        total = stream_ref[x, pl.ds(pl.multiple_of(kv * QUARTER, 8), QUARTER), :] + total
        upper, lower = total[:SB], total[SB:]
        first = jnp.where(lanes < PART, upper, pltpu.roll(lower, PART, 1)).astype(jnp.bfloat16)
        second = jnp.where(lanes < PART, pltpu.roll(upper, PART, 1), lower).astype(jnp.bfloat16)
        for target in range(KN):
            out_ref[target, x, 0] = first
            out_ref[target, x, 1] = second


def after_projection(
    parent_ref, parts_ref, cos_ref, sin_ref, q_ref, all_ref, k_ref, v_ref, hold
):
    total = parts_ref[0]
    for source in range(1, ZN):
        total = total + parts_ref[source]
    cosines = cos_ref[...]
    sines = sin_ref[...]

    def turn(part):
        return part * cosines + pltpu.roll(part, HD // 2, 1) * sines

    for head in range(HEADS):
        hold[head * SB : (head + 1) * SB] = turn(total[:, head * HD : (head + 1) * HD])
    queries = hold[...].astype(jnp.bfloat16)
    q_ref[...] = queries
    for target in range(ZN):
        all_ref[target] = queries
    start = HEADS * HD
    fresh_key = turn(total[:, start : start + HD]).astype(jnp.bfloat16).astype(jnp.float32)
    fresh_value = total[:, start + HD :].astype(jnp.bfloat16).astype(jnp.float32)
    for index, (step, token) in enumerate(PAIRS):
        for ref, fresh in ((k_ref, fresh_key), (v_ref, fresh_value)):
            if token == step:
                ref[index] = fresh[step * GROUP : (step + 1) * GROUP]
            else:
                before = PAIRS.index((step - 1, token))
                for beam in range(GROUP):
                    parent = parent_ref[step * GROUP + beam]
                    ref[index, pl.ds(beam, 1), :] = ref[before, pl.ds(parent, 1), :]


def scan(place_ref, table_ref, length_ref, near_list, far_list, count_ref):
    x, core, z = place_ref[0], place_ref[1], place_ref[3]
    blocks = table_ref.shape[0] // (ZN * GROUP)
    half = SLOTS // 2

    def scan_beam(beam, found):
        used = lax.shift_right_logical(length_ref[beam] + (HD - 1), 7)

        def scan_block(block, found):
            slot = table_ref[beam * blocks + block]
            near, far = found
            hit = lax.shift_right_logical(slot, 8) == z
            hops = jnp.bitwise_and(lax.shift_right_logical(slot, 6) - x, XN - 1)
            opposite = hops == 2
            offset = jnp.bitwise_and(slot, half - 1)
            upper = jnp.bitwise_and(lax.shift_right_logical(slot, 4), 1)
            foreign = jnp.bitwise_xor(jnp.bitwise_and(lax.shift_right_logical(slot, 5), 1), core)
            chip = jnp.where(hops == 0, 0, jnp.where(hops == 3, 1, 2))
            segment = jnp.where(opposite, upper + 2 * foreign, chip * 4 + upper + 2 * foreign)
            code = ((beam * blocks + block) * SLOTS + segment) * SLOTS + offset

            @pl.when(hit & opposite)
            def _():
                far_list[far] = code

            @pl.when(hit & jnp.logical_not(opposite))
            def _():
                near_list[near] = code

            return (
                near + (hit & jnp.logical_not(opposite)).astype(jnp.int32),
                far + (hit & opposite).astype(jnp.int32),
            )

        return lax.fori_loop(0, used, scan_block, found)

    near, far = lax.fori_loop(0, ZN * GROUP, scan_beam, (0, 0))
    count_ref[0] = near
    count_ref[1] = far


def attend(list_ref, found, length_ref, q_ref, root_ref, sources, state, pages, arrived):
    top_ref, sum_ref, hold = state

    def fetch(item):
        code = list_ref[item]
        lane = lax.rem(item, DEPTH)
        offset = jnp.bitwise_and(code, SLOTS - 1)
        segment = jnp.bitwise_and(lax.shift_right_logical(code, 5), SLOTS - 1)
        for index, (ref, base) in enumerate(sources):

            @pl.when(segment == index)
            def _(ref=ref, base=base):
                pltpu.make_async_copy(
                    ref.at[base + offset], pages.at[lane], arrived.at[lane]
                ).start()

    for item in range(DEPTH):

        @pl.when(item < found)
        def _(item=item):
            fetch(item)

    tokens = lax.broadcasted_iota(jnp.int32, (SB, HD), 1)

    def visit(item, carry):
        lane = lax.rem(item, DEPTH)
        place = lax.shift_right_logical(list_ref[item], 10)
        beam = lax.shift_right_logical(place, 6)
        group = lax.shift_right_logical(beam, 3)
        count = length_ref[beam] - jnp.bitwise_and(place, 63) * HD
        live = (root_ref[group] == jnp.bitwise_and(beam, 7)) & (tokens < count)
        live = jnp.concatenate([live] * HEADS, axis=0)
        pltpu.make_async_copy(sources[0][0].at[0], pages.at[lane], arrived.at[lane]).wait()
        scores = (
            lax.dot_general(
                q_ref[group],
                pages[lane, 0],
                (((1,), (1,)), ((), ())),
                preferred_element_type=jnp.float32,
            )
            * SCALE
        )
        scores = jnp.where(live, scores, NEGATIVE)
        old = top_ref[group]
        new = jnp.maximum(old, jnp.max(scores, axis=1, keepdims=True))
        weights = jnp.where(live, jnp.exp(scores - new), 0.0)
        fade = jnp.exp(old - new)
        top_ref[group] = new
        sum_ref[group] = sum_ref[group] * fade + jnp.sum(weights, axis=1, keepdims=True)
        hold[group] = hold[group] * fade + jnp.dot(
            weights.astype(jnp.bfloat16), pages[lane, 1], preferred_element_type=jnp.float32
        )

        @pl.when(item + DEPTH < found)
        def _():
            fetch(item + DEPTH)

        return carry

    lax.fori_loop(0, found, visit, 0)


def attend_near(list_ref, count_ref, length_ref, q_ref, root_ref, *rest):
    wholes = rest[:6]
    top_ref, sum_ref, hold, pages, arrived = rest[6:]
    sources = [(whole, base) for whole in wholes for base in (0, SLOTS // 2)]
    top_ref[...] = jnp.full_like(top_ref, NEGATIVE)
    sum_ref[...] = jnp.zeros_like(sum_ref)
    hold[...] = jnp.zeros_like(hold)
    state = (top_ref, sum_ref, hold)
    attend(
        list_ref, count_ref[0], length_ref, q_ref, root_ref, sources, state, pages, arrived
    )


def attend_far(list_ref, count_ref, length_ref, q_ref, root_ref, *rest):
    parts, before, out_ref, state = rest[:4], rest[4:7], rest[7], rest[8:11]
    pages, arrived = rest[11:]
    for ref, start in zip(state, before):
        ref[...] = start[...]
    sources = [(part, 0) for part in parts]
    attend(
        list_ref, count_ref[1], length_ref, q_ref, root_ref, sources, state, pages, arrived
    )
    top_ref, sum_ref, hold = state
    lanes = lax.broadcasted_iota(jnp.int32, (GROUP, HD), 1)

    def pack(group, carry):
        tile = jnp.zeros((GROUP, HD), jnp.float32)
        for part in range(HEADS * STEPS):
            rows = slice(part * GROUP, (part + 1) * GROUP)
            tile = jnp.where(lanes == part, top_ref[group, rows, :], tile)
            tile = jnp.where(lanes == part + HD // 2, sum_ref[group, rows, :], tile)
        out_ref[group] = seal([hold[group]], tile)
        return carry

    lax.fori_loop(0, ZN, pack, 0)


def seal(sums, stat):
    high = stat.astype(jnp.bfloat16).astype(jnp.float32)
    middle = (stat - high).astype(jnp.bfloat16).astype(jnp.float32)
    low = stat - high - middle
    return jnp.concatenate(sums + [high, middle, low], axis=0).astype(jnp.bfloat16)


def unseal(block):
    block = block.astype(jnp.float32)
    stat = block[ROWS : ROWS + GROUP] + block[ROWS + GROUP : ROWS + 2 * GROUP]
    return block[:ROWS], stat + block[ROWS + 2 * GROUP :]


def finish(parts_ref, q_ref, k_ref, v_ref, out_ref, hold):
    count = parts_ref.shape[0]
    sums, stats = zip(*[unseal(parts_ref[source]) for source in range(count)])
    cached_top = functools.reduce(jnp.maximum, stats)
    queries = q_ref[...].astype(jnp.float32)
    lanes = lax.broadcasted_iota(jnp.int32, (GROUP, HD), 1)
    fresh = {}
    tops = cached_top
    for head in range(HEADS):
        for step in range(STEPS):
            part = head * STEPS + step
            row = head * SB + step * GROUP
            tile = queries[row : row + GROUP]
            for token in range(step + 1):
                key = k_ref[PAIRS.index((step, token))]
                score = jnp.sum(tile * key, axis=1, keepdims=True) * SCALE
                fresh[part, token] = score
                tops = jnp.where(lanes == part, jnp.maximum(tops, score), tops)
    fades = [jnp.exp(stat - tops) for stat in stats]
    total = sum(fade * pltpu.roll(stat, HD // 2, 1) for fade, stat in zip(fades, stats))
    for head in range(HEADS):
        for step in range(STEPS):
            part = head * STEPS + step
            rows = slice(part * GROUP, (part + 1) * GROUP)
            ceiling = tops[:, part : part + 1]
            below = total[:, part : part + 1]
            above = sum(
                fades[source][:, part : part + 1] * sums[source][rows] for source in range(count)
            )
            for token in range(step + 1):
                weight = jnp.exp(fresh[part, token] - ceiling)
                below = below + weight
                above = above + weight.astype(jnp.bfloat16).astype(jnp.float32) * v_ref[
                    PAIRS.index((step, token))
                ]
            hold[step * GROUP : (step + 1) * GROUP, head * HD : (head + 1) * HD] = above / below
    attended = hold[...].astype(jnp.bfloat16)
    for target in range(ZN):
        out_ref[target] = attended


def compose(parents_near):
    digits = jnp.arange(GROUP, dtype=jnp.int32)
    roots = [parents_near[0]]
    for step in range(1, STEPS):
        pick = parents_near[step][:, :, None] == digits
        roots.append(jnp.sum(jnp.where(pick, roots[-1][:, None, :], 0), axis=-1))
    return jnp.stack(roots)


def body(
    embeds, attn_gain, w_query, w_key, w_value, w_out, cache_kv, lengths, block_table, parents
):
    z = lax.axis_index("z")
    x = lax.axis_index("x")
    core = lax.axis_index("core")
    here = (z * XN + x) * CN + core
    groups = ZN * JN
    beams = groups * GROUP
    half_slots = SLOTS // 2
    width = PART * groups

    place = jnp.stack([x, core, lax.axis_index("kv"), z]).astype(jnp.int32)
    vmem = pl.BlockSpec(memory_space=pltpu.VMEM)
    smem = pl.BlockSpec(memory_space=pltpu.SMEM)
    cache = cache_kv[:, 0]

    base = jnp.arange(groups, dtype=jnp.int32)[None, :, None] * GROUP
    parents_near = parents.reshape(STEPS, groups, GROUP) - base
    roots_near = compose(parents_near)
    length_of = lengths.reshape(groups, GROUP)
    own_roots = lax.dynamic_slice_in_dim(roots_near, here, 1, 1)[:, 0]
    own_parents = lax.dynamic_slice_in_dim(parents_near, here, 1, 1)[:, 0]
    own_lengths = lax.dynamic_slice_in_dim(length_of, here, 1, 0)[0]
    digits = jnp.arange(GROUP, dtype=jnp.int32)
    position = jnp.sum(
        jnp.where(own_roots[:, :, None] == digits, own_lengths[None, None, :], 0), axis=-1
    ) + jnp.arange(STEPS, dtype=jnp.int32)[:, None]
    exponent = jnp.arange(HD // 2, dtype=jnp.float32) * (2.0 / HD)
    frequency = ROPE_BASE ** (-exponent)
    angles = position.reshape(SB).astype(jnp.float32)[:, None] * frequency[None, :]
    cosines = jnp.cos(angles)
    sines = jnp.sin(angles)
    cosines = jnp.concatenate([cosines, cosines], axis=1)
    sines = jnp.concatenate([-sines, sines], axis=1)
    lead = x * CN + core
    table = lax.dynamic_index_in_dim(
        block_table.reshape(ZN, JN, GROUP * block_table.shape[1]), lead, 1, keepdims=False
    ).reshape(-1)
    spans = lax.dynamic_index_in_dim(lengths.reshape(ZN, JN, GROUP), lead, 1, keepdims=False)
    spans = spans.reshape(-1)
    listing = jax.ShapeDtypeStruct((SLOTS * JN,), jnp.int32)
    near_list, far_list, counts = pl.pallas_call(
        scan,
        out_shape=(listing, listing, jax.ShapeDtypeStruct((2,), jnp.int32)),
        in_specs=[smem] * 3,
        out_specs=(smem,) * 3,
    )(place, table, spans)
    root_tiles = lax.dynamic_index_in_dim(
        roots_near.reshape(STEPS, ZN, JN, GROUP), lead, 2, keepdims=False
    )
    root_tiles = root_tiles.transpose(1, 0, 2).reshape(ZN, SB)
    root_tiles = jnp.broadcast_to(root_tiles[:, :, None], (ZN, SB, HD))

    rows = ZN * SB
    half = rows // 2
    by_row = embeds.reshape(STEPS, ZN // 2, 2, JN, GROUP, PART).transpose(3, 1, 0, 4, 2, 5)
    by_row = by_row.reshape(JN, half, 2 * PART)
    high = lax.reduce_precision(attn_gain, 8, 7)
    middle = lax.reduce_precision(attn_gain - high, 8, 7)
    low = attn_gain - high - middle
    gain_rows = jnp.stack(
        [jnp.concatenate([high, middle]), jnp.concatenate([low, jnp.zeros_like(low)])]
    ).astype(jnp.bfloat16)
    gain_rows = jnp.concatenate([gain_rows, jnp.zeros((6, HD), jnp.bfloat16)])
    packed = jnp.concatenate([by_row, jnp.broadcast_to(gain_rows[None], (JN, 8, HD))], axis=1)
    packed, w_query, w_key, w_value = lax.optimization_barrier((packed, w_query, w_key, w_value))
    weights = ring(jnp.concatenate([w_query, w_key, w_value], axis=1))
    packed = exchange(packed, XC)
    stream = packed[:, :half].reshape(XN, CN, ZN // 2, SB, 2, PART).transpose(0, 2, 4, 3, 1, 5)
    stream = stream.reshape(XN, rows, 2 * PART).astype(jnp.float32)
    tails = packed[:, half : half + 2].astype(jnp.float32)
    gain = tails[:, 0, :PART] + tails[:, 0, PART:] + tails[:, 1, :PART]
    gain = gain.reshape(XN, 1, 2 * PART)
    squares = jnp.sum(stream * stream, axis=(0, 2))
    squares = jnp.pad(squares, (0, 256 - rows)).reshape(2, 128)
    cache, squares = lax.optimization_barrier((cache, squares))
    left = shift(cache, 1)
    right = shift(cache, -1)
    across = [shift(left[:half_slots], 1), shift(right[half_slots:], -1)]
    squares = jnp.sum(spread(squares, "z", ZN), axis=0).reshape(256)[:rows]
    inverse = lax.rsqrt(squares / width + EPSILON)
    normed = (stream * inverse[None, :, None] * gain).astype(jnp.bfloat16)
    columns = weights[0].shape[1]
    projected = pl.pallas_call(
        project,
        out_shape=jax.ShapeDtypeStruct((rows, columns), jnp.float32),
        in_specs=[smem] + [vmem] * (1 + XN),
        out_specs=vmem,
        scratch_shapes=[pltpu.VMEM((XN, 2 * PART, columns), jnp.bfloat16)],
    )(place, normed, *weights)
    projected = exchange(projected.reshape(ZN, SB, columns), "z")

    small = jax.ShapeDtypeStruct((len(PAIRS), GROUP, HD), jnp.float32)
    queries, everyone, key_chain, value_chain = pl.pallas_call(
        after_projection,
        out_shape=(
            jax.ShapeDtypeStruct((ROWS, HD), jnp.bfloat16),
            jax.ShapeDtypeStruct((ZN, ROWS, HD), jnp.bfloat16),
            small,
            small,
        ),
        in_specs=[smem, vmem, vmem, vmem],
        out_specs=(vmem,) * 4,
        scratch_shapes=[pltpu.VMEM((ROWS, HD), jnp.float32)],
    )(own_parents.reshape(SB), projected, cosines, sines)
    queries, cache, left, right = lax.optimization_barrier((queries, cache, left, right))
    near = [part for whole in (cache, left, right) for part in (whole, swap(whole))]
    last = PAIRS.index((STEPS - 1, 0))
    appended = jnp.stack([key_chain[last:], value_chain[last:]], axis=2)
    appended = appended[:, :, None].astype(jnp.bfloat16)

    everyone = exchange(everyone, "z")
    everyone, turned = lax.optimization_barrier((everyone, w_out.T))
    turned = ring(turned)
    state = (jax.ShapeDtypeStruct((ZN, ROWS, HD), jnp.float32),) * 3
    ring_buffers = [
        pltpu.VMEM((DEPTH,) + cache.shape[1:], jnp.bfloat16),
        pltpu.SemaphoreType.DMA((DEPTH,)),
    ]
    anywhere = pl.BlockSpec(memory_space=pl.ANY)
    before = pl.pallas_call(
        attend_near,
        out_shape=state,
        in_specs=[smem, smem, smem, vmem, vmem] + [anywhere] * 6,
        out_specs=(vmem,) * 3,
        scratch_shapes=ring_buffers,
        cost_estimate=pl.CostEstimate(flops=1, bytes_accessed=1, transcendentals=0),
    )(near_list, counts, spans, everyone, root_tiles, *near)
    across, before = lax.optimization_barrier((across, before))
    across = across + [swap(part) for part in across]
    partial = pl.pallas_call(
        attend_far,
        out_shape=jax.ShapeDtypeStruct((ZN, BLOCK, HD), jnp.bfloat16),
        in_specs=[smem, smem, smem, vmem, vmem] + [anywhere] * 4 + [vmem] * 3,
        out_specs=vmem,
        scratch_shapes=[pltpu.VMEM(part.shape, part.dtype) for part in state] + ring_buffers,
    )(far_list, counts, spans, everyone, root_tiles, *across, *before)

    partial = exchange(partial, "z")
    partial, turned = lax.optimization_barrier((partial, turned))
    attended = pl.pallas_call(
        finish,
        out_shape=jax.ShapeDtypeStruct((ZN, SB, HEADS * HD), jnp.bfloat16),
        in_specs=[vmem] * 4,
        out_specs=vmem,
        scratch_shapes=[pltpu.VMEM((SB, HEADS * HD), jnp.float32)],
    )(partial, queries, key_chain, value_chain)

    attended = exchange(attended, "z").reshape(rows, HEADS * HD)
    result = pl.pallas_call(
        deliver,
        out_shape=jax.ShapeDtypeStruct((KN, XN, QUARTER, 2 * PART), jnp.float32),
        in_specs=[smem] + [vmem] * (1 + XN),
        out_specs=vmem,
        scratch_shapes=[pltpu.VMEM((XN, 2 * PART, HEADS * HD), jnp.bfloat16)],
    )(place, attended, *turned)
    result = exchange(result, "kv")
    result = pl.pallas_call(
        settle,
        out_shape=jax.ShapeDtypeStruct((KN, XN, CN, SB, 2 * PART), jnp.bfloat16),
        in_specs=[smem, vmem, vmem],
        out_specs=vmem,
    )(place, result, stream)
    result = exchange(result.reshape(KN * JN, SB, 2 * PART), ("kv",) + XC)
    result = result.reshape(KN, JN, STEPS, GROUP, 2, PART).transpose(2, 0, 4, 1, 3, 5)
    return (result.reshape(STEPS, beams, PART), appended)


def solution(mesh):
    fine = Mesh(mesh.devices.reshape(-1, ZN, XN, CN), ("kv",) + BLK)
    return jax.shard_map(
        body,
        mesh=fine,
        in_specs=(
            P(None, None, BLK),
            P(BLK),
            P(BLK, "kv"),
            P(BLK, "kv"),
            P(BLK, "kv"),
            P("kv", BLK),
            P(BLK, "kv", None, None, None),
            P(),
            P(),
            P(),
        ),
        out_specs=(P(None, None, BLK), P(None, BLK, "kv", None, None)),
        check_vma=False,
    )
```

```python
import functools
import math

import jax
import jax.numpy as jnp
from jax import lax
from jax.experimental import pallas as pl
from jax.experimental.pallas import tpu as pltpu
from jax.sharding import Mesh
from jax.sharding import PartitionSpec as P

GROUP = 8
NEGATIVE = -1e30
EPSILON = 1e-05
ROPE_BASE = 5000000.0
STEPS = 3
HEADS = 8
HD = 128
SB = STEPS * GROUP
ROWS = HEADS * SB
BLOCK = ROWS + 3 * GROUP
ZN, XN, CN = 8, 4, 2
JN = XN * CN
KN = 4
PART = 64
SLOTS = 32
DEPTH = 12
QUARTER = ZN * SB // KN
SMALL = pltpu.CompilerParams(vmem_limit_bytes=16 << 20)
PAIRS = [(s, u) for s in range(STEPS) for u in range(s + 1)]
SCALE = 1.0 / math.sqrt(HD)
XC = ("x", "core")
BLK = ("z", "x", "core")


def exchange(value, axis):
    return lax.all_to_all(value, axis, 0, 0, tiled=True)


def spread(value, axis, count):
    return exchange(jnp.broadcast_to(value[None], (count,) + value.shape), axis)


def swap(value):
    return lax.ppermute(value, "core", [(0, 1), (1, 0)])


def shift(value, hop):
    return lax.ppermute(value, "x", [(i, (i + hop) % XN) for i in range(XN)])


def ring(value):
    return [value] + [shift(value, hop) for hop in range(1, XN)]


def join(place_ref, chunks, wide):
    core = place_ref[1]
    for hop in range(XN):
        wide[hop, pl.ds(pl.multiple_of(core * PART, PART), PART), :] = chunks[hop][...]
        wide[hop, pl.ds(pl.multiple_of((1 - core) * PART, PART), PART), :] = chunks[XN + hop][...]


def project(place_ref, rows_ref, *rest):
    chunks, out_ref, wide = rest[: 2 * XN], rest[2 * XN], rest[2 * XN + 1]
    join(place_ref, chunks, wide)
    x = place_ref[0]
    for start in range(0, out_ref.shape[1], 256):
        out_ref[:, start : start + 256] = sum(
            jnp.dot(
                rows_ref[(x + XN - hop) % XN],
                wide[hop, :, start : start + 256],
                preferred_element_type=jnp.float32,
            )
            for hop in range(XN)
        )


def deliver(place_ref, rows_ref, *rest):
    chunks, outs, wide = rest[: 2 * XN], rest[2 * XN : 2 * XN + KN], rest[2 * XN + KN]
    hold = rest[2 * XN + KN + 1]
    join(place_ref, chunks, wide)
    x, kv = place_ref[0], place_ref[2]
    for hop in range(XN):
        hold[...] = lax.dot_general(
            rows_ref[...],
            wide[hop],
            (((1,), (1,)), ((), ())),
            preferred_element_type=jnp.float32,
        )
        for far in range(KN):
            start = pl.multiple_of(lax.rem(kv + far, KN) * QUARTER, 8)
            outs[far][lax.rem(x + XN - hop, XN)] = hold[pl.ds(start, QUARTER), :]


def settle(place_ref, *rest):
    parts, stream_ref, out_ref = rest[:KN], rest[KN], rest[KN + 1]
    kv = place_ref[2]
    lanes = lax.broadcasted_iota(jnp.int32, (SB, 2 * PART), 1)
    for x in range(XN):
        total = parts[0][x]
        for part in parts[1:]:
            total = total + part[x]
        total = stream_ref[x, pl.ds(pl.multiple_of(kv * QUARTER, 8), QUARTER), :] + total
        upper, lower = total[:SB], total[SB:]
        first = jnp.where(lanes < PART, upper, pltpu.roll(lower, PART, 1)).astype(jnp.bfloat16)
        second = jnp.where(lanes < PART, pltpu.roll(upper, PART, 1), lower).astype(jnp.bfloat16)
        for target in range(KN):
            out_ref[target, x, 0] = first
            out_ref[target, x, 1] = second


def after_projection(
    parent_ref, parts_ref, cos_ref, sin_ref, q_ref, all_ref, k_ref, v_ref, hold
):
    total = parts_ref[0]
    for source in range(1, ZN):
        total = total + parts_ref[source]
    cosines = cos_ref[...]
    sines = sin_ref[...]

    def turn(part):
        return part * cosines + pltpu.roll(part, HD // 2, 1) * sines

    for head in range(HEADS):
        hold[head * SB : (head + 1) * SB] = turn(total[:, head * HD : (head + 1) * HD])
    queries = hold[...].astype(jnp.bfloat16)
    q_ref[...] = queries
    for target in range(ZN):
        all_ref[target] = queries
    start = HEADS * HD
    fresh_key = turn(total[:, start : start + HD]).astype(jnp.bfloat16).astype(jnp.float32)
    fresh_value = total[:, start + HD :].astype(jnp.bfloat16).astype(jnp.float32)
    for index, (step, token) in enumerate(PAIRS):
        for ref, fresh in ((k_ref, fresh_key), (v_ref, fresh_value)):
            if token == step:
                ref[index] = fresh[step * GROUP : (step + 1) * GROUP]
            else:
                before = PAIRS.index((step - 1, token))
                for beam in range(GROUP):
                    parent = parent_ref[step * GROUP + beam]
                    ref[index, pl.ds(beam, 1), :] = ref[before, pl.ds(parent, 1), :]


def scan(place_ref, table_ref, length_ref, near_list, far_list, count_ref):
    x, core, z = place_ref[0], place_ref[1], place_ref[3]
    blocks = table_ref.shape[0] // (ZN * GROUP)
    half = SLOTS // 2

    def scan_beam(beam, found):
        used = lax.shift_right_logical(length_ref[beam] + (HD - 1), 7)

        def scan_block(block, found):
            slot = table_ref[beam * blocks + block]
            near, far = found
            hit = lax.shift_right_logical(slot, 8) == z
            hops = jnp.bitwise_and(lax.shift_right_logical(slot, 6) - x, XN - 1)
            opposite = hops == 2
            offset = jnp.bitwise_and(slot, half - 1)
            upper = jnp.bitwise_and(lax.shift_right_logical(slot, 4), 1)
            foreign = jnp.bitwise_xor(jnp.bitwise_and(lax.shift_right_logical(slot, 5), 1), core)
            chip = jnp.where(hops == 0, 0, jnp.where(hops == 3, 1, 2))
            segment = jnp.where(opposite, upper + 2 * foreign, chip * 4 + upper + 2 * foreign)
            code = ((beam * blocks + block) * SLOTS + segment) * SLOTS + offset

            @pl.when(hit & opposite)
            def _():
                far_list[far] = code

            @pl.when(hit & jnp.logical_not(opposite))
            def _():
                near_list[near] = code

            return (
                near + (hit & jnp.logical_not(opposite)).astype(jnp.int32),
                far + (hit & opposite).astype(jnp.int32),
            )

        return lax.fori_loop(0, used, scan_block, found)

    near, far = lax.fori_loop(0, ZN * GROUP, scan_beam, (0, 0))
    count_ref[0] = near
    count_ref[1] = far


def attend(list_ref, found, length_ref, q_ref, root_ref, sources, state, pages, arrived):
    top_ref, sum_ref, hold = state

    def fetch(item):
        code = list_ref[item]
        lane = lax.rem(item, DEPTH)
        offset = jnp.bitwise_and(code, SLOTS - 1)
        segment = jnp.bitwise_and(lax.shift_right_logical(code, 5), SLOTS - 1)
        for index, (ref, base) in enumerate(sources):

            @pl.when(segment == index)
            def _(ref=ref, base=base):
                pltpu.make_async_copy(
                    ref.at[base + offset], pages.at[lane], arrived.at[lane]
                ).start()

    for item in range(DEPTH):

        @pl.when(item < found)
        def _(item=item):
            fetch(item)

    tokens = lax.broadcasted_iota(jnp.int32, (SB, HD), 1)

    def visit(item, carry):
        lane = lax.rem(item, DEPTH)
        place = lax.shift_right_logical(list_ref[item], 10)
        beam = lax.shift_right_logical(place, 6)
        group = lax.shift_right_logical(beam, 3)
        count = length_ref[beam] - jnp.bitwise_and(place, 63) * HD
        live = (root_ref[group] == jnp.bitwise_and(beam, 7)) & (tokens < count)
        live = jnp.concatenate([live] * HEADS, axis=0)
        pltpu.make_async_copy(sources[0][0].at[0], pages.at[lane], arrived.at[lane]).wait()
        scores = (
            lax.dot_general(
                q_ref[group],
                pages[lane, 0],
                (((1,), (1,)), ((), ())),
                preferred_element_type=jnp.float32,
            )
            * SCALE
        )
        scores = jnp.where(live, scores, NEGATIVE)
        old = top_ref[group]
        new = jnp.maximum(old, jnp.max(scores, axis=1, keepdims=True))
        weights = jnp.where(live, jnp.exp(scores - new), 0.0)
        fade = jnp.exp(old - new)
        top_ref[group] = new
        sum_ref[group] = sum_ref[group] * fade + jnp.sum(weights, axis=1, keepdims=True)
        hold[group] = hold[group] * fade + jnp.dot(
            weights.astype(jnp.bfloat16), pages[lane, 1], preferred_element_type=jnp.float32
        )

        @pl.when(item + DEPTH < found)
        def _():
            fetch(item + DEPTH)

        return carry

    lax.fori_loop(0, found, visit, 0)


def attend_near(list_ref, count_ref, length_ref, q_ref, root_ref, *rest):
    wholes = rest[:6]
    top_ref, sum_ref, hold, pages, arrived = rest[6:]
    sources = [(whole, base) for whole in wholes for base in (0, SLOTS // 2)]
    top_ref[...] = jnp.full_like(top_ref, NEGATIVE)
    sum_ref[...] = jnp.zeros_like(sum_ref)
    hold[...] = jnp.zeros_like(hold)
    state = (top_ref, sum_ref, hold)
    attend(
        list_ref, count_ref[0], length_ref, q_ref, root_ref, sources, state, pages, arrived
    )


def attend_far(list_ref, count_ref, length_ref, q_ref, root_ref, *rest):
    parts, before, out_ref, state = rest[:4], rest[4:7], rest[7], rest[8:11]
    pages, arrived = rest[11:]
    for ref, start in zip(state, before):
        ref[...] = start[...]
    sources = [(part, 0) for part in parts]
    attend(
        list_ref, count_ref[1], length_ref, q_ref, root_ref, sources, state, pages, arrived
    )
    top_ref, sum_ref, hold = state
    lanes = lax.broadcasted_iota(jnp.int32, (GROUP, HD), 1)

    def pack(group, carry):
        tile = jnp.zeros((GROUP, HD), jnp.float32)
        for part in range(HEADS * STEPS):
            rows = slice(part * GROUP, (part + 1) * GROUP)
            tile = jnp.where(lanes == part, top_ref[group, rows, :], tile)
            tile = jnp.where(lanes == part + HD // 2, sum_ref[group, rows, :], tile)
        out_ref[group] = seal([hold[group]], tile)
        return carry

    lax.fori_loop(0, ZN, pack, 0)


def seal(sums, stat):
    high = stat.astype(jnp.bfloat16).astype(jnp.float32)
    middle = (stat - high).astype(jnp.bfloat16).astype(jnp.float32)
    low = stat - high - middle
    return jnp.concatenate(sums + [high, middle, low], axis=0).astype(jnp.bfloat16)


def unseal(block):
    block = block.astype(jnp.float32)
    stat = block[ROWS : ROWS + GROUP] + block[ROWS + GROUP : ROWS + 2 * GROUP]
    return block[:ROWS], stat + block[ROWS + 2 * GROUP :]


def finish(parts_ref, q_ref, k_ref, v_ref, out_ref, hold):
    count = parts_ref.shape[0]
    sums, stats = zip(*[unseal(parts_ref[source]) for source in range(count)])
    cached_top = functools.reduce(jnp.maximum, stats)
    queries = q_ref[...].astype(jnp.float32)
    lanes = lax.broadcasted_iota(jnp.int32, (GROUP, HD), 1)
    fresh = {}
    tops = cached_top
    for head in range(HEADS):
        for step in range(STEPS):
            part = head * STEPS + step
            row = head * SB + step * GROUP
            tile = queries[row : row + GROUP]
            for token in range(step + 1):
                key = k_ref[PAIRS.index((step, token))]
                score = jnp.sum(tile * key, axis=1, keepdims=True) * SCALE
                fresh[part, token] = score
                tops = jnp.where(lanes == part, jnp.maximum(tops, score), tops)
    fades = [jnp.exp(stat - tops) for stat in stats]
    total = sum(fade * pltpu.roll(stat, HD // 2, 1) for fade, stat in zip(fades, stats))
    for head in range(HEADS):
        for step in range(STEPS):
            part = head * STEPS + step
            rows = slice(part * GROUP, (part + 1) * GROUP)
            ceiling = tops[:, part : part + 1]
            below = total[:, part : part + 1]
            above = sum(
                fades[source][:, part : part + 1] * sums[source][rows] for source in range(count)
            )
            for token in range(step + 1):
                weight = jnp.exp(fresh[part, token] - ceiling)
                below = below + weight
                above = above + weight.astype(jnp.bfloat16).astype(jnp.float32) * v_ref[
                    PAIRS.index((step, token))
                ]
            hold[step * GROUP : (step + 1) * GROUP, head * HD : (head + 1) * HD] = above / below
    attended = hold[...].astype(jnp.bfloat16)
    for target in range(ZN):
        out_ref[target] = attended


def compose(parents_near):
    digits = jnp.arange(GROUP, dtype=jnp.int32)
    roots = [parents_near[0]]
    for step in range(1, STEPS):
        pick = parents_near[step][:, :, None] == digits
        roots.append(jnp.sum(jnp.where(pick, roots[-1][:, None, :], 0), axis=-1))
    return jnp.stack(roots)


def body(
    embeds, attn_gain, w_query, w_key, w_value, w_out, cache_kv, lengths, block_table, parents
):
    z = lax.axis_index("z")
    x = lax.axis_index("x")
    core = lax.axis_index("core")
    here = (z * XN + x) * CN + core
    groups = ZN * JN
    beams = groups * GROUP
    half_slots = SLOTS // 2
    width = PART * groups

    place = jnp.stack([x, core, lax.axis_index("kv"), z]).astype(jnp.int32)
    vmem = pl.BlockSpec(memory_space=pltpu.VMEM)
    smem = pl.BlockSpec(memory_space=pltpu.SMEM)
    cache = cache_kv[:, 0]

    base = jnp.arange(groups, dtype=jnp.int32)[None, :, None] * GROUP
    parents_near = parents.reshape(STEPS, groups, GROUP) - base
    roots_near = compose(parents_near)
    length_of = lengths.reshape(groups, GROUP)
    own_roots = lax.dynamic_slice_in_dim(roots_near, here, 1, 1)[:, 0]
    own_parents = lax.dynamic_slice_in_dim(parents_near, here, 1, 1)[:, 0]
    own_lengths = lax.dynamic_slice_in_dim(length_of, here, 1, 0)[0]
    digits = jnp.arange(GROUP, dtype=jnp.int32)
    position = jnp.sum(
        jnp.where(own_roots[:, :, None] == digits, own_lengths[None, None, :], 0), axis=-1
    ) + jnp.arange(STEPS, dtype=jnp.int32)[:, None]
    exponent = jnp.arange(HD // 2, dtype=jnp.float32) * (2.0 / HD)
    frequency = ROPE_BASE ** (-exponent)
    angles = position.reshape(SB).astype(jnp.float32)[:, None] * frequency[None, :]
    cosines = jnp.cos(angles)
    sines = jnp.sin(angles)
    cosines = jnp.concatenate([cosines, cosines], axis=1)
    sines = jnp.concatenate([-sines, sines], axis=1)
    lead = x * CN + core
    table = lax.dynamic_index_in_dim(
        block_table.reshape(ZN, JN, GROUP * block_table.shape[1]), lead, 1, keepdims=False
    ).reshape(-1)
    spans = lax.dynamic_index_in_dim(lengths.reshape(ZN, JN, GROUP), lead, 1, keepdims=False)
    spans = spans.reshape(-1)
    listing = jax.ShapeDtypeStruct((SLOTS * JN,), jnp.int32)
    near_list, far_list, counts = pl.pallas_call(
        scan,
        compiler_params=SMALL,
        out_shape=(listing, listing, jax.ShapeDtypeStruct((2,), jnp.int32)),
        in_specs=[smem] * 3,
        out_specs=(smem,) * 3,
    )(place, table, spans)
    root_tiles = lax.dynamic_index_in_dim(
        roots_near.reshape(STEPS, ZN, JN, GROUP), lead, 2, keepdims=False
    )
    root_tiles = root_tiles.transpose(1, 0, 2).reshape(ZN, SB)

    rows = ZN * SB
    half = rows // 2
    by_row = embeds.reshape(STEPS, ZN // 2, 2, JN, GROUP, PART).transpose(3, 1, 0, 4, 2, 5)
    by_row = by_row.reshape(JN, half, 2 * PART)
    high = lax.reduce_precision(attn_gain, 8, 7)
    middle = lax.reduce_precision(attn_gain - high, 8, 7)
    low = attn_gain - high - middle
    gain_rows = jnp.stack(
        [jnp.concatenate([high, middle]), jnp.concatenate([low, jnp.zeros_like(low)])]
    ).astype(jnp.bfloat16)
    gain_rows = jnp.concatenate([gain_rows, jnp.zeros((6, HD), jnp.bfloat16)])
    packed = jnp.concatenate([by_row, jnp.broadcast_to(gain_rows[None], (JN, 8, HD))], axis=1)
    weights = jnp.concatenate([w_query, w_key, w_value], axis=1)
    cache, weights = lax.optimization_barrier((cache, weights))
    weights = ring(weights)
    left = shift(cache, 1)
    right = shift(cache, -1)
    across = [shift(left[:half_slots], 1), shift(right[half_slots:], -1)]
    packed = exchange(packed, XC)
    packed, weights = lax.optimization_barrier((packed, weights))
    weights = weights + [swap(part) for part in weights]
    stream = packed[:, :half].reshape(XN, CN, ZN // 2, SB, 2, PART).transpose(0, 2, 4, 3, 1, 5)
    stream = stream.reshape(XN, rows, 2 * PART).astype(jnp.float32)
    tails = packed[:, half : half + 2].astype(jnp.float32)
    gain = tails[:, 0, :PART] + tails[:, 0, PART:] + tails[:, 1, :PART]
    gain = gain.reshape(XN, 1, 2 * PART)
    squares = jnp.sum(stream * stream, axis=(0, 2))
    squares = jnp.pad(squares, (0, 256 - rows)).reshape(2, 128)
    squares = jnp.sum(spread(squares, "z", ZN), axis=0).reshape(256)[:rows]
    inverse = lax.rsqrt(squares / width + EPSILON)
    normed = (stream * inverse[None, :, None] * gain).astype(jnp.bfloat16)
    columns = weights[0].shape[1]
    projected = pl.pallas_call(
        project,
        compiler_params=SMALL,
        out_shape=jax.ShapeDtypeStruct((rows, columns), jnp.float32),
        in_specs=[smem] + [vmem] * (1 + 2 * XN),
        out_specs=vmem,
        scratch_shapes=[pltpu.VMEM((XN, 2 * PART, columns), jnp.bfloat16)],
    )(place, normed, *weights)
    projected = exchange(projected.reshape(ZN, SB, columns), "z")
    projected, near_list = lax.optimization_barrier((projected, near_list))

    small = jax.ShapeDtypeStruct((len(PAIRS), GROUP, HD), jnp.float32)
    queries, everyone, key_chain, value_chain = pl.pallas_call(
        after_projection,
        compiler_params=SMALL,
        out_shape=(
            jax.ShapeDtypeStruct((ROWS, HD), jnp.bfloat16),
            jax.ShapeDtypeStruct((ZN, ROWS, HD), jnp.bfloat16),
            small,
            small,
        ),
        in_specs=[smem, vmem, vmem, vmem],
        out_specs=(vmem,) * 4,
        scratch_shapes=[pltpu.VMEM((ROWS, HD), jnp.float32)],
    )(own_parents.reshape(SB), projected, cosines, sines)
    root_tiles = jnp.broadcast_to(root_tiles[:, :, None], (ZN, SB, HD))
    near = [part for whole in (cache, left, right) for part in (whole, swap(whole))]
    last = PAIRS.index((STEPS - 1, 0))
    appended = jnp.stack([key_chain[last:], value_chain[last:]], axis=2)
    appended = appended[:, :, None].astype(jnp.bfloat16)

    everyone = exchange(everyone, "z")
    everyone, turned, across = lax.optimization_barrier((everyone, w_out.T, across))
    across = across + [swap(part) for part in across]
    turned = ring(turned)
    turned = turned + [swap(part) for part in turned]
    state = (jax.ShapeDtypeStruct((ZN, ROWS, HD), jnp.float32),) * 3
    ring_buffers = [
        pltpu.VMEM((DEPTH,) + cache.shape[1:], jnp.bfloat16),
        pltpu.SemaphoreType.DMA((DEPTH,)),
    ]
    anywhere = pl.BlockSpec(memory_space=pl.ANY)
    before = pl.pallas_call(
        attend_near,
        compiler_params=SMALL,
        out_shape=state,
        in_specs=[smem, smem, smem, vmem, vmem] + [anywhere] * 6,
        out_specs=(vmem,) * 3,
        scratch_shapes=ring_buffers,
        cost_estimate=pl.CostEstimate(flops=1, bytes_accessed=1, transcendentals=0),
    )(near_list, counts, spans, everyone, root_tiles, *near)
    partial = pl.pallas_call(
        attend_far,
        compiler_params=SMALL,
        out_shape=jax.ShapeDtypeStruct((ZN, BLOCK, HD), jnp.bfloat16),
        in_specs=[smem, smem, smem, vmem, vmem] + [anywhere] * 4 + [vmem] * 3,
        out_specs=vmem,
        scratch_shapes=[pltpu.VMEM(part.shape, part.dtype) for part in state] + ring_buffers,
    )(far_list, counts, spans, everyone, root_tiles, *across, *before)

    partial = exchange(partial, "z")
    partial, turned = lax.optimization_barrier((partial, turned))
    attended = pl.pallas_call(
        finish,
        compiler_params=SMALL,
        out_shape=jax.ShapeDtypeStruct((ZN, SB, HEADS * HD), jnp.bfloat16),
        in_specs=[vmem] * 4,
        out_specs=vmem,
        scratch_shapes=[pltpu.VMEM((SB, HEADS * HD), jnp.float32)],
    )(partial, queries, key_chain, value_chain)

    attended = exchange(attended, "z").reshape(rows, HEADS * HD)
    share = jax.ShapeDtypeStruct((XN, QUARTER, 2 * PART), jnp.float32)
    shares = pl.pallas_call(
        deliver,
        compiler_params=SMALL,
        out_shape=(share,) * KN,
        in_specs=[smem] + [vmem] * (1 + 2 * XN),
        out_specs=(vmem,) * KN,
        scratch_shapes=[
            pltpu.VMEM((XN, 2 * PART, HEADS * HD), jnp.bfloat16),
            pltpu.VMEM((rows, 2 * PART), jnp.float32),
        ],
    )(place, attended, *turned)
    shares = [shares[0]] + [
        lax.ppermute(shares[far], "kv", [(i, (i + far) % KN) for i in range(KN)])
        for far in range(1, KN)
    ]
    result = pl.pallas_call(
        settle,
        compiler_params=SMALL,
        out_shape=jax.ShapeDtypeStruct((KN, XN, CN, SB, 2 * PART), jnp.bfloat16),
        in_specs=[smem] + [vmem] * (KN + 1),
        out_specs=vmem,
    )(place, *shares, stream)
    result = exchange(result.reshape(KN * JN, SB, 2 * PART), ("kv",) + XC)
    result = result.reshape(KN, JN, STEPS, GROUP, 2, PART).transpose(2, 0, 4, 1, 3, 5)
    return (result.reshape(STEPS, beams, PART), appended)


def solution(mesh):
    fine = Mesh(mesh.devices.reshape(-1, ZN, XN, CN), ("kv",) + BLK)
    return jax.shard_map(
        body,
        mesh=fine,
        in_specs=(
            P(None, None, BLK),
            P(BLK),
            P(BLK, "kv"),
            P(BLK, "kv"),
            P(BLK, "kv"),
            P("kv", BLK),
            P(BLK, "kv", None, None, None),
            P(),
            P(),
            P(),
        ),
        out_specs=(P(None, None, BLK), P(None, BLK, "kv", None, None)),
        check_vma=False,
    )
```

```python
import functools
import math

import jax
import jax.numpy as jnp
from jax import lax
from jax.experimental import pallas as pl
from jax.experimental.pallas import tpu as pltpu
from jax.sharding import Mesh
from jax.sharding import PartitionSpec as P

GROUP = 8
NEGATIVE = -1e30
EPSILON = 1e-05
ROPE_BASE = 5000000.0
STEPS = 3
HEADS = 8
HD = 128
SB = STEPS * GROUP
ROWS = HEADS * SB
BLOCK = ROWS + 3 * GROUP
ZN, XN, CN = 8, 4, 2
JN = XN * CN
KN = 4
PART = 64
SLOTS = 32
DEPTH = 12
QUARTER = ZN * SB // KN
SMALL = pltpu.CompilerParams(vmem_limit_bytes=16 << 20)
PAIRS = [(s, u) for s in range(STEPS) for u in range(s + 1)]
SCALE = 1.0 / math.sqrt(HD)
XC = ("x", "core")
BLK = ("z", "x", "core")


def exchange(value, axis):
    return lax.all_to_all(value, axis, 0, 0, tiled=True)


def spread(value, axis, count):
    return exchange(jnp.broadcast_to(value[None], (count,) + value.shape), axis)


def swap(value):
    return lax.ppermute(value, "core", [(0, 1), (1, 0)])


def shift(value, hop):
    return lax.ppermute(value, "x", [(i, (i + hop) % XN) for i in range(XN)])


def ring(value):
    return [value] + [shift(value, hop) for hop in range(1, XN)]


def join(place_ref, chunks, wide):
    core = place_ref[1]
    for hop in range(XN):
        wide[hop, pl.ds(pl.multiple_of(core * PART, PART), PART), :] = chunks[hop][...]
        wide[hop, pl.ds(pl.multiple_of((1 - core) * PART, PART), PART), :] = chunks[XN + hop][...]


def project(place_ref, rows_ref, *rest):
    chunks, out_ref, wide = rest[: 2 * XN], rest[2 * XN], rest[2 * XN + 1]
    join(place_ref, chunks, wide)
    x = place_ref[0]
    for start in range(0, out_ref.shape[1], 256):
        out_ref[:, start : start + 256] = sum(
            jnp.dot(
                rows_ref[(x + XN - hop) % XN],
                wide[hop, :, start : start + 256],
                preferred_element_type=jnp.float32,
            )
            for hop in range(XN)
        )


def deliver(place_ref, rows_ref, *rest):
    chunks, outs, wide = rest[: 2 * XN], rest[2 * XN : 2 * XN + KN], rest[2 * XN + KN]
    hold = rest[2 * XN + KN + 1]
    join(place_ref, chunks, wide)
    x, kv = place_ref[0], place_ref[2]
    for hop in range(XN):
        hold[...] = lax.dot_general(
            rows_ref[...],
            wide[hop],
            (((1,), (1,)), ((), ())),
            preferred_element_type=jnp.float32,
        )
        for far in range(KN):
            start = pl.multiple_of(lax.rem(kv + far, KN) * QUARTER, 8)
            outs[far][lax.rem(x + XN - hop, XN)] = hold[pl.ds(start, QUARTER), :]


def settle(place_ref, *rest):
    parts, stream_ref, out_ref = rest[:KN], rest[KN], rest[KN + 1]
    kv = place_ref[2]
    lanes = lax.broadcasted_iota(jnp.int32, (SB, 2 * PART), 1)
    for x in range(XN):
        total = parts[0][x]
        for part in parts[1:]:
            total = total + part[x]
        total = stream_ref[x, pl.ds(pl.multiple_of(kv * QUARTER, 8), QUARTER), :] + total
        upper, lower = total[:SB], total[SB:]
        first = jnp.where(lanes < PART, upper, pltpu.roll(lower, PART, 1)).astype(jnp.bfloat16)
        second = jnp.where(lanes < PART, pltpu.roll(upper, PART, 1), lower).astype(jnp.bfloat16)
        for target in range(KN):
            out_ref[target, x, 0] = first
            out_ref[target, x, 1] = second


def after_projection(
    parent_ref, parts_ref, cos_ref, sin_ref, q_ref, all_ref, k_ref, v_ref, hold
):
    total = parts_ref[0]
    for source in range(1, ZN):
        total = total + parts_ref[source]
    cosines = cos_ref[...]
    sines = sin_ref[...]

    def turn(part):
        return part * cosines + pltpu.roll(part, HD // 2, 1) * sines

    for head in range(HEADS):
        hold[head * SB : (head + 1) * SB] = turn(total[:, head * HD : (head + 1) * HD])
    queries = hold[...].astype(jnp.bfloat16)
    q_ref[...] = queries
    for target in range(ZN):
        all_ref[target] = queries
    start = HEADS * HD
    fresh_key = turn(total[:, start : start + HD]).astype(jnp.bfloat16).astype(jnp.float32)
    fresh_value = total[:, start + HD :].astype(jnp.bfloat16).astype(jnp.float32)
    for index, (step, token) in enumerate(PAIRS):
        for ref, fresh in ((k_ref, fresh_key), (v_ref, fresh_value)):
            if token == step:
                ref[index] = fresh[step * GROUP : (step + 1) * GROUP]
            else:
                before = PAIRS.index((step - 1, token))
                for beam in range(GROUP):
                    parent = parent_ref[step * GROUP + beam]
                    ref[index, pl.ds(beam, 1), :] = ref[before, pl.ds(parent, 1), :]


def scan(place_ref, table_ref, length_ref, near_list, far_list, count_ref):
    x, core, z = place_ref[0], place_ref[1], place_ref[3]
    blocks = table_ref.shape[0] // (ZN * GROUP)
    half = SLOTS // 2

    def scan_beam(beam, found):
        used = lax.shift_right_logical(length_ref[beam] + (HD - 1), 7)

        def scan_block(block, found):
            slot = table_ref[beam * blocks + block]
            near, far = found
            hit = lax.shift_right_logical(slot, 8) == z
            hops = jnp.bitwise_and(lax.shift_right_logical(slot, 6) - x, XN - 1)
            opposite = hops == 2
            offset = jnp.bitwise_and(slot, half - 1)
            upper = jnp.bitwise_and(lax.shift_right_logical(slot, 4), 1)
            foreign = jnp.bitwise_xor(jnp.bitwise_and(lax.shift_right_logical(slot, 5), 1), core)
            chip = jnp.where(hops == 0, 0, jnp.where(hops == 3, 1, 2))
            segment = jnp.where(opposite, upper + 2 * foreign, chip * 4 + upper + 2 * foreign)
            code = ((beam * blocks + block) * SLOTS + segment) * SLOTS + offset

            @pl.when(hit & opposite)
            def _():
                far_list[far] = code

            @pl.when(hit & jnp.logical_not(opposite))
            def _():
                near_list[near] = code

            return (
                near + (hit & jnp.logical_not(opposite)).astype(jnp.int32),
                far + (hit & opposite).astype(jnp.int32),
            )

        return lax.fori_loop(0, used, scan_block, found)

    near, far = lax.fori_loop(0, ZN * GROUP, scan_beam, (0, 0))
    count_ref[0] = near
    count_ref[1] = far


def attend(list_ref, found, length_ref, q_ref, root_ref, sources, state, pages, arrived):
    top_ref, sum_ref, hold = state

    def fetch(item):
        code = list_ref[item]
        lane = lax.rem(item, DEPTH)
        offset = jnp.bitwise_and(code, SLOTS - 1)
        segment = jnp.bitwise_and(lax.shift_right_logical(code, 5), SLOTS - 1)
        for index, (ref, base) in enumerate(sources):

            @pl.when(segment == index)
            def _(ref=ref, base=base):
                pltpu.make_async_copy(
                    ref.at[base + offset], pages.at[lane], arrived.at[lane]
                ).start()

    for item in range(DEPTH):

        @pl.when(item < found)
        def _(item=item):
            fetch(item)

    tokens = lax.broadcasted_iota(jnp.int32, (SB, HD), 1)

    def visit(item, carry):
        lane = lax.rem(item, DEPTH)
        place = lax.shift_right_logical(list_ref[item], 10)
        beam = lax.shift_right_logical(place, 6)
        group = lax.shift_right_logical(beam, 3)
        count = length_ref[beam] - jnp.bitwise_and(place, 63) * HD
        live = (root_ref[group] == jnp.bitwise_and(beam, 7)) & (tokens < count)
        live = jnp.concatenate([live] * HEADS, axis=0)
        pltpu.make_async_copy(sources[0][0].at[0], pages.at[lane], arrived.at[lane]).wait()
        scores = (
            lax.dot_general(
                q_ref[group],
                pages[lane, 0],
                (((1,), (1,)), ((), ())),
                preferred_element_type=jnp.float32,
            )
            * SCALE
        )
        scores = jnp.where(live, scores, NEGATIVE)
        old = top_ref[group]
        new = jnp.maximum(old, jnp.max(scores, axis=1, keepdims=True))
        weights = jnp.where(live, jnp.exp(scores - new), 0.0)
        fade = jnp.exp(old - new)
        top_ref[group] = new
        sum_ref[group] = sum_ref[group] * fade + jnp.sum(weights, axis=1, keepdims=True)
        hold[group] = hold[group] * fade + jnp.dot(
            weights.astype(jnp.bfloat16), pages[lane, 1], preferred_element_type=jnp.float32
        )

        @pl.when(item + DEPTH < found)
        def _():
            fetch(item + DEPTH)

        return carry

    lax.fori_loop(0, found, visit, 0)


def attend_near(list_ref, count_ref, length_ref, q_ref, root_ref, *rest):
    wholes = rest[:6]
    top_ref, sum_ref, hold, pages, arrived = rest[6:]
    sources = [(whole, base) for whole in wholes for base in (0, SLOTS // 2)]
    top_ref[...] = jnp.full_like(top_ref, NEGATIVE)
    sum_ref[...] = jnp.zeros_like(sum_ref)
    hold[...] = jnp.zeros_like(hold)
    state = (top_ref, sum_ref, hold)
    attend(
        list_ref, count_ref[0], length_ref, q_ref, root_ref, sources, state, pages, arrived
    )


def attend_far(list_ref, count_ref, length_ref, q_ref, root_ref, *rest):
    parts, before, out_ref, state = rest[:4], rest[4:7], rest[7], rest[8:11]
    pages, arrived = rest[11:]
    for ref, start in zip(state, before):
        ref[...] = start[...]
    sources = [(part, 0) for part in parts]
    attend(
        list_ref, count_ref[1], length_ref, q_ref, root_ref, sources, state, pages, arrived
    )
    top_ref, sum_ref, hold = state
    lanes = lax.broadcasted_iota(jnp.int32, (GROUP, HD), 1)

    def pack(group, carry):
        tile = jnp.zeros((GROUP, HD), jnp.float32)
        for part in range(HEADS * STEPS):
            rows = slice(part * GROUP, (part + 1) * GROUP)
            tile = jnp.where(lanes == part, top_ref[group, rows, :], tile)
            tile = jnp.where(lanes == part + HD // 2, sum_ref[group, rows, :], tile)
        out_ref[group] = seal([hold[group]], tile)
        return carry

    lax.fori_loop(0, ZN, pack, 0)


def seal(sums, stat):
    high = stat.astype(jnp.bfloat16).astype(jnp.float32)
    middle = (stat - high).astype(jnp.bfloat16).astype(jnp.float32)
    low = stat - high - middle
    return jnp.concatenate(sums + [high, middle, low], axis=0).astype(jnp.bfloat16)


def unseal(block):
    block = block.astype(jnp.float32)
    stat = block[ROWS : ROWS + GROUP] + block[ROWS + GROUP : ROWS + 2 * GROUP]
    return block[:ROWS], stat + block[ROWS + 2 * GROUP :]


def finish(parts_ref, q_ref, k_ref, v_ref, out_ref, hold):
    count = parts_ref.shape[0]
    sums, stats = zip(*[unseal(parts_ref[source]) for source in range(count)])
    cached_top = functools.reduce(jnp.maximum, stats)
    queries = q_ref[...].astype(jnp.float32)
    lanes = lax.broadcasted_iota(jnp.int32, (GROUP, HD), 1)
    fresh = {}
    tops = cached_top
    for head in range(HEADS):
        for step in range(STEPS):
            part = head * STEPS + step
            row = head * SB + step * GROUP
            tile = queries[row : row + GROUP]
            for token in range(step + 1):
                key = k_ref[PAIRS.index((step, token))]
                score = jnp.sum(tile * key, axis=1, keepdims=True) * SCALE
                fresh[part, token] = score
                tops = jnp.where(lanes == part, jnp.maximum(tops, score), tops)
    fades = [jnp.exp(stat - tops) for stat in stats]
    total = sum(fade * pltpu.roll(stat, HD // 2, 1) for fade, stat in zip(fades, stats))
    for head in range(HEADS):
        for step in range(STEPS):
            part = head * STEPS + step
            rows = slice(part * GROUP, (part + 1) * GROUP)
            ceiling = tops[:, part : part + 1]
            below = total[:, part : part + 1]
            above = sum(
                fades[source][:, part : part + 1] * sums[source][rows] for source in range(count)
            )
            for token in range(step + 1):
                weight = jnp.exp(fresh[part, token] - ceiling)
                below = below + weight
                above = above + weight.astype(jnp.bfloat16).astype(jnp.float32) * v_ref[
                    PAIRS.index((step, token))
                ]
            hold[step * GROUP : (step + 1) * GROUP, head * HD : (head + 1) * HD] = above / below
    attended = hold[...].astype(jnp.bfloat16)
    for target in range(ZN):
        out_ref[target] = attended


def compose(parents_near):
    digits = jnp.arange(GROUP, dtype=jnp.int32)
    roots = [parents_near[0]]
    for step in range(1, STEPS):
        pick = parents_near[step][:, :, None] == digits
        roots.append(jnp.sum(jnp.where(pick, roots[-1][:, None, :], 0), axis=-1))
    return jnp.stack(roots)


def body(
    embeds, attn_gain, w_query, w_key, w_value, w_out, cache_kv, lengths, block_table, parents
):
    z = lax.axis_index("z")
    x = lax.axis_index("x")
    core = lax.axis_index("core")
    here = (z * XN + x) * CN + core
    groups = ZN * JN
    beams = groups * GROUP
    half_slots = SLOTS // 2
    width = PART * groups

    place = jnp.stack([x, core, lax.axis_index("kv"), z]).astype(jnp.int32)
    vmem = pl.BlockSpec(memory_space=pltpu.VMEM)
    smem = pl.BlockSpec(memory_space=pltpu.SMEM)
    cache = cache_kv[:, 0]

    base = jnp.arange(groups, dtype=jnp.int32)[None, :, None] * GROUP
    parents_near = parents.reshape(STEPS, groups, GROUP) - base
    roots_near = compose(parents_near)
    length_of = lengths.reshape(groups, GROUP)
    own_roots = lax.dynamic_slice_in_dim(roots_near, here, 1, 1)[:, 0]
    own_parents = lax.dynamic_slice_in_dim(parents_near, here, 1, 1)[:, 0]
    own_lengths = lax.dynamic_slice_in_dim(length_of, here, 1, 0)[0]
    digits = jnp.arange(GROUP, dtype=jnp.int32)
    position = jnp.sum(
        jnp.where(own_roots[:, :, None] == digits, own_lengths[None, None, :], 0), axis=-1
    ) + jnp.arange(STEPS, dtype=jnp.int32)[:, None]
    exponent = jnp.arange(HD // 2, dtype=jnp.float32) * (2.0 / HD)
    frequency = ROPE_BASE ** (-exponent)
    angles = position.reshape(SB).astype(jnp.float32)[:, None] * frequency[None, :]
    cosines = jnp.cos(angles)
    sines = jnp.sin(angles)
    cosines = jnp.concatenate([cosines, cosines], axis=1)
    sines = jnp.concatenate([-sines, sines], axis=1)
    lead = x * CN + core
    table = lax.dynamic_index_in_dim(
        block_table.reshape(ZN, JN, GROUP * block_table.shape[1]), lead, 1, keepdims=False
    ).reshape(-1)
    spans = lax.dynamic_index_in_dim(lengths.reshape(ZN, JN, GROUP), lead, 1, keepdims=False)
    root_tiles = lax.dynamic_index_in_dim(
        roots_near.reshape(STEPS, ZN, JN, GROUP), lead, 2, keepdims=False
    )
    alive = jnp.any(root_tiles[0][:, :, None] == digits, axis=1)
    spans = jnp.where(alive, spans, 0).reshape(-1)
    listing = jax.ShapeDtypeStruct((SLOTS * JN,), jnp.int32)
    near_list, far_list, counts = pl.pallas_call(
        scan,
        compiler_params=SMALL,
        out_shape=(listing, listing, jax.ShapeDtypeStruct((2,), jnp.int32)),
        in_specs=[smem] * 3,
        out_specs=(smem,) * 3,
    )(place, table, spans)
    root_tiles = root_tiles.transpose(1, 0, 2).reshape(ZN, SB)

    rows = ZN * SB
    half = rows // 2
    by_row = embeds.reshape(STEPS, ZN // 2, 2, JN, GROUP, PART).transpose(3, 1, 0, 4, 2, 5)
    by_row = by_row.reshape(JN, half, 2 * PART)
    high = lax.reduce_precision(attn_gain, 8, 7)
    middle = lax.reduce_precision(attn_gain - high, 8, 7)
    low = attn_gain - high - middle
    gain_rows = jnp.stack(
        [jnp.concatenate([high, middle]), jnp.concatenate([low, jnp.zeros_like(low)])]
    ).astype(jnp.bfloat16)
    gain_rows = jnp.concatenate([gain_rows, jnp.zeros((6, HD), jnp.bfloat16)])
    packed = jnp.concatenate([by_row, jnp.broadcast_to(gain_rows[None], (JN, 8, HD))], axis=1)
    weights = jnp.concatenate([w_query, w_key, w_value], axis=1)
    cache, weights = lax.optimization_barrier((cache, weights))
    weights = ring(weights)
    left = shift(cache, 1)
    right = shift(cache, -1)
    across = [shift(left[:half_slots], 1), shift(right[half_slots:], -1)]
    packed = exchange(packed, XC)
    stream = packed[:, :half].reshape(XN, CN, ZN // 2, SB, 2, PART).transpose(0, 2, 4, 3, 1, 5)
    stream = stream.reshape(XN, rows, 2 * PART).astype(jnp.float32)
    tails = packed[:, half : half + 2].astype(jnp.float32)
    gain = tails[:, 0, :PART] + tails[:, 0, PART:] + tails[:, 1, :PART]
    gain = gain.reshape(XN, 1, 2 * PART)
    squares = jnp.sum(stream * stream, axis=(0, 2))
    squares = jnp.pad(squares, (0, 256 - rows)).reshape(2, 128)
    squares = jnp.sum(spread(squares, "z", ZN), axis=0).reshape(256)[:rows]
    stream, weights = lax.optimization_barrier((stream, weights))
    weights = weights + [swap(part) for part in weights]
    inverse = lax.rsqrt(squares / width + EPSILON)
    normed = (stream * inverse[None, :, None] * gain).astype(jnp.bfloat16)
    columns = weights[0].shape[1]
    projected = pl.pallas_call(
        project,
        compiler_params=SMALL,
        out_shape=jax.ShapeDtypeStruct((rows, columns), jnp.float32),
        in_specs=[smem] + [vmem] * (1 + 2 * XN),
        out_specs=vmem,
        scratch_shapes=[pltpu.VMEM((XN, 2 * PART, columns), jnp.bfloat16)],
    )(place, normed, *weights)
    projected = exchange(projected.reshape(ZN, SB, columns), "z")
    root_tiles = jnp.broadcast_to(root_tiles[:, :, None], (ZN, SB, HD))
    projected, near_list, root_tiles = lax.optimization_barrier(
        (projected, near_list, root_tiles)
    )

    small = jax.ShapeDtypeStruct((len(PAIRS), GROUP, HD), jnp.float32)
    queries, everyone, key_chain, value_chain = pl.pallas_call(
        after_projection,
        compiler_params=SMALL,
        out_shape=(
            jax.ShapeDtypeStruct((ROWS, HD), jnp.bfloat16),
            jax.ShapeDtypeStruct((ZN, ROWS, HD), jnp.bfloat16),
            small,
            small,
        ),
        in_specs=[smem, vmem, vmem, vmem],
        out_specs=(vmem,) * 4,
        scratch_shapes=[pltpu.VMEM((ROWS, HD), jnp.float32)],
    )(own_parents.reshape(SB), projected, cosines, sines)
    near = [part for whole in (cache, left, right) for part in (whole, swap(whole))]
    last = PAIRS.index((STEPS - 1, 0))
    appended = jnp.stack([key_chain[last:], value_chain[last:]], axis=2)
    appended = appended[:, :, None].astype(jnp.bfloat16)

    everyone = exchange(everyone, "z")
    everyone, turned, across = lax.optimization_barrier((everyone, w_out.T, across))
    across = across + [swap(part) for part in across]
    turned = ring(turned)
    turned = turned + [swap(part) for part in turned]
    state = (jax.ShapeDtypeStruct((ZN, ROWS, HD), jnp.float32),) * 3
    ring_buffers = [
        pltpu.VMEM((DEPTH,) + cache.shape[1:], jnp.bfloat16),
        pltpu.SemaphoreType.DMA((DEPTH,)),
    ]
    anywhere = pl.BlockSpec(memory_space=pltpu.HBM)
    before = pl.pallas_call(
        attend_near,
        compiler_params=SMALL,
        out_shape=state,
        in_specs=[smem, smem, smem, vmem, vmem] + [anywhere] * 6,
        out_specs=(vmem,) * 3,
        scratch_shapes=ring_buffers,
        cost_estimate=pl.CostEstimate(flops=1, bytes_accessed=1, transcendentals=0),
    )(near_list, counts, spans, everyone, root_tiles, *near)
    partial = pl.pallas_call(
        attend_far,
        compiler_params=SMALL,
        out_shape=jax.ShapeDtypeStruct((ZN, BLOCK, HD), jnp.bfloat16),
        in_specs=[smem, smem, smem, vmem, vmem] + [anywhere] * 4 + [vmem] * 3,
        out_specs=vmem,
        scratch_shapes=[pltpu.VMEM(part.shape, part.dtype) for part in state] + ring_buffers,
    )(far_list, counts, spans, everyone, root_tiles, *across, *before)

    partial = exchange(partial, "z")
    partial, turned = lax.optimization_barrier((partial, turned))
    attended = pl.pallas_call(
        finish,
        compiler_params=SMALL,
        out_shape=jax.ShapeDtypeStruct((ZN, SB, HEADS * HD), jnp.bfloat16),
        in_specs=[vmem] * 4,
        out_specs=vmem,
        scratch_shapes=[pltpu.VMEM((SB, HEADS * HD), jnp.float32)],
    )(partial, queries, key_chain, value_chain)

    attended = exchange(attended, "z").reshape(rows, HEADS * HD)
    share = jax.ShapeDtypeStruct((XN, QUARTER, 2 * PART), jnp.float32)
    shares = pl.pallas_call(
        deliver,
        compiler_params=SMALL,
        out_shape=(share,) * KN,
        in_specs=[smem] + [vmem] * (1 + 2 * XN),
        out_specs=(vmem,) * KN,
        scratch_shapes=[
            pltpu.VMEM((XN, 2 * PART, HEADS * HD), jnp.bfloat16),
            pltpu.VMEM((rows, 2 * PART), jnp.float32),
        ],
    )(place, attended, *turned)
    shares = [shares[0]] + [
        lax.ppermute(shares[far], "kv", [(i, (i + far) % KN) for i in range(KN)])
        for far in range(1, KN)
    ]
    result = pl.pallas_call(
        settle,
        compiler_params=SMALL,
        out_shape=jax.ShapeDtypeStruct((KN, XN, CN, SB, 2 * PART), jnp.bfloat16),
        in_specs=[smem] + [vmem] * (KN + 1),
        out_specs=vmem,
    )(place, *shares, stream)
    result = exchange(result.reshape(KN * JN, SB, 2 * PART), ("kv",) + XC)
    result = result.reshape(KN, JN, STEPS, GROUP, 2, PART).transpose(2, 0, 4, 1, 3, 5)
    return (result.reshape(STEPS, beams, PART), appended)


def solution(mesh):
    fine = Mesh(mesh.devices.reshape(-1, ZN, XN, CN), ("kv",) + BLK)
    return jax.shard_map(
        body,
        mesh=fine,
        in_specs=(
            P(None, None, BLK),
            P(BLK),
            P(BLK, "kv"),
            P(BLK, "kv"),
            P(BLK, "kv"),
            P("kv", BLK),
            P(BLK, "kv", None, None, None),
            P(),
            P(),
            P(),
        ),
        out_specs=(P(None, None, BLK), P(None, BLK, "kv", None, None)),
        check_vma=False,
    )
```

```python
import functools
import math

import jax
import jax.numpy as jnp
from jax import lax
from jax.experimental import pallas as pl
from jax.experimental.pallas import tpu as pltpu
from jax.sharding import Mesh
from jax.sharding import PartitionSpec as P

GROUP = 8
NEGATIVE = -1e30
EPSILON = 1e-05
ROPE_BASE = 5000000.0
STEPS = 3
HEADS = 8
HD = 128
SB = STEPS * GROUP
ROWS = HEADS * SB
BLOCK = ROWS + 3 * GROUP
ZN, XN, CN = 8, 4, 2
JN = XN * CN
KN = 4
PART = 64
SLOTS = 32
DEPTH = 12
QUARTER = ZN * SB // KN
SMALL = pltpu.CompilerParams(vmem_limit_bytes=16 << 20)
PAIRS = [(s, u) for s in range(STEPS) for u in range(s + 1)]
SCALE = 1.0 / math.sqrt(HD)
XC = ("x", "core")
BLK = ("z", "x", "core")


def exchange(value, axis):
    return lax.all_to_all(value, axis, 0, 0, tiled=True)


def spread(value, axis, count):
    return exchange(jnp.broadcast_to(value[None], (count,) + value.shape), axis)


def swap(value):
    return lax.ppermute(value, "core", [(0, 1), (1, 0)])


def shift(value, hop):
    return lax.ppermute(value, "x", [(i, (i + hop) % XN) for i in range(XN)])


def ring(value):
    return [value] + [shift(value, hop) for hop in range(1, XN)]


def join(place_ref, chunks, wide):
    core = place_ref[1]
    for hop in range(XN):
        wide[hop, pl.ds(pl.multiple_of(core * PART, PART), PART), :] = chunks[hop][...]
        wide[hop, pl.ds(pl.multiple_of((1 - core) * PART, PART), PART), :] = chunks[XN + hop][...]


def project(place_ref, rows_ref, *rest):
    chunks, out_ref, wide = rest[: 2 * XN], rest[2 * XN], rest[2 * XN + 1]
    join(place_ref, chunks, wide)
    x = place_ref[0]
    for start in range(0, out_ref.shape[1], 256):
        out_ref[:, start : start + 256] = sum(
            jnp.dot(
                rows_ref[(x + XN - hop) % XN],
                wide[hop, :, start : start + 256],
                preferred_element_type=jnp.float32,
            )
            for hop in range(XN)
        )


def deliver(place_ref, rows_ref, *rest):
    chunks, outs, wide = rest[: 2 * XN], rest[2 * XN : 2 * XN + KN], rest[2 * XN + KN]
    hold = rest[2 * XN + KN + 1]
    join(place_ref, chunks, wide)
    x, kv = place_ref[0], place_ref[2]
    for hop in range(XN):
        hold[...] = lax.dot_general(
            rows_ref[...],
            wide[hop],
            (((1,), (1,)), ((), ())),
            preferred_element_type=jnp.float32,
        )
        for far in range(KN):
            start = pl.multiple_of(lax.rem(kv + far, KN) * QUARTER, 8)
            outs[far][lax.rem(x + XN - hop, XN)] = hold[pl.ds(start, QUARTER), :]


def settle(place_ref, *rest):
    parts, stream_ref, out_ref = rest[:KN], rest[KN], rest[KN + 1]
    kv = place_ref[2]
    lanes = lax.broadcasted_iota(jnp.int32, (SB, 2 * PART), 1)
    for x in range(XN):
        total = parts[0][x]
        for part in parts[1:]:
            total = total + part[x]
        total = stream_ref[x, pl.ds(pl.multiple_of(kv * QUARTER, 8), QUARTER), :] + total
        upper, lower = total[:SB], total[SB:]
        first = jnp.where(lanes < PART, upper, pltpu.roll(lower, PART, 1)).astype(jnp.bfloat16)
        second = jnp.where(lanes < PART, pltpu.roll(upper, PART, 1), lower).astype(jnp.bfloat16)
        for target in range(KN):
            out_ref[target, x, 0] = first
            out_ref[target, x, 1] = second


def after_projection(
    parent_ref, parts_ref, cos_ref, sin_ref, q_ref, all_ref, k_ref, v_ref, hold
):
    total = parts_ref[0]
    for source in range(1, ZN):
        total = total + parts_ref[source]
    cosines = cos_ref[...]
    sines = sin_ref[...]

    def turn(part):
        return part * cosines + pltpu.roll(part, HD // 2, 1) * sines

    for head in range(HEADS):
        hold[head * SB : (head + 1) * SB] = turn(total[:, head * HD : (head + 1) * HD])
    queries = hold[...].astype(jnp.bfloat16)
    q_ref[...] = queries
    for target in range(ZN):
        all_ref[target] = queries
    start = HEADS * HD
    fresh_key = turn(total[:, start : start + HD]).astype(jnp.bfloat16).astype(jnp.float32)
    fresh_value = total[:, start + HD :].astype(jnp.bfloat16).astype(jnp.float32)
    for index, (step, token) in enumerate(PAIRS):
        for ref, fresh in ((k_ref, fresh_key), (v_ref, fresh_value)):
            if token == step:
                ref[index] = fresh[step * GROUP : (step + 1) * GROUP]
            else:
                before = PAIRS.index((step - 1, token))
                for beam in range(GROUP):
                    parent = parent_ref[step * GROUP + beam]
                    ref[index, pl.ds(beam, 1), :] = ref[before, pl.ds(parent, 1), :]


def scan(place_ref, table_ref, length_ref, near_list, far_list, count_ref):
    x, core, z = place_ref[0], place_ref[1], place_ref[3]
    blocks = table_ref.shape[0] // (ZN * GROUP)
    half = SLOTS // 2

    def scan_beam(beam, found):
        used = lax.shift_right_logical(length_ref[beam] + (HD - 1), 7)

        def scan_block(block, found):
            slot = table_ref[beam * blocks + block]
            near, far = found
            hit = lax.shift_right_logical(slot, 8) == z
            hops = jnp.bitwise_and(lax.shift_right_logical(slot, 6) - x, XN - 1)
            opposite = hops == 2
            offset = jnp.bitwise_and(slot, half - 1)
            upper = jnp.bitwise_and(lax.shift_right_logical(slot, 4), 1)
            foreign = jnp.bitwise_xor(jnp.bitwise_and(lax.shift_right_logical(slot, 5), 1), core)
            chip = jnp.where(hops == 0, 0, jnp.where(hops == 3, 1, 2))
            segment = jnp.where(opposite, upper + 2 * foreign, chip * 4 + upper + 2 * foreign)
            code = ((beam * blocks + block) * SLOTS + segment) * SLOTS + offset

            @pl.when(hit & opposite)
            def _():
                far_list[far] = code

            @pl.when(hit & jnp.logical_not(opposite))
            def _():
                near_list[near] = code

            return (
                near + (hit & jnp.logical_not(opposite)).astype(jnp.int32),
                far + (hit & opposite).astype(jnp.int32),
            )

        return lax.fori_loop(0, used, scan_block, found)

    near, far = lax.fori_loop(0, ZN * GROUP, scan_beam, (0, 0))
    count_ref[0] = near
    count_ref[1] = far


def attend(list_ref, found, length_ref, q_ref, root_ref, sources, state, pages, arrived):
    top_ref, sum_ref, hold = state

    def fetch(item):
        code = list_ref[item]
        lane = lax.rem(item, DEPTH)
        offset = jnp.bitwise_and(code, SLOTS - 1)
        segment = jnp.bitwise_and(lax.shift_right_logical(code, 5), SLOTS - 1)
        for index, (ref, base) in enumerate(sources):

            @pl.when(segment == index)
            def _(ref=ref, base=base):
                pltpu.make_async_copy(
                    ref.at[base + offset], pages.at[lane], arrived.at[lane]
                ).start()

    for item in range(DEPTH):

        @pl.when(item < found)
        def _(item=item):
            fetch(item)

    tokens = lax.broadcasted_iota(jnp.int32, (SB, HD), 1)

    def visit(item, carry):
        lane = lax.rem(item, DEPTH)
        place = lax.shift_right_logical(list_ref[item], 10)
        beam = lax.shift_right_logical(place, 6)
        group = lax.shift_right_logical(beam, 3)
        count = length_ref[beam] - jnp.bitwise_and(place, 63) * HD
        live = (root_ref[group] == jnp.bitwise_and(beam, 7)) & (tokens < count)
        live = jnp.concatenate([live] * HEADS, axis=0)
        pltpu.make_async_copy(sources[0][0].at[0], pages.at[lane], arrived.at[lane]).wait()
        scores = (
            lax.dot_general(
                q_ref[group],
                pages[lane, 0],
                (((1,), (1,)), ((), ())),
                preferred_element_type=jnp.float32,
            )
            * SCALE
        )
        scores = jnp.where(live, scores, NEGATIVE)
        old = top_ref[group]
        new = jnp.maximum(old, jnp.max(scores, axis=1, keepdims=True))
        weights = jnp.where(live, jnp.exp(scores - new), 0.0)
        fade = jnp.exp(old - new)
        top_ref[group] = new
        sum_ref[group] = sum_ref[group] * fade + jnp.sum(weights, axis=1, keepdims=True)
        hold[group] = hold[group] * fade + jnp.dot(
            weights.astype(jnp.bfloat16), pages[lane, 1], preferred_element_type=jnp.float32
        )

        @pl.when(item + DEPTH < found)
        def _():
            fetch(item + DEPTH)

        return carry

    lax.fori_loop(0, found, visit, 0)


def attend_near(list_ref, count_ref, length_ref, q_ref, root_ref, *rest):
    wholes = rest[:6]
    top_ref, sum_ref, hold, pages, arrived = rest[6:]
    sources = [(whole, base) for whole in wholes for base in (0, SLOTS // 2)]
    top_ref[...] = jnp.full_like(top_ref, NEGATIVE)
    sum_ref[...] = jnp.zeros_like(sum_ref)
    hold[...] = jnp.zeros_like(hold)
    state = (top_ref, sum_ref, hold)
    attend(
        list_ref, count_ref[0], length_ref, q_ref, root_ref, sources, state, pages, arrived
    )


def attend_far(list_ref, count_ref, length_ref, q_ref, root_ref, *rest):
    parts, before, out_ref, state = rest[:4], rest[4:7], rest[7], rest[8:11]
    pages, arrived = rest[11:]
    for ref, start in zip(state, before):
        ref[...] = start[...]
    sources = [(part, 0) for part in parts]
    attend(
        list_ref, count_ref[1], length_ref, q_ref, root_ref, sources, state, pages, arrived
    )
    top_ref, sum_ref, hold = state
    lanes = lax.broadcasted_iota(jnp.int32, (GROUP, HD), 1)

    def pack(group, carry):
        tile = jnp.zeros((GROUP, HD), jnp.float32)
        for part in range(HEADS * STEPS):
            rows = slice(part * GROUP, (part + 1) * GROUP)
            tile = jnp.where(lanes == part, top_ref[group, rows, :], tile)
            tile = jnp.where(lanes == part + HD // 2, sum_ref[group, rows, :], tile)
        out_ref[group] = seal([hold[group]], tile)
        return carry

    lax.fori_loop(0, ZN, pack, 0)


def seal(sums, stat):
    high = stat.astype(jnp.bfloat16).astype(jnp.float32)
    middle = (stat - high).astype(jnp.bfloat16).astype(jnp.float32)
    low = stat - high - middle
    return jnp.concatenate(sums + [high, middle, low], axis=0).astype(jnp.bfloat16)


def unseal(block):
    block = block.astype(jnp.float32)
    stat = block[ROWS : ROWS + GROUP] + block[ROWS + GROUP : ROWS + 2 * GROUP]
    return block[:ROWS], stat + block[ROWS + 2 * GROUP :]


def finish(parts_ref, q_ref, k_ref, v_ref, out_ref, hold):
    count = parts_ref.shape[0]
    sums, stats = zip(*[unseal(parts_ref[source]) for source in range(count)])
    cached_top = functools.reduce(jnp.maximum, stats)
    queries = q_ref[...].astype(jnp.float32)
    lanes = lax.broadcasted_iota(jnp.int32, (GROUP, HD), 1)
    fresh = {}
    tops = cached_top
    for head in range(HEADS):
        for step in range(STEPS):
            part = head * STEPS + step
            row = head * SB + step * GROUP
            tile = queries[row : row + GROUP]
            for token in range(step + 1):
                key = k_ref[PAIRS.index((step, token))]
                score = jnp.sum(tile * key, axis=1, keepdims=True) * SCALE
                fresh[part, token] = score
                tops = jnp.where(lanes == part, jnp.maximum(tops, score), tops)
    fades = [jnp.exp(stat - tops) for stat in stats]
    total = sum(fade * pltpu.roll(stat, HD // 2, 1) for fade, stat in zip(fades, stats))
    for head in range(HEADS):
        for step in range(STEPS):
            part = head * STEPS + step
            rows = slice(part * GROUP, (part + 1) * GROUP)
            ceiling = tops[:, part : part + 1]
            below = total[:, part : part + 1]
            above = sum(
                fades[source][:, part : part + 1] * sums[source][rows] for source in range(count)
            )
            for token in range(step + 1):
                weight = jnp.exp(fresh[part, token] - ceiling)
                below = below + weight
                above = above + weight.astype(jnp.bfloat16).astype(jnp.float32) * v_ref[
                    PAIRS.index((step, token))
                ]
            hold[step * GROUP : (step + 1) * GROUP, head * HD : (head + 1) * HD] = above / below
    attended = hold[...].astype(jnp.bfloat16)
    for target in range(ZN):
        out_ref[target] = attended


def compose(parents_near):
    digits = jnp.arange(GROUP, dtype=jnp.int32)
    roots = [parents_near[0]]
    for step in range(1, STEPS):
        pick = parents_near[step][:, :, None] == digits
        roots.append(jnp.sum(jnp.where(pick, roots[-1][:, None, :], 0), axis=-1))
    return jnp.stack(roots)


def body(
    embeds, attn_gain, w_query, w_key, w_value, w_out, cache_kv, lengths, block_table, parents
):
    z = lax.axis_index("z")
    x = lax.axis_index("x")
    core = lax.axis_index("core")
    here = (z * XN + x) * CN + core
    groups = ZN * JN
    beams = groups * GROUP
    half_slots = SLOTS // 2
    width = PART * groups

    place = jnp.stack([x, core, lax.axis_index("kv"), z]).astype(jnp.int32)
    vmem = pl.BlockSpec(memory_space=pltpu.VMEM)
    smem = pl.BlockSpec(memory_space=pltpu.SMEM)
    cache = cache_kv[:, 0]

    base = jnp.arange(groups, dtype=jnp.int32)[None, :, None] * GROUP
    parents_near = parents.reshape(STEPS, groups, GROUP) - base
    roots_near = compose(parents_near)
    length_of = lengths.reshape(groups, GROUP)
    own_roots = lax.dynamic_slice_in_dim(roots_near, here, 1, 1)[:, 0]
    own_parents = lax.dynamic_slice_in_dim(parents_near, here, 1, 1)[:, 0]
    own_lengths = lax.dynamic_slice_in_dim(length_of, here, 1, 0)[0]
    digits = jnp.arange(GROUP, dtype=jnp.int32)
    position = jnp.sum(
        jnp.where(own_roots[:, :, None] == digits, own_lengths[None, None, :], 0), axis=-1
    ) + jnp.arange(STEPS, dtype=jnp.int32)[:, None]
    exponent = jnp.arange(HD // 2, dtype=jnp.float32) * (2.0 / HD)
    frequency = ROPE_BASE ** (-exponent)
    angles = position.reshape(SB).astype(jnp.float32)[:, None] * frequency[None, :]
    cosines = jnp.cos(angles)
    sines = jnp.sin(angles)
    cosines = jnp.concatenate([cosines, cosines], axis=1)
    sines = jnp.concatenate([-sines, sines], axis=1)
    lead = x * CN + core
    table = lax.dynamic_index_in_dim(
        block_table.reshape(ZN, JN, GROUP * block_table.shape[1]), lead, 1, keepdims=False
    ).reshape(-1)
    spans = lax.dynamic_index_in_dim(lengths.reshape(ZN, JN, GROUP), lead, 1, keepdims=False)
    root_tiles = lax.dynamic_index_in_dim(
        roots_near.reshape(STEPS, ZN, JN, GROUP), lead, 2, keepdims=False
    )
    alive = jnp.any(root_tiles[0][:, :, None] == digits, axis=1)
    spans = jnp.where(alive, spans, 0).reshape(-1)
    listing = jax.ShapeDtypeStruct((SLOTS * JN,), jnp.int32)
    near_list, far_list, counts = pl.pallas_call(
        scan,
        compiler_params=SMALL,
        out_shape=(listing, listing, jax.ShapeDtypeStruct((2,), jnp.int32)),
        in_specs=[smem] * 3,
        out_specs=(smem,) * 3,
    )(place, table, spans)
    root_tiles = root_tiles.transpose(1, 0, 2).reshape(ZN, SB)

    rows = ZN * SB
    half = rows // 2
    by_row = embeds.reshape(STEPS, ZN // 2, 2, JN, GROUP, PART).transpose(3, 1, 0, 4, 2, 5)
    by_row = by_row.reshape(JN, half, 2 * PART)
    high = lax.reduce_precision(attn_gain, 8, 7)
    middle = lax.reduce_precision(attn_gain - high, 8, 7)
    low = attn_gain - high - middle
    gain_rows = jnp.stack(
        [jnp.concatenate([high, middle]), jnp.concatenate([low, jnp.zeros_like(low)])]
    ).astype(jnp.bfloat16)
    gain_rows = jnp.concatenate([gain_rows, jnp.zeros((6, HD), jnp.bfloat16)])
    packed = jnp.concatenate([by_row, jnp.broadcast_to(gain_rows[None], (JN, 8, HD))], axis=1)
    weights = jnp.concatenate([w_query, w_key, w_value], axis=1)
    weights = ring(weights)
    packed = exchange(packed, XC)
    stream = packed[:, :half].reshape(XN, CN, ZN // 2, SB, 2, PART).transpose(0, 2, 4, 3, 1, 5)
    stream = stream.reshape(XN, rows, 2 * PART).astype(jnp.float32)
    tails = packed[:, half : half + 2].astype(jnp.float32)
    gain = tails[:, 0, :PART] + tails[:, 0, PART:] + tails[:, 1, :PART]
    gain = gain.reshape(XN, 1, 2 * PART)
    squares = jnp.sum(stream * stream, axis=(0, 2))
    squares = jnp.pad(squares, (0, 256 - rows)).reshape(2, 128)
    cache, squares = lax.optimization_barrier((cache, squares))
    left = shift(cache, 1)
    right = shift(cache, -1)
    across = [shift(left[:half_slots], 1), shift(right[half_slots:], -1)]
    squares = jnp.sum(spread(squares, "z", ZN), axis=0).reshape(256)[:rows]
    stream, weights = lax.optimization_barrier((stream, weights))
    weights = weights + [swap(part) for part in weights]
    inverse = lax.rsqrt(squares / width + EPSILON)
    normed = (stream * inverse[None, :, None] * gain).astype(jnp.bfloat16)
    columns = weights[0].shape[1]
    projected = pl.pallas_call(
        project,
        compiler_params=SMALL,
        out_shape=jax.ShapeDtypeStruct((rows, columns), jnp.float32),
        in_specs=[smem] + [vmem] * (1 + 2 * XN),
        out_specs=vmem,
        scratch_shapes=[pltpu.VMEM((XN, 2 * PART, columns), jnp.bfloat16)],
    )(place, normed, *weights)
    projected = exchange(projected.reshape(ZN, SB, columns), "z")
    root_tiles = jnp.broadcast_to(root_tiles[:, :, None], (ZN, SB, HD))
    projected, near_list, root_tiles = lax.optimization_barrier(
        (projected, near_list, root_tiles)
    )

    small = jax.ShapeDtypeStruct((len(PAIRS), GROUP, HD), jnp.float32)
    queries, everyone, key_chain, value_chain = pl.pallas_call(
        after_projection,
        compiler_params=SMALL,
        out_shape=(
            jax.ShapeDtypeStruct((ROWS, HD), jnp.bfloat16),
            jax.ShapeDtypeStruct((ZN, ROWS, HD), jnp.bfloat16),
            small,
            small,
        ),
        in_specs=[smem, vmem, vmem, vmem],
        out_specs=(vmem,) * 4,
        scratch_shapes=[pltpu.VMEM((ROWS, HD), jnp.float32)],
    )(own_parents.reshape(SB), projected, cosines, sines)
    near = [part for whole in (cache, left, right) for part in (whole, swap(whole))]
    last = PAIRS.index((STEPS - 1, 0))
    appended = jnp.stack([key_chain[last:], value_chain[last:]], axis=2)
    appended = appended[:, :, None].astype(jnp.bfloat16)

    everyone = exchange(everyone, "z")
    everyone, turned, across = lax.optimization_barrier((everyone, w_out.T, across))
    across = across + [swap(part) for part in across]
    turned = ring(turned)
    turned = turned + [swap(part) for part in turned]
    state = (jax.ShapeDtypeStruct((ZN, ROWS, HD), jnp.float32),) * 3
    ring_buffers = [
        pltpu.VMEM((DEPTH,) + cache.shape[1:], jnp.bfloat16),
        pltpu.SemaphoreType.DMA((DEPTH,)),
    ]
    anywhere = pl.BlockSpec(memory_space=pltpu.HBM)
    before = pl.pallas_call(
        attend_near,
        compiler_params=SMALL,
        out_shape=state,
        in_specs=[smem, smem, smem, vmem, vmem] + [anywhere] * 6,
        out_specs=(vmem,) * 3,
        scratch_shapes=ring_buffers,
        cost_estimate=pl.CostEstimate(flops=1, bytes_accessed=1, transcendentals=0),
    )(near_list, counts, spans, everyone, root_tiles, *near)
    partial = pl.pallas_call(
        attend_far,
        compiler_params=SMALL,
        out_shape=jax.ShapeDtypeStruct((ZN, BLOCK, HD), jnp.bfloat16),
        in_specs=[smem, smem, smem, vmem, vmem] + [anywhere] * 4 + [vmem] * 3,
        out_specs=vmem,
        scratch_shapes=[pltpu.VMEM(part.shape, part.dtype) for part in state] + ring_buffers,
    )(far_list, counts, spans, everyone, root_tiles, *across, *before)

    partial = exchange(partial, "z")
    partial, turned = lax.optimization_barrier((partial, turned))
    attended = pl.pallas_call(
        finish,
        compiler_params=SMALL,
        out_shape=jax.ShapeDtypeStruct((ZN, SB, HEADS * HD), jnp.bfloat16),
        in_specs=[vmem] * 4,
        out_specs=vmem,
        scratch_shapes=[pltpu.VMEM((SB, HEADS * HD), jnp.float32)],
    )(partial, queries, key_chain, value_chain)

    attended = exchange(attended, "z").reshape(rows, HEADS * HD)
    share = jax.ShapeDtypeStruct((XN, QUARTER, 2 * PART), jnp.float32)
    shares = pl.pallas_call(
        deliver,
        compiler_params=SMALL,
        out_shape=(share,) * KN,
        in_specs=[smem] + [vmem] * (1 + 2 * XN),
        out_specs=(vmem,) * KN,
        scratch_shapes=[
            pltpu.VMEM((XN, 2 * PART, HEADS * HD), jnp.bfloat16),
            pltpu.VMEM((rows, 2 * PART), jnp.float32),
        ],
    )(place, attended, *turned)
    shares = [shares[0]] + [
        lax.ppermute(shares[far], "kv", [(i, (i + far) % KN) for i in range(KN)])
        for far in range(1, KN)
    ]
    result = pl.pallas_call(
        settle,
        compiler_params=SMALL,
        out_shape=jax.ShapeDtypeStruct((KN, XN, CN, SB, 2 * PART), jnp.bfloat16),
        in_specs=[smem] + [vmem] * (KN + 1),
        out_specs=vmem,
    )(place, *shares, stream)
    result = exchange(result.reshape(KN * JN, SB, 2 * PART), ("kv",) + XC)
    result = result.reshape(KN, JN, STEPS, GROUP, 2, PART).transpose(2, 0, 4, 1, 3, 5)
    return (result.reshape(STEPS, beams, PART), appended)


def solution(mesh):
    fine = Mesh(mesh.devices.reshape(-1, ZN, XN, CN), ("kv",) + BLK)
    return jax.shard_map(
        body,
        mesh=fine,
        in_specs=(
            P(None, None, BLK),
            P(BLK),
            P(BLK, "kv"),
            P(BLK, "kv"),
            P(BLK, "kv"),
            P("kv", BLK),
            P(BLK, "kv", None, None, None),
            P(),
            P(),
            P(),
        ),
        out_specs=(P(None, None, BLK), P(None, BLK, "kv", None, None)),
        check_vma=False,
    )
```

```python
import functools
import math

import jax
import jax.numpy as jnp
from jax import lax
from jax.experimental import pallas as pl
from jax.experimental.pallas import tpu as pltpu
from jax.sharding import Mesh
from jax.sharding import PartitionSpec as P

GROUP = 8
NEGATIVE = -1e30
EPSILON = 1e-05
ROPE_BASE = 5000000.0
STEPS = 3
HEADS = 8
HD = 128
SB = STEPS * GROUP
ROWS = HEADS * SB
BLOCK = ROWS + 3 * GROUP
ZN, XN, CN = 8, 4, 2
JN = XN * CN
KN = 4
PART = 64
SLOTS = 32
DEPTH = 12
QUARTER = ZN * SB // KN
SMALL = pltpu.CompilerParams(vmem_limit_bytes=16 << 20)
PAIRS = [(s, u) for s in range(STEPS) for u in range(s + 1)]
SCALE = 1.0 / math.sqrt(HD)
XC = ("x", "core")
BLK = ("z", "x", "core")


def exchange(value, axis):
    return lax.all_to_all(value, axis, 0, 0, tiled=True)


def spread(value, axis, count):
    return exchange(jnp.broadcast_to(value[None], (count,) + value.shape), axis)


def swap(value):
    return lax.ppermute(value, "core", [(0, 1), (1, 0)])


def shift(value, hop):
    return lax.ppermute(value, "x", [(i, (i + hop) % XN) for i in range(XN)])


def ring(value):
    return [value] + [shift(value, hop) for hop in range(1, XN)]


def join(place_ref, chunks, wide):
    core = place_ref[1]
    for hop in range(XN):
        wide[hop, pl.ds(pl.multiple_of(core * PART, PART), PART), :] = chunks[hop][...]
        wide[hop, pl.ds(pl.multiple_of((1 - core) * PART, PART), PART), :] = chunks[XN + hop][...]


def project(place_ref, rows_ref, *rest):
    chunks, out_ref, wide = rest[: 2 * XN], rest[2 * XN], rest[2 * XN + 1]
    join(place_ref, chunks, wide)
    x = place_ref[0]
    for start in range(0, out_ref.shape[1], 256):
        out_ref[:, start : start + 256] = sum(
            jnp.dot(
                rows_ref[(x + XN - hop) % XN],
                wide[hop, :, start : start + 256],
                preferred_element_type=jnp.float32,
            )
            for hop in range(XN)
        )


def deliver(place_ref, rows_ref, *rest):
    chunks, outs, wide = rest[: 2 * XN], rest[2 * XN : 2 * XN + KN], rest[2 * XN + KN]
    hold = rest[2 * XN + KN + 1]
    join(place_ref, chunks, wide)
    x, kv = place_ref[0], place_ref[2]
    for hop in range(XN):
        hold[...] = lax.dot_general(
            rows_ref[...],
            wide[hop],
            (((1,), (1,)), ((), ())),
            preferred_element_type=jnp.float32,
        )
        for far in range(KN):
            start = pl.multiple_of(lax.rem(kv + far, KN) * QUARTER, 8)
            outs[far][lax.rem(x + XN - hop, XN)] = hold[pl.ds(start, QUARTER), :]


def settle(place_ref, *rest):
    parts, stream_ref, out_ref = rest[:KN], rest[KN], rest[KN + 1]
    kv = place_ref[2]
    lanes = lax.broadcasted_iota(jnp.int32, (SB, 2 * PART), 1)
    for x in range(XN):
        total = parts[0][x]
        for part in parts[1:]:
            total = total + part[x]
        total = stream_ref[x, pl.ds(pl.multiple_of(kv * QUARTER, 8), QUARTER), :] + total
        upper, lower = total[:SB], total[SB:]
        first = jnp.where(lanes < PART, upper, pltpu.roll(lower, PART, 1)).astype(jnp.bfloat16)
        second = jnp.where(lanes < PART, pltpu.roll(upper, PART, 1), lower).astype(jnp.bfloat16)
        for target in range(KN):
            out_ref[target, x, 0] = first
            out_ref[target, x, 1] = second


def after_projection(
    parent_ref, parts_ref, cos_ref, sin_ref, q_ref, all_ref, k_ref, v_ref, hold
):
    total = parts_ref[0]
    for source in range(1, ZN):
        total = total + parts_ref[source]
    cosines = cos_ref[...]
    sines = sin_ref[...]

    def turn(part):
        return part * cosines + pltpu.roll(part, HD // 2, 1) * sines

    for head in range(HEADS):
        hold[head * SB : (head + 1) * SB] = turn(total[:, head * HD : (head + 1) * HD])
    queries = hold[...].astype(jnp.bfloat16)
    q_ref[...] = queries
    for target in range(ZN):
        all_ref[target] = queries
    start = HEADS * HD
    fresh_key = turn(total[:, start : start + HD]).astype(jnp.bfloat16).astype(jnp.float32)
    fresh_value = total[:, start + HD :].astype(jnp.bfloat16).astype(jnp.float32)
    for index, (step, token) in enumerate(PAIRS):
        for ref, fresh in ((k_ref, fresh_key), (v_ref, fresh_value)):
            if token == step:
                ref[index] = fresh[step * GROUP : (step + 1) * GROUP]
            else:
                before = PAIRS.index((step - 1, token))
                for beam in range(GROUP):
                    parent = parent_ref[step * GROUP + beam]
                    ref[index, pl.ds(beam, 1), :] = ref[before, pl.ds(parent, 1), :]


def scan(place_ref, table_ref, length_ref, near_list, far_list, count_ref):
    x, core, z = place_ref[0], place_ref[1], place_ref[3]
    blocks = table_ref.shape[0] // (ZN * GROUP)
    half = SLOTS // 2

    def scan_beam(beam, found):
        used = lax.shift_right_logical(length_ref[beam] + (HD - 1), 7)

        def scan_block(block, found):
            slot = table_ref[beam * blocks + block]
            near, far = found
            hit = lax.shift_right_logical(slot, 8) == z
            hops = jnp.bitwise_and(lax.shift_right_logical(slot, 6) - x, XN - 1)
            opposite = hops == 2
            offset = jnp.bitwise_and(slot, half - 1)
            upper = jnp.bitwise_and(lax.shift_right_logical(slot, 4), 1)
            foreign = jnp.bitwise_xor(jnp.bitwise_and(lax.shift_right_logical(slot, 5), 1), core)
            chip = jnp.where(hops == 0, 0, jnp.where(hops == 3, 1, 2))
            segment = jnp.where(opposite, upper + 2 * foreign, chip * 4 + upper + 2 * foreign)
            code = ((beam * blocks + block) * SLOTS + segment) * SLOTS + offset

            @pl.when(hit & opposite)
            def _():
                far_list[far] = code

            @pl.when(hit & jnp.logical_not(opposite))
            def _():
                near_list[near] = code

            return (
                near + (hit & jnp.logical_not(opposite)).astype(jnp.int32),
                far + (hit & opposite).astype(jnp.int32),
            )

        return lax.fori_loop(0, used, scan_block, found)

    near, far = lax.fori_loop(0, ZN * GROUP, scan_beam, (0, 0))
    count_ref[0] = near
    count_ref[1] = far


def attend(list_ref, found, length_ref, q_ref, root_ref, sources, state, pages, arrived):
    top_ref, sum_ref, hold = state

    def fetch(item):
        code = list_ref[item]
        lane = lax.rem(item, DEPTH)
        offset = jnp.bitwise_and(code, SLOTS - 1)
        segment = jnp.bitwise_and(lax.shift_right_logical(code, 5), SLOTS - 1)
        for index, (ref, base) in enumerate(sources):

            @pl.when(segment == index)
            def _(ref=ref, base=base):
                pltpu.make_async_copy(
                    ref.at[base + offset], pages.at[lane], arrived.at[lane]
                ).start()

    for item in range(DEPTH):

        @pl.when(item < found)
        def _(item=item):
            fetch(item)

    tokens = lax.broadcasted_iota(jnp.int32, (SB, HD), 1)

    def visit(item, carry):
        lane = lax.rem(item, DEPTH)
        place = lax.shift_right_logical(list_ref[item], 10)
        beam = lax.shift_right_logical(place, 6)
        group = lax.shift_right_logical(beam, 3)
        count = length_ref[beam] - jnp.bitwise_and(place, 63) * HD
        live = (root_ref[group] == jnp.bitwise_and(beam, 7)) & (tokens < count)
        live = jnp.concatenate([live] * HEADS, axis=0)
        pltpu.make_async_copy(sources[0][0].at[0], pages.at[lane], arrived.at[lane]).wait()
        scores = (
            lax.dot_general(
                q_ref[group],
                pages[lane, 0],
                (((1,), (1,)), ((), ())),
                preferred_element_type=jnp.float32,
            )
            * SCALE
        )
        scores = jnp.where(live, scores, NEGATIVE)
        old = top_ref[group]
        new = jnp.maximum(old, jnp.max(scores, axis=1, keepdims=True))
        weights = jnp.where(live, jnp.exp(scores - new), 0.0)
        fade = jnp.exp(old - new)
        top_ref[group] = new
        sum_ref[group] = sum_ref[group] * fade + jnp.sum(weights, axis=1, keepdims=True)
        hold[group] = hold[group] * fade + jnp.dot(
            weights.astype(jnp.bfloat16), pages[lane, 1], preferred_element_type=jnp.float32
        )

        @pl.when(item + DEPTH < found)
        def _():
            fetch(item + DEPTH)

        return carry

    lax.fori_loop(0, found, visit, 0)


def attend_near(list_ref, count_ref, length_ref, q_ref, root_ref, *rest):
    wholes = rest[:6]
    top_ref, sum_ref, hold, pages, arrived = rest[6:]
    sources = [(whole, base) for whole in wholes for base in (0, SLOTS // 2)]
    top_ref[...] = jnp.full_like(top_ref, NEGATIVE)
    sum_ref[...] = jnp.zeros_like(sum_ref)
    hold[...] = jnp.zeros_like(hold)
    state = (top_ref, sum_ref, hold)
    attend(
        list_ref, count_ref[0], length_ref, q_ref, root_ref, sources, state, pages, arrived
    )


def attend_far(list_ref, count_ref, length_ref, q_ref, root_ref, *rest):
    parts, before, out_ref, state = rest[:4], rest[4:7], rest[7], rest[8:11]
    pages, arrived = rest[11:]
    for ref, start in zip(state, before):
        ref[...] = start[...]
    sources = [(part, 0) for part in parts]
    attend(
        list_ref, count_ref[1], length_ref, q_ref, root_ref, sources, state, pages, arrived
    )
    top_ref, sum_ref, hold = state
    lanes = lax.broadcasted_iota(jnp.int32, (GROUP, HD), 1)

    def pack(group, carry):
        tile = jnp.zeros((GROUP, HD), jnp.float32)
        for part in range(HEADS * STEPS):
            rows = slice(part * GROUP, (part + 1) * GROUP)
            tile = jnp.where(lanes == part, top_ref[group, rows, :], tile)
            tile = jnp.where(lanes == part + HD // 2, sum_ref[group, rows, :], tile)
        out_ref[group] = seal([hold[group]], tile)
        return carry

    lax.fori_loop(0, ZN, pack, 0)


def seal(sums, stat):
    high = stat.astype(jnp.bfloat16).astype(jnp.float32)
    middle = (stat - high).astype(jnp.bfloat16).astype(jnp.float32)
    low = stat - high - middle
    return jnp.concatenate(sums + [high, middle, low], axis=0).astype(jnp.bfloat16)


def unseal(block):
    block = block.astype(jnp.float32)
    stat = block[ROWS : ROWS + GROUP] + block[ROWS + GROUP : ROWS + 2 * GROUP]
    return block[:ROWS], stat + block[ROWS + 2 * GROUP :]


def finish(parts_ref, q_ref, k_ref, v_ref, out_ref, hold):
    count = parts_ref.shape[0]
    sums, stats = zip(*[unseal(parts_ref[source]) for source in range(count)])
    cached_top = functools.reduce(jnp.maximum, stats)
    queries = q_ref[...].astype(jnp.float32)
    lanes = lax.broadcasted_iota(jnp.int32, (GROUP, HD), 1)
    fresh = {}
    tops = cached_top
    for head in range(HEADS):
        for step in range(STEPS):
            part = head * STEPS + step
            row = head * SB + step * GROUP
            tile = queries[row : row + GROUP]
            for token in range(step + 1):
                key = k_ref[PAIRS.index((step, token))]
                score = jnp.sum(tile * key, axis=1, keepdims=True) * SCALE
                fresh[part, token] = score
                tops = jnp.where(lanes == part, jnp.maximum(tops, score), tops)
    fades = [jnp.exp(stat - tops) for stat in stats]
    total = sum(fade * pltpu.roll(stat, HD // 2, 1) for fade, stat in zip(fades, stats))
    for head in range(HEADS):
        for step in range(STEPS):
            part = head * STEPS + step
            rows = slice(part * GROUP, (part + 1) * GROUP)
            ceiling = tops[:, part : part + 1]
            below = total[:, part : part + 1]
            above = sum(
                fades[source][:, part : part + 1] * sums[source][rows] for source in range(count)
            )
            for token in range(step + 1):
                weight = jnp.exp(fresh[part, token] - ceiling)
                below = below + weight
                above = above + weight.astype(jnp.bfloat16).astype(jnp.float32) * v_ref[
                    PAIRS.index((step, token))
                ]
            hold[step * GROUP : (step + 1) * GROUP, head * HD : (head + 1) * HD] = above / below
    attended = hold[...].astype(jnp.bfloat16)
    for target in range(ZN):
        out_ref[target] = attended


def compose(parents_near):
    digits = jnp.arange(GROUP, dtype=jnp.int32)
    roots = [parents_near[0]]
    for step in range(1, STEPS):
        pick = parents_near[step][:, :, None] == digits
        roots.append(jnp.sum(jnp.where(pick, roots[-1][:, None, :], 0), axis=-1))
    return jnp.stack(roots)


def body(
    embeds, attn_gain, w_query, w_key, w_value, w_out, cache_kv, lengths, block_table, parents
):
    z = lax.axis_index("z")
    x = lax.axis_index("x")
    core = lax.axis_index("core")
    here = (z * XN + x) * CN + core
    groups = ZN * JN
    beams = groups * GROUP
    half_slots = SLOTS // 2
    width = PART * groups

    place = jnp.stack([x, core, lax.axis_index("kv"), z]).astype(jnp.int32)
    vmem = pl.BlockSpec(memory_space=pltpu.VMEM)
    smem = pl.BlockSpec(memory_space=pltpu.SMEM)
    cache = cache_kv[:, 0]

    base = jnp.arange(groups, dtype=jnp.int32)[None, :, None] * GROUP
    parents_near = parents.reshape(STEPS, groups, GROUP) - base
    roots_near = compose(parents_near)
    length_of = lengths.reshape(groups, GROUP)
    own_roots = lax.dynamic_slice_in_dim(roots_near, here, 1, 1)[:, 0]
    own_parents = lax.dynamic_slice_in_dim(parents_near, here, 1, 1)[:, 0]
    own_lengths = lax.dynamic_slice_in_dim(length_of, here, 1, 0)[0]
    digits = jnp.arange(GROUP, dtype=jnp.int32)
    position = jnp.sum(
        jnp.where(own_roots[:, :, None] == digits, own_lengths[None, None, :], 0), axis=-1
    ) + jnp.arange(STEPS, dtype=jnp.int32)[:, None]
    exponent = jnp.arange(HD // 2, dtype=jnp.float32) * (2.0 / HD)
    frequency = ROPE_BASE ** (-exponent)
    angles = position.reshape(SB).astype(jnp.float32)[:, None] * frequency[None, :]
    cosines = jnp.cos(angles)
    sines = jnp.sin(angles)
    cosines = jnp.concatenate([cosines, cosines], axis=1)
    sines = jnp.concatenate([-sines, sines], axis=1)
    lead = x * CN + core
    table = lax.dynamic_index_in_dim(
        block_table.reshape(ZN, JN, GROUP * block_table.shape[1]), lead, 1, keepdims=False
    ).reshape(-1)
    spans = lax.dynamic_index_in_dim(lengths.reshape(ZN, JN, GROUP), lead, 1, keepdims=False)
    root_tiles = lax.dynamic_index_in_dim(
        roots_near.reshape(STEPS, ZN, JN, GROUP), lead, 2, keepdims=False
    )
    alive = jnp.any(root_tiles[0][:, :, None] == digits, axis=1)
    spans = jnp.where(alive, spans, 0).reshape(-1)
    listing = jax.ShapeDtypeStruct((SLOTS * JN,), jnp.int32)
    near_list, far_list, counts = pl.pallas_call(
        scan,
        compiler_params=SMALL,
        out_shape=(listing, listing, jax.ShapeDtypeStruct((2,), jnp.int32)),
        in_specs=[smem] * 3,
        out_specs=(smem,) * 3,
    )(place, table, spans)
    root_tiles = root_tiles.transpose(1, 0, 2).reshape(ZN, SB)

    rows = ZN * SB
    half = rows // 2
    by_row = embeds.reshape(STEPS, ZN // 2, 2, JN, GROUP, PART).transpose(3, 1, 0, 4, 2, 5)
    by_row = by_row.reshape(JN, half, 2 * PART)
    high = lax.reduce_precision(attn_gain, 8, 7)
    middle = lax.reduce_precision(attn_gain - high, 8, 7)
    low = attn_gain - high - middle
    gain_rows = jnp.stack(
        [jnp.concatenate([high, middle]), jnp.concatenate([low, jnp.zeros_like(low)])]
    ).astype(jnp.bfloat16)
    gain_rows = jnp.concatenate([gain_rows, jnp.zeros((6, HD), jnp.bfloat16)])
    packed = jnp.concatenate([by_row, jnp.broadcast_to(gain_rows[None], (JN, 8, HD))], axis=1)
    weights = jnp.concatenate([w_query, w_key, w_value], axis=1)
    weights = ring(weights)
    packed = exchange(packed, XC)
    stream = packed[:, :half].reshape(XN, CN, ZN // 2, SB, 2, PART).transpose(0, 2, 4, 3, 1, 5)
    stream = stream.reshape(XN, rows, 2 * PART).astype(jnp.float32)
    tails = packed[:, half : half + 2].astype(jnp.float32)
    gain = tails[:, 0, :PART] + tails[:, 0, PART:] + tails[:, 1, :PART]
    gain = gain.reshape(XN, 1, 2 * PART)
    squares = jnp.sum(stream * stream, axis=(0, 2))
    squares = jnp.pad(squares, (0, 256 - rows)).reshape(2, 128)
    cache, squares = lax.optimization_barrier((cache, squares))
    left = shift(cache, 1)
    right = shift(cache, -1)
    root_tiles = jnp.broadcast_to(root_tiles[:, :, None], (ZN, SB, HD))
    left, right, near_list, root_tiles, own_parents, cosines, sines = lax.optimization_barrier(
        (left, right, near_list, root_tiles, own_parents, cosines, sines)
    )
    across = [shift(left[:half_slots], 1), shift(right[half_slots:], -1)]
    squares = jnp.sum(spread(squares, "z", ZN), axis=0).reshape(256)[:rows]
    stream, weights = lax.optimization_barrier((stream, weights))
    weights = weights + [swap(part) for part in weights]
    inverse = lax.rsqrt(squares / width + EPSILON)
    normed = (stream * inverse[None, :, None] * gain).astype(jnp.bfloat16)
    columns = weights[0].shape[1]
    projected = pl.pallas_call(
        project,
        compiler_params=SMALL,
        out_shape=jax.ShapeDtypeStruct((rows, columns), jnp.float32),
        in_specs=[smem] + [vmem] * (1 + 2 * XN),
        out_specs=vmem,
        scratch_shapes=[pltpu.VMEM((XN, 2 * PART, columns), jnp.bfloat16)],
    )(place, normed, *weights)
    projected = exchange(projected.reshape(ZN, SB, columns), "z")

    small = jax.ShapeDtypeStruct((len(PAIRS), GROUP, HD), jnp.float32)
    queries, everyone, key_chain, value_chain = pl.pallas_call(
        after_projection,
        compiler_params=SMALL,
        out_shape=(
            jax.ShapeDtypeStruct((ROWS, HD), jnp.bfloat16),
            jax.ShapeDtypeStruct((ZN, ROWS, HD), jnp.bfloat16),
            small,
            small,
        ),
        in_specs=[smem, vmem, vmem, vmem],
        out_specs=(vmem,) * 4,
        scratch_shapes=[pltpu.VMEM((ROWS, HD), jnp.float32)],
    )(own_parents.reshape(SB), projected, cosines, sines)
    near = [part for whole in (cache, left, right) for part in (whole, swap(whole))]
    last = PAIRS.index((STEPS - 1, 0))
    appended = jnp.stack([key_chain[last:], value_chain[last:]], axis=2)
    appended = appended[:, :, None].astype(jnp.bfloat16)

    everyone = exchange(everyone, "z")
    everyone, turned, across = lax.optimization_barrier((everyone, w_out.T, across))
    across = across + [swap(part) for part in across]
    turned = ring(turned)
    turned = turned + [swap(part) for part in turned]
    state = (jax.ShapeDtypeStruct((ZN, ROWS, HD), jnp.float32),) * 3
    ring_buffers = [
        pltpu.VMEM((DEPTH,) + cache.shape[1:], jnp.bfloat16),
        pltpu.SemaphoreType.DMA((DEPTH,)),
    ]
    anywhere = pl.BlockSpec(memory_space=pltpu.HBM)
    before = pl.pallas_call(
        attend_near,
        compiler_params=SMALL,
        out_shape=state,
        in_specs=[smem, smem, smem, vmem, vmem] + [anywhere] * 6,
        out_specs=(vmem,) * 3,
        scratch_shapes=ring_buffers,
        cost_estimate=pl.CostEstimate(flops=1, bytes_accessed=1, transcendentals=0),
    )(near_list, counts, spans, everyone, root_tiles, *near)
    partial = pl.pallas_call(
        attend_far,
        compiler_params=SMALL,
        out_shape=jax.ShapeDtypeStruct((ZN, BLOCK, HD), jnp.bfloat16),
        in_specs=[smem, smem, smem, vmem, vmem] + [anywhere] * 4 + [vmem] * 3,
        out_specs=vmem,
        scratch_shapes=[pltpu.VMEM(part.shape, part.dtype) for part in state] + ring_buffers,
    )(far_list, counts, spans, everyone, root_tiles, *across, *before)

    partial = exchange(partial, "z")
    partial, turned = lax.optimization_barrier((partial, turned))
    attended = pl.pallas_call(
        finish,
        compiler_params=SMALL,
        out_shape=jax.ShapeDtypeStruct((ZN, SB, HEADS * HD), jnp.bfloat16),
        in_specs=[vmem] * 4,
        out_specs=vmem,
        scratch_shapes=[pltpu.VMEM((SB, HEADS * HD), jnp.float32)],
    )(partial, queries, key_chain, value_chain)

    attended = exchange(attended, "z").reshape(rows, HEADS * HD)
    share = jax.ShapeDtypeStruct((XN, QUARTER, 2 * PART), jnp.float32)
    shares = pl.pallas_call(
        deliver,
        compiler_params=SMALL,
        out_shape=(share,) * KN,
        in_specs=[smem] + [vmem] * (1 + 2 * XN),
        out_specs=(vmem,) * KN,
        scratch_shapes=[
            pltpu.VMEM((XN, 2 * PART, HEADS * HD), jnp.bfloat16),
            pltpu.VMEM((rows, 2 * PART), jnp.float32),
        ],
    )(place, attended, *turned)
    shares = [shares[0]] + [
        lax.ppermute(shares[far], "kv", [(i, (i + far) % KN) for i in range(KN)])
        for far in range(1, KN)
    ]
    result = pl.pallas_call(
        settle,
        compiler_params=SMALL,
        out_shape=jax.ShapeDtypeStruct((KN, XN, CN, SB, 2 * PART), jnp.bfloat16),
        in_specs=[smem] + [vmem] * (KN + 1),
        out_specs=vmem,
    )(place, *shares, stream)
    result = exchange(result.reshape(KN * JN, SB, 2 * PART), ("kv",) + XC)
    result = result.reshape(KN, JN, STEPS, GROUP, 2, PART).transpose(2, 0, 4, 1, 3, 5)
    return (result.reshape(STEPS, beams, PART), appended)


def solution(mesh):
    fine = Mesh(mesh.devices.reshape(-1, ZN, XN, CN), ("kv",) + BLK)
    return jax.shard_map(
        body,
        mesh=fine,
        in_specs=(
            P(None, None, BLK),
            P(BLK),
            P(BLK, "kv"),
            P(BLK, "kv"),
            P(BLK, "kv"),
            P("kv", BLK),
            P(BLK, "kv", None, None, None),
            P(),
            P(),
            P(),
        ),
        out_specs=(P(None, None, BLK), P(None, BLK, "kv", None, None)),
        check_vma=False,
    )
```

```python
import functools
import math

import jax
import jax.numpy as jnp
from jax import lax
from jax.experimental import pallas as pl
from jax.experimental.pallas import tpu as pltpu
from jax.sharding import Mesh
from jax.sharding import PartitionSpec as P

GROUP = 8
NEGATIVE = -1e30
EPSILON = 1e-05
ROPE_BASE = 5000000.0
STEPS = 3
HEADS = 8
HD = 128
SB = STEPS * GROUP
ROWS = HEADS * SB
BLOCK = ROWS + 3 * GROUP
ZN, XN, CN = 8, 4, 2
JN = XN * CN
KN = 4
PART = 64
SLOTS = 32
DEPTH = 12
QUARTER = ZN * SB // KN
SMALL = pltpu.CompilerParams(vmem_limit_bytes=16 << 20)
PAIRS = [(s, u) for s in range(STEPS) for u in range(s + 1)]
SCALE = 1.0 / math.sqrt(HD)
XC = ("x", "core")
BLK = ("z", "x", "core")


def exchange(value, axis):
    return lax.all_to_all(value, axis, 0, 0, tiled=True)


def spread(value, axis, count):
    return exchange(jnp.broadcast_to(value[None], (count,) + value.shape), axis)


def swap(value):
    return lax.ppermute(value, "core", [(0, 1), (1, 0)])


def shift(value, hop):
    return lax.ppermute(value, "x", [(i, (i + hop) % XN) for i in range(XN)])


def ring(value):
    return [value] + [shift(value, hop) for hop in range(1, XN)]


def join(place_ref, chunks, wide):
    core = place_ref[1]
    for hop in range(XN):
        wide[hop, pl.ds(pl.multiple_of(core * PART, PART), PART), :] = chunks[hop][...]
        wide[hop, pl.ds(pl.multiple_of((1 - core) * PART, PART), PART), :] = chunks[XN + hop][...]


def project(place_ref, rows_ref, *rest):
    chunks, out_ref, wide = rest[: 2 * XN], rest[2 * XN], rest[2 * XN + 1]
    join(place_ref, chunks, wide)
    x = place_ref[0]
    for start in range(0, out_ref.shape[1], 256):
        out_ref[:, start : start + 256] = sum(
            jnp.dot(
                rows_ref[(x + XN - hop) % XN],
                wide[hop, :, start : start + 256],
                preferred_element_type=jnp.float32,
            )
            for hop in range(XN)
        )


def deliver(place_ref, rows_ref, *rest):
    chunks, outs, wide = rest[: 2 * XN], rest[2 * XN : 2 * XN + KN], rest[2 * XN + KN]
    hold = rest[2 * XN + KN + 1]
    join(place_ref, chunks, wide)
    x, kv = place_ref[0], place_ref[2]
    for hop in range(XN):
        hold[...] = lax.dot_general(
            rows_ref[...],
            wide[hop],
            (((1,), (1,)), ((), ())),
            preferred_element_type=jnp.float32,
        )
        for far in range(KN):
            start = pl.multiple_of(lax.rem(kv + far, KN) * QUARTER, 8)
            outs[far][lax.rem(x + XN - hop, XN)] = hold[pl.ds(start, QUARTER), :]


def settle(place_ref, *rest):
    parts, stream_ref, out_ref = rest[:KN], rest[KN], rest[KN + 1]
    kv = place_ref[2]
    lanes = lax.broadcasted_iota(jnp.int32, (SB, 2 * PART), 1)
    for x in range(XN):
        total = parts[0][x]
        for part in parts[1:]:
            total = total + part[x]
        total = stream_ref[x, pl.ds(pl.multiple_of(kv * QUARTER, 8), QUARTER), :] + total
        upper, lower = total[:SB], total[SB:]
        first = jnp.where(lanes < PART, upper, pltpu.roll(lower, PART, 1)).astype(jnp.bfloat16)
        second = jnp.where(lanes < PART, pltpu.roll(upper, PART, 1), lower).astype(jnp.bfloat16)
        for target in range(KN):
            out_ref[target, x, 0] = first
            out_ref[target, x, 1] = second


def after_projection(
    parent_ref, parts_ref, cos_ref, sin_ref, q_ref, all_ref, k_ref, v_ref, hold
):
    total = parts_ref[0]
    for source in range(1, ZN):
        total = total + parts_ref[source]
    cosines = cos_ref[...]
    sines = sin_ref[...]

    def turn(part):
        return part * cosines + pltpu.roll(part, HD // 2, 1) * sines

    for head in range(HEADS):
        hold[head * SB : (head + 1) * SB] = turn(total[:, head * HD : (head + 1) * HD])
    queries = hold[...].astype(jnp.bfloat16)
    q_ref[...] = queries
    for target in range(ZN):
        all_ref[target] = queries
    start = HEADS * HD
    fresh_key = turn(total[:, start : start + HD]).astype(jnp.bfloat16).astype(jnp.float32)
    fresh_value = total[:, start + HD :].astype(jnp.bfloat16).astype(jnp.float32)
    for index, (step, token) in enumerate(PAIRS):
        for ref, fresh in ((k_ref, fresh_key), (v_ref, fresh_value)):
            if token == step:
                ref[index] = fresh[step * GROUP : (step + 1) * GROUP]
            else:
                before = PAIRS.index((step - 1, token))
                for beam in range(GROUP):
                    parent = parent_ref[step * GROUP + beam]
                    ref[index, pl.ds(beam, 1), :] = ref[before, pl.ds(parent, 1), :]


def scan(
    place_ref, parent_ref, table_ref, length_ref, near_list, far_list, count_ref
):
    x, core, z = place_ref[0], place_ref[1], place_ref[3]
    blocks = table_ref.shape[0] // (ZN * GROUP)
    half = SLOTS // 2

    def scan_beam(beam, found):
        group = lax.shift_right_logical(beam, 3) * JN + x * CN + core
        heirs = jnp.int32(0)
        for member in range(GROUP):
            parent = jnp.bitwise_and(parent_ref[group * GROUP + member], GROUP - 1)
            heirs = heirs + (parent == jnp.bitwise_and(beam, GROUP - 1)).astype(jnp.int32)
        used = lax.shift_right_logical(length_ref[beam] + (HD - 1), 7)
        used = jnp.where(heirs > 0, used, 0)

        def scan_block(block, found):
            slot = table_ref[beam * blocks + block]
            near, far = found
            hit = lax.shift_right_logical(slot, 8) == z
            hops = jnp.bitwise_and(lax.shift_right_logical(slot, 6) - x, XN - 1)
            opposite = hops == 2
            offset = jnp.bitwise_and(slot, half - 1)
            upper = jnp.bitwise_and(lax.shift_right_logical(slot, 4), 1)
            foreign = jnp.bitwise_xor(jnp.bitwise_and(lax.shift_right_logical(slot, 5), 1), core)
            chip = jnp.where(hops == 0, 0, jnp.where(hops == 3, 1, 2))
            segment = jnp.where(opposite, upper + 2 * foreign, chip * 4 + upper + 2 * foreign)
            code = ((beam * blocks + block) * SLOTS + segment) * SLOTS + offset

            @pl.when(hit & opposite)
            def _():
                far_list[far] = code

            @pl.when(hit & jnp.logical_not(opposite))
            def _():
                near_list[near] = code

            return (
                near + (hit & jnp.logical_not(opposite)).astype(jnp.int32),
                far + (hit & opposite).astype(jnp.int32),
            )

        return lax.fori_loop(0, used, scan_block, found)

    near, far = lax.fori_loop(0, ZN * GROUP, scan_beam, (0, 0))
    count_ref[0] = near
    count_ref[1] = far


def attend(list_ref, found, length_ref, q_ref, root_ref, sources, state, pages, arrived):
    top_ref, sum_ref, hold = state

    def fetch(item):
        code = list_ref[item]
        lane = lax.rem(item, DEPTH)
        offset = jnp.bitwise_and(code, SLOTS - 1)
        segment = jnp.bitwise_and(lax.shift_right_logical(code, 5), SLOTS - 1)
        for index, (ref, base) in enumerate(sources):

            @pl.when(segment == index)
            def _(ref=ref, base=base):
                pltpu.make_async_copy(
                    ref.at[base + offset], pages.at[lane], arrived.at[lane]
                ).start()

    for item in range(DEPTH):

        @pl.when(item < found)
        def _(item=item):
            fetch(item)

    tokens = lax.broadcasted_iota(jnp.int32, (SB, HD), 1)

    def visit(item, carry):
        lane = lax.rem(item, DEPTH)
        place = lax.shift_right_logical(list_ref[item], 10)
        beam = lax.shift_right_logical(place, 6)
        group = lax.shift_right_logical(beam, 3)
        count = length_ref[beam] - jnp.bitwise_and(place, 63) * HD
        live = (root_ref[group] == jnp.bitwise_and(beam, 7)) & (tokens < count)
        live = jnp.concatenate([live] * HEADS, axis=0)
        pltpu.make_async_copy(sources[0][0].at[0], pages.at[lane], arrived.at[lane]).wait()
        scores = (
            lax.dot_general(
                q_ref[group],
                pages[lane, 0],
                (((1,), (1,)), ((), ())),
                preferred_element_type=jnp.float32,
            )
            * SCALE
        )
        scores = jnp.where(live, scores, NEGATIVE)
        old = top_ref[group]
        new = jnp.maximum(old, jnp.max(scores, axis=1, keepdims=True))
        weights = jnp.where(live, jnp.exp(scores - new), 0.0)
        fade = jnp.exp(old - new)
        top_ref[group] = new
        sum_ref[group] = sum_ref[group] * fade + jnp.sum(weights, axis=1, keepdims=True)
        hold[group] = hold[group] * fade + jnp.dot(
            weights.astype(jnp.bfloat16), pages[lane, 1], preferred_element_type=jnp.float32
        )

        @pl.when(item + DEPTH < found)
        def _():
            fetch(item + DEPTH)

        return carry

    lax.fori_loop(0, found, visit, 0)


def attend_near(list_ref, count_ref, length_ref, q_ref, root_ref, *rest):
    wholes = rest[:6]
    top_ref, sum_ref, hold, pages, arrived = rest[6:]
    sources = [(whole, base) for whole in wholes for base in (0, SLOTS // 2)]
    top_ref[...] = jnp.full_like(top_ref, NEGATIVE)
    sum_ref[...] = jnp.zeros_like(sum_ref)
    hold[...] = jnp.zeros_like(hold)
    state = (top_ref, sum_ref, hold)
    attend(
        list_ref, count_ref[0], length_ref, q_ref, root_ref, sources, state, pages, arrived
    )


def attend_far(list_ref, count_ref, length_ref, q_ref, root_ref, *rest):
    parts, before, out_ref, state = rest[:4], rest[4:7], rest[7], rest[8:11]
    pages, arrived = rest[11:]
    for ref, start in zip(state, before):
        ref[...] = start[...]
    sources = [(part, 0) for part in parts]
    attend(
        list_ref, count_ref[1], length_ref, q_ref, root_ref, sources, state, pages, arrived
    )
    top_ref, sum_ref, hold = state
    lanes = lax.broadcasted_iota(jnp.int32, (GROUP, HD), 1)

    def pack(group, carry):
        tile = jnp.zeros((GROUP, HD), jnp.float32)
        for part in range(HEADS * STEPS):
            rows = slice(part * GROUP, (part + 1) * GROUP)
            tile = jnp.where(lanes == part, top_ref[group, rows, :], tile)
            tile = jnp.where(lanes == part + HD // 2, sum_ref[group, rows, :], tile)
        out_ref[group] = seal([hold[group]], tile)
        return carry

    lax.fori_loop(0, ZN, pack, 0)


def seal(sums, stat):
    high = stat.astype(jnp.bfloat16).astype(jnp.float32)
    middle = (stat - high).astype(jnp.bfloat16).astype(jnp.float32)
    low = stat - high - middle
    return jnp.concatenate(sums + [high, middle, low], axis=0).astype(jnp.bfloat16)


def unseal(block):
    block = block.astype(jnp.float32)
    stat = block[ROWS : ROWS + GROUP] + block[ROWS + GROUP : ROWS + 2 * GROUP]
    return block[:ROWS], stat + block[ROWS + 2 * GROUP :]


def finish(parts_ref, q_ref, k_ref, v_ref, out_ref, hold):
    count = parts_ref.shape[0]
    sums, stats = zip(*[unseal(parts_ref[source]) for source in range(count)])
    cached_top = functools.reduce(jnp.maximum, stats)
    queries = q_ref[...].astype(jnp.float32)
    lanes = lax.broadcasted_iota(jnp.int32, (GROUP, HD), 1)
    fresh = {}
    tops = cached_top
    for head in range(HEADS):
        for step in range(STEPS):
            part = head * STEPS + step
            row = head * SB + step * GROUP
            tile = queries[row : row + GROUP]
            for token in range(step + 1):
                key = k_ref[PAIRS.index((step, token))]
                score = jnp.sum(tile * key, axis=1, keepdims=True) * SCALE
                fresh[part, token] = score
                tops = jnp.where(lanes == part, jnp.maximum(tops, score), tops)
    fades = [jnp.exp(stat - tops) for stat in stats]
    total = sum(fade * pltpu.roll(stat, HD // 2, 1) for fade, stat in zip(fades, stats))
    for head in range(HEADS):
        for step in range(STEPS):
            part = head * STEPS + step
            rows = slice(part * GROUP, (part + 1) * GROUP)
            ceiling = tops[:, part : part + 1]
            below = total[:, part : part + 1]
            above = sum(
                fades[source][:, part : part + 1] * sums[source][rows] for source in range(count)
            )
            for token in range(step + 1):
                weight = jnp.exp(fresh[part, token] - ceiling)
                below = below + weight
                above = above + weight.astype(jnp.bfloat16).astype(jnp.float32) * v_ref[
                    PAIRS.index((step, token))
                ]
            hold[step * GROUP : (step + 1) * GROUP, head * HD : (head + 1) * HD] = above / below
    attended = hold[...].astype(jnp.bfloat16)
    for target in range(ZN):
        out_ref[target] = attended


def compose(parents_near):
    digits = jnp.arange(GROUP, dtype=jnp.int32)
    roots = [parents_near[0]]
    for step in range(1, STEPS):
        pick = parents_near[step][:, :, None] == digits
        roots.append(jnp.sum(jnp.where(pick, roots[-1][:, None, :], 0), axis=-1))
    return jnp.stack(roots)


def body(
    embeds, attn_gain, w_query, w_key, w_value, w_out, cache_kv, lengths, block_table, parents
):
    z = lax.axis_index("z")
    x = lax.axis_index("x")
    core = lax.axis_index("core")
    here = (z * XN + x) * CN + core
    groups = ZN * JN
    beams = groups * GROUP
    half_slots = SLOTS // 2
    width = PART * groups

    place = jnp.stack([x, core, lax.axis_index("kv"), z]).astype(jnp.int32)
    vmem = pl.BlockSpec(memory_space=pltpu.VMEM)
    smem = pl.BlockSpec(memory_space=pltpu.SMEM)
    cache = cache_kv[:, 0]

    base = jnp.arange(groups, dtype=jnp.int32)[None, :, None] * GROUP
    parents_near = parents.reshape(STEPS, groups, GROUP) - base
    roots_near = compose(parents_near)
    length_of = lengths.reshape(groups, GROUP)
    own_roots = lax.dynamic_slice_in_dim(roots_near, here, 1, 1)[:, 0]
    own_parents = lax.dynamic_slice_in_dim(parents_near, here, 1, 1)[:, 0]
    own_lengths = lax.dynamic_slice_in_dim(length_of, here, 1, 0)[0]
    digits = jnp.arange(GROUP, dtype=jnp.int32)
    position = jnp.sum(
        jnp.where(own_roots[:, :, None] == digits, own_lengths[None, None, :], 0), axis=-1
    ) + jnp.arange(STEPS, dtype=jnp.int32)[:, None]
    exponent = jnp.arange(HD // 2, dtype=jnp.float32) * (2.0 / HD)
    frequency = ROPE_BASE ** (-exponent)
    angles = position.reshape(SB).astype(jnp.float32)[:, None] * frequency[None, :]
    cosines = jnp.cos(angles)
    sines = jnp.sin(angles)
    cosines = jnp.concatenate([cosines, cosines], axis=1)
    sines = jnp.concatenate([-sines, sines], axis=1)
    lead = x * CN + core
    table = lax.dynamic_index_in_dim(
        block_table.reshape(ZN, JN, GROUP * block_table.shape[1]), lead, 1, keepdims=False
    ).reshape(-1)
    spans = lax.dynamic_index_in_dim(lengths.reshape(ZN, JN, GROUP), lead, 1, keepdims=False)
    spans = spans.reshape(-1)
    listing = jax.ShapeDtypeStruct((SLOTS * JN,), jnp.int32)
    near_list, far_list, counts = pl.pallas_call(
        scan,
        compiler_params=SMALL,
        out_shape=(listing, listing, jax.ShapeDtypeStruct((2,), jnp.int32)),
        in_specs=[smem] * 4,
        out_specs=(smem,) * 3,
    )(place, parents.reshape(-1), table, spans)
    root_tiles = lax.dynamic_index_in_dim(
        roots_near.reshape(STEPS, ZN, JN, GROUP), lead, 2, keepdims=False
    )
    root_tiles = root_tiles.transpose(1, 0, 2).reshape(ZN, SB)

    rows = ZN * SB
    half = rows // 2
    by_row = embeds.reshape(STEPS, ZN // 2, 2, JN, GROUP, PART).transpose(3, 1, 0, 4, 2, 5)
    by_row = by_row.reshape(JN, half, 2 * PART)
    high = lax.reduce_precision(attn_gain, 8, 7)
    middle = lax.reduce_precision(attn_gain - high, 8, 7)
    low = attn_gain - high - middle
    gain_rows = jnp.stack(
        [jnp.concatenate([high, middle]), jnp.concatenate([low, jnp.zeros_like(low)])]
    ).astype(jnp.bfloat16)
    gain_rows = jnp.concatenate([gain_rows, jnp.zeros((6, HD), jnp.bfloat16)])
    packed = jnp.concatenate([by_row, jnp.broadcast_to(gain_rows[None], (JN, 8, HD))], axis=1)
    weights = jnp.concatenate([w_query, w_key, w_value], axis=1)
    cache, weights = lax.optimization_barrier((cache, weights))
    weights = ring(weights)
    left = shift(cache, 1)
    right = shift(cache, -1)
    across = [shift(left[:half_slots], 1), shift(right[half_slots:], -1)]
    packed = exchange(packed, XC)
    packed, weights = lax.optimization_barrier((packed, weights))
    weights = weights + [swap(part) for part in weights]
    stream = packed[:, :half].reshape(XN, CN, ZN // 2, SB, 2, PART).transpose(0, 2, 4, 3, 1, 5)
    stream = stream.reshape(XN, rows, 2 * PART).astype(jnp.float32)
    tails = packed[:, half : half + 2].astype(jnp.float32)
    gain = tails[:, 0, :PART] + tails[:, 0, PART:] + tails[:, 1, :PART]
    gain = gain.reshape(XN, 1, 2 * PART)
    squares = jnp.sum(stream * stream, axis=(0, 2))
    squares = jnp.pad(squares, (0, 256 - rows)).reshape(2, 128)
    squares = jnp.sum(spread(squares, "z", ZN), axis=0).reshape(256)[:rows]
    inverse = lax.rsqrt(squares / width + EPSILON)
    normed = (stream * inverse[None, :, None] * gain).astype(jnp.bfloat16)
    columns = weights[0].shape[1]
    projected = pl.pallas_call(
        project,
        compiler_params=SMALL,
        out_shape=jax.ShapeDtypeStruct((rows, columns), jnp.float32),
        in_specs=[smem] + [vmem] * (1 + 2 * XN),
        out_specs=vmem,
        scratch_shapes=[pltpu.VMEM((XN, 2 * PART, columns), jnp.bfloat16)],
    )(place, normed, *weights)
    projected = exchange(projected.reshape(ZN, SB, columns), "z")
    projected, near_list = lax.optimization_barrier((projected, near_list))

    small = jax.ShapeDtypeStruct((len(PAIRS), GROUP, HD), jnp.float32)
    queries, everyone, key_chain, value_chain = pl.pallas_call(
        after_projection,
        compiler_params=SMALL,
        out_shape=(
            jax.ShapeDtypeStruct((ROWS, HD), jnp.bfloat16),
            jax.ShapeDtypeStruct((ZN, ROWS, HD), jnp.bfloat16),
            small,
            small,
        ),
        in_specs=[smem, vmem, vmem, vmem],
        out_specs=(vmem,) * 4,
        scratch_shapes=[pltpu.VMEM((ROWS, HD), jnp.float32)],
    )(own_parents.reshape(SB), projected, cosines, sines)
    root_tiles = jnp.broadcast_to(root_tiles[:, :, None], (ZN, SB, HD))
    near = [part for whole in (cache, left, right) for part in (whole, swap(whole))]
    last = PAIRS.index((STEPS - 1, 0))
    appended = jnp.stack([key_chain[last:], value_chain[last:]], axis=2)
    appended = appended[:, :, None].astype(jnp.bfloat16)

    everyone = exchange(everyone, "z")
    everyone, turned, across = lax.optimization_barrier((everyone, w_out.T, across))
    across = across + [swap(part) for part in across]
    turned = ring(turned)
    turned = turned + [swap(part) for part in turned]
    state = (jax.ShapeDtypeStruct((ZN, ROWS, HD), jnp.float32),) * 3
    ring_buffers = [
        pltpu.VMEM((DEPTH,) + cache.shape[1:], jnp.bfloat16),
        pltpu.SemaphoreType.DMA((DEPTH,)),
    ]
    anywhere = pl.BlockSpec(memory_space=pltpu.HBM)
    before = pl.pallas_call(
        attend_near,
        compiler_params=SMALL,
        out_shape=state,
        in_specs=[smem, smem, smem, vmem, vmem] + [anywhere] * 6,
        out_specs=(vmem,) * 3,
        scratch_shapes=ring_buffers,
        cost_estimate=pl.CostEstimate(flops=1, bytes_accessed=1, transcendentals=0),
    )(near_list, counts, spans, everyone, root_tiles, *near)
    partial = pl.pallas_call(
        attend_far,
        compiler_params=SMALL,
        out_shape=jax.ShapeDtypeStruct((ZN, BLOCK, HD), jnp.bfloat16),
        in_specs=[smem, smem, smem, vmem, vmem] + [anywhere] * 4 + [vmem] * 3,
        out_specs=vmem,
        scratch_shapes=[pltpu.VMEM(part.shape, part.dtype) for part in state] + ring_buffers,
    )(far_list, counts, spans, everyone, root_tiles, *across, *before)

    partial = exchange(partial, "z")
    partial, turned = lax.optimization_barrier((partial, turned))
    attended = pl.pallas_call(
        finish,
        compiler_params=SMALL,
        out_shape=jax.ShapeDtypeStruct((ZN, SB, HEADS * HD), jnp.bfloat16),
        in_specs=[vmem] * 4,
        out_specs=vmem,
        scratch_shapes=[pltpu.VMEM((SB, HEADS * HD), jnp.float32)],
    )(partial, queries, key_chain, value_chain)

    attended = exchange(attended, "z").reshape(rows, HEADS * HD)
    share = jax.ShapeDtypeStruct((XN, QUARTER, 2 * PART), jnp.float32)
    shares = pl.pallas_call(
        deliver,
        compiler_params=SMALL,
        out_shape=(share,) * KN,
        in_specs=[smem] + [vmem] * (1 + 2 * XN),
        out_specs=(vmem,) * KN,
        scratch_shapes=[
            pltpu.VMEM((XN, 2 * PART, HEADS * HD), jnp.bfloat16),
            pltpu.VMEM((rows, 2 * PART), jnp.float32),
        ],
    )(place, attended, *turned)
    shares = [shares[0]] + [
        lax.ppermute(shares[far], "kv", [(i, (i + far) % KN) for i in range(KN)])
        for far in range(1, KN)
    ]
    result = pl.pallas_call(
        settle,
        compiler_params=SMALL,
        out_shape=jax.ShapeDtypeStruct((KN, XN, CN, SB, 2 * PART), jnp.bfloat16),
        in_specs=[smem] + [vmem] * (KN + 1),
        out_specs=vmem,
    )(place, *shares, stream)
    result = exchange(result.reshape(KN * JN, SB, 2 * PART), ("kv",) + XC)
    result = result.reshape(KN, JN, STEPS, GROUP, 2, PART).transpose(2, 0, 4, 1, 3, 5)
    return (result.reshape(STEPS, beams, PART), appended)


def solution(mesh):
    fine = Mesh(mesh.devices.reshape(-1, ZN, XN, CN), ("kv",) + BLK)
    return jax.shard_map(
        body,
        mesh=fine,
        in_specs=(
            P(None, None, BLK),
            P(BLK),
            P(BLK, "kv"),
            P(BLK, "kv"),
            P(BLK, "kv"),
            P("kv", BLK),
            P(BLK, "kv", None, None, None),
            P(),
            P(),
            P(),
        ),
        out_specs=(P(None, None, BLK), P(None, BLK, "kv", None, None)),
        check_vma=False,
    )
```
